32 devices in a mesh: page: 16 (over z, y, x), seq: 2 (over core).
Axes of the slice: x: 2, y: 2, z: 4, core: 2. Of those that a mesh axis runs over, the one named last changes fastest.
Arguments:
- hidden: bfloat16 [32, 512, 768], P('page', 'seq'), may hold values from -6 to 6
- lengths: int32 [32], P('page'), may hold values from 64 to 512, as said below
- w_query: bfloat16 [768, 768], P(('page', 'seq')), may hold values from -0.21875 to 0.21875
- w_key: bfloat16 [768, 768], P(('page', 'seq')), may hold values from -0.21875 to 0.21875
- w_value: bfloat16 [768, 768], P(('page', 'seq')), may hold values from -0.21875 to 0.21875
- w_output: bfloat16 [768, 768], P(('page', 'seq')), may hold values from -0.625 to 0.625
- b_query: bfloat16 [768], P(('page', 'seq')), may hold values from -3 to 3
- b_value: bfloat16 [768], P(('page', 'seq')), may hold values from -3 to 3
- b_output: bfloat16 [768], P(('page', 'seq')), may hold values from -3 to 3
- attn_gain: bfloat16 [768], P(('page', 'seq')), may hold values from 0.5 to 1.5
- attn_shift: bfloat16 [768], P(('page', 'seq')), may hold values from -3 to 3
- w_inner: bfloat16 [768, 3072], P(('page', 'seq')), may hold values from -0.21875 to 0.21875
- b_inner: bfloat16 [3072], P(('page', 'seq')), may hold values from -3 to 3
- w_outer: bfloat16 [3072, 768], P(('page', 'seq')), may hold values from -0.109375 to 0.109375
- b_outer: bfloat16 [768], P(('page', 'seq')), may hold values from -3 to 3
- ffn_gain: bfloat16 [768], P(('page', 'seq')), may hold values from 0.5 to 1.5
- ffn_shift: bfloat16 [768], P(('page', 'seq')), may hold values from -3 to 3
- cotangent: bfloat16 [32, 512, 768], P('page', 'seq'), may hold values from -6 to 6
Outputs:
- layer_out: bfloat16 [32, 512, 768], P('page', 'seq')
- hidden_grad: bfloat16 [32, 512, 768], P('page', 'seq')
- query_w_grad: float32 [768, 768], P(('page', 'seq'))
- key_w_grad: float32 [768, 768], P(('page', 'seq'))
- value_w_grad: float32 [768, 768], P(('page', 'seq'))
- output_w_grad: float32 [768, 768], P(('page', 'seq'))
- query_b_grad: float32 [768], P(('page', 'seq'))
- value_b_grad: float32 [768], P(('page', 'seq'))
- output_b_grad: float32 [768], P(('page', 'seq'))
- attn_gain_grad: float32 [768], P(('page', 'seq'))
- attn_shift_grad: float32 [768], P(('page', 'seq'))
- inner_w_grad: float32 [768, 3072], P(('page', 'seq'))
- inner_b_grad: float32 [3072], P(('page', 'seq'))
- outer_w_grad: float32 [3072, 768], P(('page', 'seq'))
- outer_b_grad: float32 [768], P(('page', 'seq'))
- ffn_gain_grad: float32 [768], P(('page', 'seq'))
- ffn_shift_grad: float32 [768], P(('page', 'seq'))
The draws below stay inside these ranges and needn't reach their ends.
Inputs may be any that keep to these rules, and one draw needn't show every extreme that they name: `lengths`: positions below a page's count hold real tokens and the rest are padding; some page is full and some has 64 real tokens.
All inputs are finite; a program needn't handle non-finite values.
Results may differ from the reference program's by a relative error of at most 0.018.
Values may be sent and summed in bfloat16 or wider, within the bound.
A program may use at most 192 MiB of HBM per device.

```python
import math
import jax
import jax.numpy as jnp
from jax import lax

D = 768
HEADS = 12
FF = 3072
PAGE_LEN = 512
PAGES = 32


def draw_lengths(key, part):
    counts = jax.random.randint(key, (PAGES,), PAGE_LEN // 8, PAGE_LEN + 1)
    counts = counts.at[0].set(PAGE_LEN)
    counts = counts.at[PAGES - 1].set(PAGE_LEN // 8)
    return counts.astype(jnp.int32)


def block_scale(rng, shape, shards, low, top_value):
    level, own = 1.0, jax.random.fold_in(rng, 6)
    for position, shards_of in shards:
        draws = jnp.exp(jax.random.uniform(jax.random.fold_in(own, position), (shards_of,), jnp.float32, low / len(shards), top_value / len(shards)))
        level = level * jnp.repeat(draws, shape[position] // shards_of).reshape([-1 if axis == position else 1 for axis in range(len(shape))])
    return level


def bell_draw(own_key, extent, scale, bound, split=(), kind=jnp.bfloat16):
    entries = scale * jax.random.normal(own_key, extent, jnp.float32)
    if split:
        entries = entries * block_scale(own_key, extent, split, -0.22, 0.18)
    return jnp.clip(entries, -bound, bound).astype(kind)


def setup_inputs(seed: int = 0) -> dict:
    keys = jax.random.split(jax.random.key(seed), 19)
    hidden = bell_draw(keys[0], (PAGES, PAGE_LEN, D), 1.0, 6.0, ((0, 16), (1, 2)))
    lengths = draw_lengths(jax.random.fold_in(keys[18], 71), 0)
    w_query = bell_draw(keys[2], (D, D), D ** -0.5, 0.21875, ((0, 32),))
    w_key = bell_draw(keys[3], (D, D), D ** -0.5, 0.21875, ((0, 32),))
    w_value = bell_draw(keys[4], (D, D), D ** -0.5, 0.21875, ((0, 32),))
    w_output = bell_draw(keys[5], (D, D), (D // 8) ** -0.5, 0.625, ((0, 32),))
    b_query = bell_draw(keys[6], (D,), 0.5, 3.0, ((0, 32),))
    b_value = bell_draw(keys[7], (D,), 0.5, 3.0, ((0, 32),))
    b_output = bell_draw(keys[8], (D,), 0.5, 3.0, ((0, 32),))
    attn_gain = jnp.clip(1.0 + 0.1 * jax.random.normal(keys[9], (D,), jnp.float32), 0.5, 1.5).astype(jnp.bfloat16)
    attn_shift = bell_draw(keys[10], (D,), 0.5, 3.0, ((0, 32),))
    w_inner = bell_draw(keys[11], (D, FF), D ** -0.5, 0.21875, ((0, 32),))
    b_inner = bell_draw(keys[12], (FF,), 0.5, 3.0, ((0, 32),))
    w_outer = bell_draw(keys[13], (FF, D), FF ** -0.5, 0.109375, ((0, 32),))
    b_outer = bell_draw(keys[14], (D,), 0.5, 3.0, ((0, 32),))
    ffn_gain = jnp.clip(1.0 + 0.1 * jax.random.normal(keys[15], (D,), jnp.float32), 0.5, 1.5).astype(jnp.bfloat16)
    ffn_shift = bell_draw(keys[16], (D,), 0.5, 3.0, ((0, 32),))
    cotangent = bell_draw(keys[17], (PAGES, PAGE_LEN, D), 1.0, 6.0, ((0, 16), (1, 2)))
    return {"hidden": hidden, "lengths": lengths, "w_query": w_query, "w_key": w_key, "w_value": w_value, "w_output": w_output, "b_query": b_query, "b_value": b_value, "b_output": b_output, "attn_gain": attn_gain, "attn_shift": attn_shift, "w_inner": w_inner, "b_inner": b_inner, "w_outer": w_outer, "b_outer": b_outer, "ffn_gain": ffn_gain, "ffn_shift": ffn_shift, "cotangent": cotangent}


@jax.custom_vjp
def low(v):
    return lax.optimization_barrier(v.astype(jnp.bfloat16)).astype(jnp.float32)

@jax.custom_vjp
def low_back(v):
    return v

def low_keep(v):
    return (low(v), None)

def low_pass(kept, grad):
    return (grad,)

def back_keep(v):
    return (v, None)

def back_low(kept, grad):
    return (low(grad),)
low.defvjp(low_keep, low_pass)
low_back.defvjp(back_keep, back_low)
highest = lax.Precision.HIGHEST
masked_value = -1e+30
norm_eps = 1e-06

def layer_norm(values, norm_gain, norm_shift):
    centre = lax.optimization_barrier(jnp.mean(values, axis=-1, keepdims=True))
    centered = values - centre
    spread = lax.optimization_barrier(jnp.mean(centered * centered, axis=-1, keepdims=True))
    return centered * lax.rsqrt(spread + norm_eps) * norm_gain + norm_shift

def project(values, weight):
    return jnp.matmul(values, weight, precision=highest)

def forward(hidden_group, page_lengths, params):
    w_query, w_key, w_value, w_output, b_query, b_value, b_output, attn_gain, attn_shift, w_inner, b_inner, w_outer, b_outer, ffn_gain, ffn_shift = params
    page_group, seq_len, model_width = hidden_group.shape
    head_dim = model_width // HEADS
    queries = low_back(low(project(hidden_group, w_query) + b_query))
    key_rows = low_back(low(project(hidden_group, w_key)))
    value_rows = low_back(low(project(hidden_group, w_value) + b_value))
    head_shape = (page_group, seq_len, HEADS, head_dim)
    scores = jnp.einsum('pqhd,pkhd->phqk', queries.reshape(head_shape), key_rows.reshape(head_shape), precision=highest) * head_dim ** (-0.5)
    usable = jnp.arange(seq_len, dtype=jnp.int32)[None, :] < page_lengths[:, None]
    scores = low_back(jnp.where(usable[:, None, None, :], scores, masked_value))
    log_norm = jax.nn.logsumexp(scores, axis=-1, keepdims=True)
    attn_probs = low(jnp.exp(scores - log_norm))
    context = jnp.einsum('phqk,pkhd->pqhd', attn_probs, value_rows.reshape(head_shape), precision=highest).reshape(page_group, seq_len, model_width)
    context = low_back(low(context))
    residual_one = hidden_group + low_back(project(context, w_output) + b_output)
    normed_one = layer_norm(residual_one, attn_gain, attn_shift)
    pre_gelu = low_back(project(low(normed_one), w_inner) + b_inner)
    post_gelu = low(jax.nn.gelu(pre_gelu, approximate=False))
    residual_two = normed_one + low_back(project(post_gelu, w_outer) + b_outer)
    return layer_norm(residual_two, ffn_gain, ffn_shift)

def reference(hidden, lengths, w_query, w_key, w_value, w_output, b_query, b_value, b_output, attn_gain, attn_shift, w_inner, b_inner, w_outer, b_outer, ffn_gain, ffn_shift, cotangent):
    params = tuple((member.astype(jnp.float32) for member in (w_query, w_key, w_value, w_output, b_query, b_value, b_output, attn_gain, attn_shift, w_inner, b_inner, w_outer, b_outer, ffn_gain, ffn_shift)))
    page_group = math.gcd(PAGES, max(1, 4096 // PAGE_LEN))
    group_count = PAGES // page_group
    hidden_groups = hidden.astype(jnp.float32).reshape(group_count, page_group, PAGE_LEN, D)
    length_groups = lengths.astype(jnp.int32).reshape(group_count, page_group)
    cot_groups = cotangent.astype(jnp.float32).reshape(group_count, page_group, PAGE_LEN, D)

    def one_group(running, batch_item):
        hidden_group, page_lengths, cot_group = batch_item

        def wrapped(inputs, weight_list):
            return forward(inputs, page_lengths, weight_list)
        result, pull_back = jax.vjp(wrapped, hidden_group, params)
        input_grad, weight_grads = pull_back(cot_group)
        running = tuple((summed + addend for summed, addend in zip(running, weight_grads)))
        return (running, (result.astype(jnp.bfloat16), input_grad.astype(jnp.bfloat16)))
    start_sums = tuple((jnp.zeros(member.shape, jnp.float32) for member in params))
    totals, (results, input_grads) = lax.scan(one_group, start_sums, (hidden_groups, length_groups, cot_groups))
    layer_out = results.reshape(PAGES, PAGE_LEN, D)
    hidden_grad = input_grads.reshape(PAGES, PAGE_LEN, D)
    return (layer_out, hidden_grad, totals[0], totals[1], totals[2], totals[3], totals[4], totals[5], totals[6], totals[7], totals[8], totals[9], totals[10], totals[11], totals[12], totals[13], totals[14])
```

```python
import functools
import jax
import jax.numpy as jnp
from jax import lax
from jax.experimental import pallas as pl
from jax.experimental.pallas import tpu as pltpu

from jax.sharding import PartitionSpec as P

MESH = pl.DeviceIdType.MESH
VMEM = pltpu.VMEM
DMA = pltpu.SemaphoreType.DMA
BF = jnp.bfloat16
F32 = jnp.float32


def page_grid(pages):
    bits = pages.bit_length() - 1
    nx = 2 ** (bits // 3)
    ny = 2 ** ((bits - bits // 3) // 2)
    return pages // (nx * ny), ny, nx


class Place:
    def __init__(self, pages):
        self.nz, self.ny, self.nx = page_grid(pages)
        self.p = lax.axis_index("page")
        self.c = lax.axis_index("seq")
        self.x = lax.rem(self.p, self.nx)
        self.y = lax.rem(self.p // self.nx, self.ny)
        self.z = self.p // (self.nx * self.ny)

    def page(self, dz=0, dy=0, dx=0):
        z = lax.rem(self.z + dz + self.nz, self.nz)
        y = lax.rem(self.y + dy + self.ny, self.ny)
        x = lax.rem(self.x + dx + self.nx, self.nx)
        return (z * self.ny + y) * self.nx + x

    def partners(self):
        out = [(self.page(dz=d), self.c) for d in range(1, self.nz)]
        out += [(self.page(dy=d), self.c) for d in range(1, self.ny)]
        out += [(self.page(dx=d), self.c) for d in range(1, self.nx)]
        return out + [(self.p, 1 - self.c)]

    def greet(self):
        barrier = pltpu.get_barrier_semaphore()
        partners = self.partners()
        for partner in partners:
            pl.semaphore_signal(barrier, inc=1, device_id=partner, device_id_type=MESH)
        pl.semaphore_wait(barrier, len(partners))


def gather_slots(pages):
    nz, ny, nx = page_grid(pages)
    fx, fy = nx - 1, ny - 1
    base, at = {}, 0
    for name, size in (
        ("z", nz - 1), ("x", nz * fx), ("y", nz * fy), ("xa", nz * fx * fy),
        ("yb", nz * fx * fy), ("core", nz * ny * nx),
    ):
        base[name] = at
        at += size
    return base, at


class Gather:
    def __init__(self, place, ref, send, recv, kind):
        self.pl, self.ref, self.send, self.recv, self.kind = place, ref, send, recv, kind
        self.base, _ = gather_slots(place.nz * place.ny * place.nx)

    def view(self, block, part):
        ref = self.ref
        if part == "all" or self.kind == "small":
            return ref.at[:, block]
        half = 0 if part == "a" else 1
        if self.kind == "panels":
            n = ref.shape[0] // 2
            return ref.at[half * n:(half + 1) * n, block]
        n = ref.shape[2] // 2
        return ref.at[:, block, half * n:(half + 1) * n]

    def copy(self, name, slot, block, part, target):
        where = self.base[name] + slot
        view = self.view(block, part)
        return pltpu.make_async_remote_copy(
            src_ref=view, dst_ref=view, send_sem=self.send.at[where], recv_sem=self.recv.at[where],
            device_id=target, device_id_type=MESH)

    def block(self, dz=0, dy=0, dx=0):
        return 2 * self.pl.page(dz, dy, dx) + self.pl.c

    def z_copy(self, dz, mine):
        p = self.pl
        return self.copy("z", dz - 1, self.block(0 if mine else -dz), "all", (p.page(dz=dz), p.c))

    def x_copy(self, dx, dz, mine):
        p = self.pl
        return self.copy("x", dz * (p.nx - 1) + dx - 1, self.block(-dz, 0, 0 if mine else -dx), "all", (p.page(dx=dx), p.c))

    def y_copy(self, dy, dz, mine):
        p = self.pl
        return self.copy("y", dz * (p.ny - 1) + dy - 1, self.block(-dz, 0 if mine else -dy, 0), "all", (p.page(dy=dy), p.c))

    def diag_slot(self, dx, dy, dz):
        p = self.pl
        return (dz * (p.ny - 1) + dy - 1) * (p.nx - 1) + dx - 1

    def xa_copy(self, dx, dy, dz, mine):
        p = self.pl
        return self.copy("xa", self.diag_slot(dx, dy, dz), self.block(-dz, -dy, 0 if mine else -dx), "a", (p.page(dx=dx), p.c))

    def yb_copy(self, dx, dy, dz, mine):
        p = self.pl
        return self.copy("yb", self.diag_slot(dx, dy, dz), self.block(-dz, 0 if mine else -dy, -dx), "b", (p.page(dy=dy), p.c))

    def core_copy(self, dz, dy, dx, mine):
        p = self.pl
        slot = (dz * p.ny + dy) * p.nx + dx
        block = 2 * p.page(-dz, -dy, -dx) + (p.c if mine else 1 - p.c)
        return self.copy("core", slot, block, "all", (p.p, 1 - p.c))

    def spread(self, dz):
        p = self.pl
        for d in range(1, p.nx):
            self.x_copy(d, dz, True).start()
        for d in range(1, p.ny):
            self.y_copy(d, dz, True).start()
        self.core_copy(dz, 0, 0, True).start()

    def begin(self):
        for d in range(1, self.pl.nz):
            self.z_copy(d, True).start()
        self.spread(0)

    def column(self, dz):
        self.z_copy(dz, False).wait_recv()
        self.spread(dz)

    def plane(self, dz):
        p = self.pl
        for dy in range(1, p.ny):
            self.y_copy(dy, dz, False).wait_recv()
            for dx in range(1, p.nx):
                self.xa_copy(dx, dy, dz, True).start()
            self.core_copy(dz, dy, 0, True).start()
        for dx in range(1, p.nx):
            self.x_copy(dx, dz, False).wait_recv()
            if self.kind != "small":
                for dy in range(1, p.ny):
                    self.yb_copy(dx, dy, dz, True).start()
            self.core_copy(dz, 0, dx, True).start()

    def corner(self, dz):
        p = self.pl
        for dy in range(1, p.ny):
            for dx in range(1, p.nx):
                self.xa_copy(dx, dy, dz, False).wait_recv()
                if self.kind != "small":
                    self.yb_copy(dx, dy, dz, False).wait_recv()
                self.core_copy(dz, dy, dx, True).start()

    def finish_core(self):
        p = self.pl
        for dz in range(p.nz):
            for dy in range(p.ny):
                for dx in range(p.nx):
                    self.core_copy(dz, dy, dx, False).wait_recv()

    def drain(self):
        p = self.pl
        for d in range(1, p.nz):
            self.z_copy(d, True).wait_send()
        for dz in range(p.nz):
            for dx in range(1, p.nx):
                self.x_copy(dx, dz, True).wait_send()
            for dy in range(1, p.ny):
                self.y_copy(dy, dz, True).wait_send()
                for dx in range(1, p.nx):
                    self.xa_copy(dx, dy, dz, True).wait_send()
                    if self.kind != "small":
                        self.yb_copy(dx, dy, dz, True).wait_send()
            for dy in range(p.ny):
                for dx in range(p.nx):
                    self.core_copy(dz, dy, dx, True).wait_send()


def gather_kernel(pages, wq, wk, wv, wo, wi, wout, small, g_attn, g_inner, g_outer, g_small, *sems):
    place = Place(pages)
    mine = 2 * place.p + place.c
    for j, ref in enumerate((wq, wk, wv, wo)):
        g_attn[j, mine] = ref[...]
    width = g_inner.shape[3]
    for j in range(g_inner.shape[0]):
        g_inner[j, mine] = wi[:, j * width:(j + 1) * width]
    g_outer[0, mine] = wout[...]
    g_small[0, mine] = small[...]
    place.greet()
    segs = [
        Gather(place, ref, sems[2 * i], sems[2 * i + 1], kind)
        for i, (ref, kind) in enumerate(
            ((g_small, "small"), (g_attn, "panels"), (g_inner, "panels"), (g_outer, "rows")))
    ]
    groups = [segs[:2], segs[2:3], segs[3:]]
    for group in groups:
        for seg in group:
            seg.begin()
        for dz in range(1, place.nz):
            for seg in group:
                seg.column(dz)
        for dz in range(place.nz):
            for seg in group:
                seg.plane(dz)
        for dz in range(place.nz):
            for seg in group:
                seg.corner(dz)
    for seg in segs:
        seg.finish_core()
    for seg in segs:
        seg.drain()


def gather_weights(pages, wq, wk, wv, wo, wi, wout, small):
    rows, width = wq.shape
    devices = 2 * pages
    panels = wi.shape[1] // width
    _, slots = gather_slots(pages)
    v = pl.BlockSpec(memory_space=VMEM)
    return pl.pallas_call(
        functools.partial(gather_kernel, pages),
        name="gather_weights",
        out_shape=(
            jax.ShapeDtypeStruct((4, devices, rows, width), BF),
            jax.ShapeDtypeStruct((panels, devices, rows, width), BF),
            jax.ShapeDtypeStruct((1, devices, wout.shape[0], width), BF),
            jax.ShapeDtypeStruct((1, devices) + small.shape, BF),
        ),
        in_specs=[v] * 7,
        out_specs=(v,) * 4,
        scratch_shapes=[DMA((slots,))] * 8,
        compiler_params=pltpu.CompilerParams(collective_id=0, has_side_effects=True, vmem_limit_bytes=40 << 20),
    )(wq, wk, wv, wo, wi, wout, small)


def reduce_slots(pages):
    nz, ny, nx = page_grid(pages)
    fx, fy = nx - 1, ny - 1
    base, at = {}, 0
    for name, size in (
        ("core", nz * ny * nx), ("xa", nz * fx * fy), ("yb", nz * fx * fy), ("x", nz * fx), ("y", nz * fy), ("z", nz - 1),
    ):
        base[name] = at
        at += size
    return base, at


def reduce_scratch(pages, panels, rows, width, kind):
    nz, ny, nx = page_grid(pages)
    fx, fy = nx - 1, ny - 1
    half = (panels // 2, rows) if kind == "panels" else (panels, rows // 2)
    _, slots = reduce_slots(pages)
    return [
        VMEM((panels, nz * ny * nx, rows, width), BF),
        VMEM((nz * fx * fy,) + half + (width,), BF),
        VMEM((nz * fx * fy,) + half + (width,), BF),
        VMEM((nz * fx, panels, rows, width), BF),
        VMEM((nz * fy, panels, rows, width), BF),
        VMEM((nz - 1, panels, rows, width), BF),
        DMA((slots,)),
        DMA((slots,)),
    ]


class Reduce:
    def __init__(self, place, part, scratch, kind):
        self.pl, self.part, self.kind = place, part, kind
        self.total, self.da, self.db, self.rx, self.ry, self.rz, self.send, self.recv = scratch
        self.base, _ = reduce_slots(place.nz * place.ny * place.nx)

    def remote(self, name, slot, src, dst, target):
        where = self.base[name] + slot
        return pltpu.make_async_remote_copy(
            src_ref=src, dst_ref=dst, send_sem=self.send.at[where], recv_sem=self.recv.at[where],
            device_id=target, device_id_type=MESH)

    def half(self, page, which):
        if self.kind == "panels":
            n = self.total.shape[0] // 2
            return self.total.at[which * n:(which + 1) * n, page]
        n = self.total.shape[2] // 2
        return self.total.at[:, page, which * n:(which + 1) * n]

    def core_copy(self, dz, dy, dx):
        p = self.pl
        page = p.page(dz, dy, dx)
        return self.remote("core", (dz * p.ny + dy) * p.nx + dx, self.part.at[:, page, 1 - p.c], self.total.at[:, page], (p.p, 1 - p.c))

    def diag(self, dz, dy, dx):
        p = self.pl
        return (dz * (p.ny - 1) + dy - 1) * (p.nx - 1) + dx - 1

    def xa_copy(self, dz, dy, dx):
        p, slot = self.pl, self.diag(dz, dy, dx)
        return self.remote("xa", slot, self.half(p.page(dz, dy, dx), 0), self.da.at[slot], (p.page(dx=dx), p.c))

    def yb_copy(self, dz, dy, dx):
        p, slot = self.pl, self.diag(dz, dy, dx)
        return self.remote("yb", slot, self.half(p.page(dz, dy, dx), 1), self.db.at[slot], (p.page(dy=dy), p.c))

    def x_copy(self, dz, dx):
        p = self.pl
        slot = dz * (p.nx - 1) + dx - 1
        return self.remote("x", slot, self.total.at[:, p.page(dz, 0, dx)], self.rx.at[slot], (p.page(dx=dx), p.c))

    def y_copy(self, dz, dy):
        p = self.pl
        slot = dz * (p.ny - 1) + dy - 1
        return self.remote("y", slot, self.total.at[:, p.page(dz, dy, 0)], self.ry.at[slot], (p.page(dy=dy), p.c))

    def z_copy(self, dz):
        p = self.pl
        return self.remote("z", dz - 1, self.total.at[:, p.page(dz, 0, 0)], self.rz.at[dz - 1], (p.page(dz=dz), p.c))

    def begin(self):
        p = self.pl
        order = [(dy, dx) for dy in range(1, p.ny) for dx in range(1, p.nx)]
        order += [(0, dx) for dx in range(1, p.nx)] + [(dy, 0) for dy in range(1, p.ny)] + [(0, 0)]
        for dy, dx in order:
            for dz in range(p.nz):
                self.core_copy(dz, dy, dx).start()

    def pair(self, dz, dy, dx):
        p = self.pl
        self.core_copy(dz, dy, dx).wait_recv()
        page = p.page(dz, dy, dx)
        return self.part[:, page, p.c].astype(F32) + self.total[:, page].astype(F32)

    def corner(self, dz):
        p = self.pl
        for dy in range(1, p.ny):
            for dx in range(1, p.nx):
                self.total[:, p.page(dz, dy, dx)] = self.pair(dz, dy, dx).astype(BF)
                self.xa_copy(dz, dy, dx).start()
                self.yb_copy(dz, dy, dx).start()

    def plane(self, dz):
        p = self.pl
        panels, rows = self.total.shape[0], self.total.shape[2]
        for dx in range(1, p.nx):
            total = self.pair(dz, 0, dx)
            page = p.page(dz, 0, dx)
            for dy in range(1, p.ny):
                self.yb_copy(dz, dy, dx).wait_recv()
                add = self.db[self.diag(dz, dy, dx)].astype(F32)
                if self.kind == "panels":
                    n = panels // 2
                    total = jnp.concatenate([total[:n], total[n:] + add], axis=0)
                else:
                    n = rows // 2
                    total = jnp.concatenate([total[:, :n], total[:, n:] + add], axis=1)
            self.total[:, page] = total.astype(BF)
            self.x_copy(dz, dx).start()
        for dy in range(1, p.ny):
            total = self.pair(dz, dy, 0)
            page = p.page(dz, dy, 0)
            for dx in range(1, p.nx):
                self.xa_copy(dz, dy, dx).wait_recv()
                add = self.da[self.diag(dz, dy, dx)].astype(F32)
                if self.kind == "panels":
                    n = panels // 2
                    total = jnp.concatenate([total[:n] + add, total[n:]], axis=0)
                else:
                    n = rows // 2
                    total = jnp.concatenate([total[:, :n] + add, total[:, n:]], axis=1)
            self.total[:, page] = total.astype(BF)
            self.y_copy(dz, dy).start()

    def column_sum(self, dz):
        p = self.pl
        total = self.pair(dz, 0, 0)
        for dx in range(1, p.nx):
            self.x_copy(dz, dx).wait_recv()
            total += self.rx[dz * (p.nx - 1) + dx - 1].astype(F32)
        for dy in range(1, p.ny):
            self.y_copy(dz, dy).wait_recv()
            total += self.ry[dz * (p.ny - 1) + dy - 1].astype(F32)
        return total

    def column(self, dz):
        self.total[:, self.pl.page(dz, 0, 0)] = self.column_sum(dz).astype(BF)
        self.z_copy(dz).start()

    def finish(self):
        total = self.column_sum(0)
        for dz in range(1, self.pl.nz):
            self.z_copy(dz).wait_recv()
            total += self.rz[dz - 1].astype(F32)
        return total

    def drain(self):
        p = self.pl

        def one(dz, _):
            for dy in range(p.ny):
                for dx in range(p.nx):
                    self.core_copy(dz, dy, dx).wait_send()
            for dy in range(1, p.ny):
                for dx in range(1, p.nx):
                    self.xa_copy(dz, dy, dx).wait_send()
                    self.yb_copy(dz, dy, dx).wait_send()
            for dx in range(1, p.nx):
                self.x_copy(dz, dx).wait_send()
            for dy in range(1, p.ny):
                self.y_copy(dz, dy).wait_send()
            return 0

        lax.fori_loop(0, p.nz, one, 0)
        for dz in range(1, p.nz):
            self.z_copy(dz).wait_send()


def vector_scratch(pages, rows, width):
    nz, ny, nx = page_grid(pages)
    n = 1 + nx - 1 + ny - 1 + nz - 1
    return [VMEM((4, rows, width), F32), VMEM((n, rows, width), F32), DMA((n,)), DMA((n,))]


class VectorSum:
    def __init__(self, place, scratch):
        self.pl = place
        self.held, self.got, self.send, self.recv = scratch

    def legs(self):
        p = self.pl
        return [
            [(p.p, 1 - p.c)],
            [(p.page(dx=d), p.c) for d in range(1, p.nx)],
            [(p.page(dy=d), p.c) for d in range(1, p.ny)],
            [(p.page(dz=d), p.c) for d in range(1, p.nz)],
        ]

    def copies(self, leg):
        legs = self.legs()
        at = sum(len(one) for one in legs[:leg])
        return [
            pltpu.make_async_remote_copy(
                src_ref=self.held.at[leg], dst_ref=self.got.at[at + i], send_sem=self.send.at[at + i],
                recv_sem=self.recv.at[at + i], device_id=target, device_id_type=MESH)
            for i, target in enumerate(legs[leg])
        ], at

    def put(self, leg, value):
        self.held[leg] = value
        for copy in self.copies(leg)[0]:
            copy.start()

    def take(self, leg):
        copies, at = self.copies(leg)
        value = self.held[leg]
        for i, copy in enumerate(copies):
            copy.wait_recv()
            value += self.got[at + i]
        return value

    def drain(self):
        for leg in range(4):
            for copy in self.copies(leg)[0]:
                copy.wait_send()


def reduce_kernel(pages, p_attn, p_inner, p_outer, vec, o_q, o_k, o_v, o_o, o_inner, o_outer, o_vec, *scratch):
    place = Place(pages)
    outer = Reduce(place, p_outer, scratch[0:8], "rows")
    inner = Reduce(place, p_inner, scratch[8:16], "panels")
    attn = Reduce(place, p_attn, scratch[16:24], "panels")
    vectors = VectorSum(place, scratch[24:28])
    place.greet()
    nz = place.nz
    segs = (outer, inner, attn)
    vectors.put(0, vec[...])
    for seg in segs:
        seg.begin()

    def loop(start, body):
        def one(dz, _):
            body(dz)
            return 0
        lax.fori_loop(start, nz, one, 0)

    loop(0, outer.corner)
    vectors.put(1, vectors.take(0))
    loop(0, inner.corner)
    loop(0, outer.plane)
    vectors.put(2, vectors.take(1))
    loop(0, attn.corner)
    loop(0, inner.plane)
    vectors.put(3, vectors.take(2))
    loop(1, outer.column)
    loop(0, attn.plane)
    loop(1, inner.column)
    o_outer[...] = outer.finish()[0]
    o_vec[...] = vectors.take(3)
    loop(1, attn.column)
    total = inner.finish()
    width = total.shape[2]
    for j in range(total.shape[0]):
        o_inner[:, j * width:(j + 1) * width] = total[j]
    total = attn.finish()
    for j, ref in enumerate((o_q, o_k, o_v, o_o)):
        ref[...] = total[j]
    for seg in segs:
        seg.drain()
    vectors.drain()


def reduce_grads(pages, p_attn, p_inner, p_outer, vec):
    panels, width = p_inner.shape[0], p_inner.shape[4]
    rows, rows_outer = p_inner.shape[3], p_outer.shape[3]
    v = pl.BlockSpec(memory_space=VMEM)
    square = jax.ShapeDtypeStruct((rows, width), F32)
    return pl.pallas_call(
        functools.partial(reduce_kernel, pages),
        name="reduce_grads",
        out_shape=(square,) * 4 + (
            jax.ShapeDtypeStruct((rows, panels * width), F32),
            jax.ShapeDtypeStruct((rows_outer, width), F32),
            jax.ShapeDtypeStruct(vec.shape, F32),
        ),
        in_specs=[v] * 4,
        out_specs=(v,) * 7,
        scratch_shapes=reduce_scratch(pages, 1, rows_outer, width, "rows")
        + reduce_scratch(pages, panels, rows, width, "panels")
        + reduce_scratch(pages, 4, rows, width, "panels")
        + vector_scratch(pages, *vec.shape),
        compiler_params=pltpu.CompilerParams(collective_id=1, has_side_effects=True, vmem_limit_bytes=56 << 20),
    )(p_attn, p_inner, p_outer, vec)


HEADS = 12


masked_value = -1e30
norm_eps = 1e-06


def layer_norm(values, norm_gain, norm_shift):
    centre = jnp.mean(values, axis=-1, keepdims=True)
    centered = values - centre
    spread = jnp.mean(centered * centered, axis=-1, keepdims=True)
    return centered * lax.rsqrt(spread + norm_eps) * norm_gain + norm_shift


def gelu_exact(values):
    return jax.nn.gelu(values, approximate=False)


def matmul(left_side, right_side):
    return jnp.dot(left_side, right_side, preferred_element_type=jnp.float32)


def column_sum(values):
    return jnp.sum(values.astype(jnp.float32), axis=0)


def usable_keys(page_lengths, seg_len):
    places = lax.broadcasted_iota(jnp.int32, (page_lengths.shape[0], seg_len), 1)
    return places < page_lengths[:, None]


def head_split(values, head_count):
    return values.reshape(
        values.shape[0], values.shape[1], head_count, values.shape[2] // head_count
    )


def page_scores(query_heads, key_piece, usable, score_scale):
    key_heads = head_split(key_piece, query_heads.shape[2])
    scores = (
        jnp.einsum("pqhd,pkhd->phqk", query_heads, key_heads, preferred_element_type=jnp.float32)
        * score_scale
    )
    return jnp.where(usable[:, None, None, :], scores, masked_value)


AXES = ("page", "seq")
VECTORS = 8


def pack_vectors(vectors, inner):
    lanes = 128
    rows = [jnp.pad(v, (0, lanes - v.shape[0])) for v in (*vectors, inner)]
    rows += [jnp.zeros((lanes,), BF)] * (16 - len(rows))
    return jnp.stack(rows)


def unpack_vectors(small, rows):
    vectors = [small[:, j, :rows].reshape(-1) for j in range(VECTORS)]
    return vectors + [small[:, VECTORS, : 4 * rows].reshape(-1)]


def gather_all(pages, wq, wk, wv, wo, wi, wout, vectors, b_inner):
    rows, width = wq.shape
    panels = wi.shape[1] // width
    if rows % 8 == 0:
        small = pack_vectors(vectors, b_inner)
        ga, gi, go, gs = gather_weights(pages, wq, wk, wv, wo, wi, wout, small)
        full = width, width
        return ga.reshape(4, *full), gi.reshape(panels, *full), go.reshape(-1, width), unpack_vectors(gs[0], rows)
    spread = lambda w: lax.all_gather(w, AXES, axis=0, tiled=True)
    ga = lax.all_gather(jnp.stack((wq, wk, wv, wo)), AXES, axis=1, tiled=True)
    gi = lax.all_gather(wi.reshape(rows, panels, width).transpose(1, 0, 2), AXES, axis=1, tiled=True)
    return ga, gi, spread(wout), [spread(v) for v in (*vectors, b_inner)]


def reduce_all(pages, pa, pi, po, vec):
    panels, width = pi.shape[0], pi.shape[2]
    rows = width // (2 * pages)
    at = lax.axis_index("page") * 2 + lax.axis_index("seq")
    if rows % 8 == 0:
        split = lambda p: p.reshape(p.shape[0], pages, 2, -1, width)
        *squares, o_inner, o_outer, total = reduce_grads(pages, split(pa), split(pi), split(po[None]), vec)
    else:
        scatter = lambda g, d: lax.psum_scatter(g.astype(F32), AXES, scatter_dimension=d, tiled=True)
        squares = list(scatter(pa, 1))
        o_inner = scatter(pi, 1).transpose(1, 0, 2).reshape(rows, -1)
        o_outer = scatter(po, 0)
        total = lax.psum(vec, AXES)
    vectors = [lax.dynamic_slice(total, (j, rows * at), (1, rows))[0] for j in range(VECTORS)]
    flat = total[VECTORS : VECTORS + panels].reshape(-1)
    return squares, o_inner, o_outer, vectors, lax.dynamic_slice(flat, (panels * rows * at,), (panels * rows,))


def per_device(
    page_count,
    hidden,
    lengths,
    w_query,
    w_key,
    w_value,
    w_output,
    b_query,
    b_value,
    b_output,
    attn_gain,
    attn_shift,
    w_inner,
    b_inner,
    w_outer,
    b_outer,
    ffn_gain,
    ffn_shift,
    cotangent,
):
    model_width = hidden.shape[2]
    head_count = HEADS
    score_scale = (model_width // head_count) ** (-0.5)
    f32 = jnp.float32
    bf16 = jnp.bfloat16
    work_hidden, work_cot = (hidden, cotangent)
    local_pages, local_tokens = (work_hidden.shape[0], work_hidden.shape[1])
    row_count = local_pages * local_tokens
    pages = page_count
    ga, gi, go, vectors = gather_all(
        pages, w_query, w_key, w_value, w_output, w_inner, w_outer,
        (b_query, b_value, b_output, attn_gain, attn_shift, b_outer, ffn_gain, ffn_shift), b_inner)
    query_full, key_full, value_full, output_full = ga[0], ga[1], ga[2], ga[3]
    query_bias, value_bias, output_bias, gain_one, shift_one, outer_bias, gain_two, shift_two, inner_bias = vectors
    outer_full = go
    panels = gi.shape[0]
    flat_rows = work_hidden.reshape(row_count, model_width)
    queries = (matmul(flat_rows, query_full) + query_bias.astype(f32)).astype(bf16)
    key_rows = matmul(flat_rows, key_full).astype(bf16)
    value_rows = (matmul(flat_rows, value_full) + value_bias.astype(f32)).astype(bf16)
    query_heads = head_split(queries.reshape(local_pages, local_tokens, model_width), head_count)
    key_pages = key_rows.reshape(local_pages, local_tokens, model_width)
    value_pages = value_rows.reshape(local_pages, local_tokens, model_width)
    stat_shape = (local_pages, head_count, local_tokens)
    stat_start = (jnp.full(stat_shape, masked_value, f32), jnp.zeros(stat_shape, f32))
    key_piece = lax.all_gather(key_pages, "seq", axis=1, tiled=True)
    usable = usable_keys(lengths, key_piece.shape[1])

    def merged():
        run_peak, run_total = stat_start
        scores = page_scores(query_heads, key_piece, usable, score_scale)
        new_peak = jnp.maximum(run_peak, jnp.max(scores, axis=-1))
        summed = jnp.sum(jnp.exp(scores - new_peak[..., None]), axis=-1)
        return (new_peak, summed)

    run_peak, run_total = merged()
    log_norm = run_peak + jnp.log(run_total)
    add_key_piece = lax.all_gather(key_pages, "seq", axis=1, tiled=True)
    value_piece = lax.all_gather(value_pages, "seq", axis=1, tiled=True)
    add_usable = usable_keys(lengths, add_key_piece.shape[1])

    def merged():
        scores = page_scores(query_heads, add_key_piece, add_usable, score_scale)
        attn_probs = jnp.exp(scores - log_norm[..., None]).astype(bf16)
        addend = jnp.einsum(
            "phqk,pkhd->pqhd",
            attn_probs,
            head_split(value_piece, head_count),
            preferred_element_type=f32,
        )
        return addend.reshape(local_pages, local_tokens, model_width)

    context = merged()
    context_low = context.astype(bf16).reshape(row_count, model_width)
    residual_one = (
        flat_rows.astype(f32) + matmul(context_low, output_full) + output_bias.astype(f32)
    )
    normed_one, pull_one = jax.vjp(
        layer_norm, residual_one, gain_one.astype(f32), shift_one.astype(f32)
    )
    normed_low = normed_one.astype(bf16)
    inner_full = gi.transpose(1, 0, 2).reshape(model_width, -1)
    pre_gelu = matmul(normed_low, inner_full) + inner_bias.astype(f32)
    post_gelu, pull_gelu = jax.vjp(gelu_exact, pre_gelu)
    post_low = post_gelu.astype(bf16)
    residual_two = normed_one + matmul(post_low, outer_full) + outer_bias.astype(f32)
    layer_out, pull_two = jax.vjp(
        layer_norm, residual_two, gain_two.astype(f32), shift_two.astype(f32)
    )
    cot_rows = work_cot.reshape(row_count, model_width).astype(f32)
    d_res_two, gain_two_grad, shift_two_grad = pull_two(cot_rows)
    d_outer = d_res_two.astype(bf16)
    outer_w_grad = matmul(post_low.T, d_outer)
    outer_b_grad = column_sum(d_outer)
    (d_pre_full,) = pull_gelu(matmul(d_outer, outer_full.T))
    d_pre = d_pre_full.astype(bf16)
    inner_w_grad = matmul(normed_low.T, d_pre)
    inner_b_grad = column_sum(d_pre)
    d_normed = d_res_two + matmul(d_pre, inner_full.T)
    d_res_one, gain_one_grad, shift_one_grad = pull_one(d_normed)
    d_attn = d_res_one.astype(bf16)
    output_w_grad = matmul(context_low.T, d_attn)
    output_b_grad = column_sum(d_attn)
    d_context = matmul(d_attn, output_full.T).astype(bf16)
    d_context_heads = head_split(
        d_context.reshape(local_pages, local_tokens, model_width), head_count
    )
    context_heads = head_split(context, head_count)
    row_delta = jnp.transpose(
        jnp.sum(d_context_heads.astype(f32) * context_heads, axis=-1), (0, 2, 1)
    )

    def add_grads(segment):
        key_piece, value_piece = segment
        seg_len = key_piece.shape[1]
        usable = usable_keys(lengths, seg_len)

        def merged():
            scores = page_scores(query_heads, key_piece, usable, score_scale)
            attn_probs = jnp.exp(scores - log_norm[..., None])
            key_heads = head_split(key_piece, head_count)
            value_heads = head_split(value_piece, head_count)
            d_probs = jnp.einsum(
                "pqhd,pkhd->phqk", d_context_heads, value_heads, preferred_element_type=f32
            )
            d_scores = (attn_probs * (d_probs - row_delta[..., None])).astype(bf16)
            query_part = jnp.einsum(
                "phqk,pkhd->pqhd", d_scores, key_heads, preferred_element_type=f32
            )
            key_part = jnp.einsum(
                "phqk,pqhd->pkhd", d_scores, query_heads, preferred_element_type=f32
            )
            value_part = jnp.einsum(
                "phqk,pqhd->pkhd",
                attn_probs.astype(bf16),
                d_context_heads,
                preferred_element_type=f32,
            )
            query_grad = query_part.reshape(local_pages, local_tokens, model_width) * score_scale
            key_grads = key_part.reshape(local_pages, seg_len, model_width) * score_scale
            value_grads = value_part.reshape(local_pages, seg_len, model_width)
            return (query_grad, key_grads, value_grads)

        return merged()

    query_grad, key_grads, value_grads = add_grads(
        (
            lax.all_gather(key_pages, "seq", axis=1, tiled=True),
            lax.all_gather(value_pages, "seq", axis=1, tiled=True),
        )
    )
    key_owned, value_owned = (
        lax.psum_scatter(
            key_grads.astype(jnp.bfloat16), "seq", scatter_dimension=1, tiled=True
        ).astype(jnp.float32),
        lax.psum_scatter(
            value_grads.astype(jnp.bfloat16), "seq", scatter_dimension=1, tiled=True
        ).astype(jnp.float32),
    )
    d_queries = query_grad.astype(bf16).reshape(row_count, model_width)
    d_keys = key_owned.astype(bf16).reshape(row_count, model_width)
    d_values = value_owned.astype(bf16).reshape(row_count, model_width)
    query_w_grad = matmul(flat_rows.T, d_queries)
    key_w_grad = matmul(flat_rows.T, d_keys)
    value_w_grad = matmul(flat_rows.T, d_values)
    query_b_grad = column_sum(d_queries)
    value_b_grad = column_sum(d_values)
    hidden_grad = (
        d_res_one
        + matmul(d_queries, query_full.T)
        + matmul(d_keys, key_full.T)
        + matmul(d_values, value_full.T)
    ).astype(bf16)
    pa = jnp.stack([g.astype(bf16) for g in (query_w_grad, key_w_grad, value_w_grad, output_w_grad)])
    pi = inner_w_grad.astype(bf16).reshape(model_width, panels, model_width).transpose(1, 0, 2)
    po = outer_w_grad.astype(bf16)
    singles = (query_b_grad, value_b_grad, output_b_grad, gain_one_grad, shift_one_grad, outer_b_grad, gain_two_grad, shift_two_grad)
    vec = jnp.concatenate([jnp.stack(singles), inner_b_grad.reshape(panels, model_width)])
    vec = jnp.pad(vec, ((0, 16 - vec.shape[0]), (0, 0)))
    squares, o_inner, o_outer, owned, o_inner_bias = reduce_all(pages, pa, pi, po, vec)
    out_pages = layer_out.astype(bf16).reshape(local_pages, local_tokens, model_width)
    grad_pages = hidden_grad.reshape(local_pages, local_tokens, model_width)
    return (
        out_pages, grad_pages, *squares, owned[0], owned[1], owned[2], owned[3], owned[4],
        o_inner, o_inner_bias, o_outer, owned[5], owned[6], owned[7])


def solution(mesh):
    in_specs = (
        P("page", "seq", None),
        P("page"),
        P(("page", "seq"), None),
        P(("page", "seq"), None),
        P(("page", "seq"), None),
        P(("page", "seq"), None),
        P(("page", "seq")),
        P(("page", "seq")),
        P(("page", "seq")),
        P(("page", "seq")),
        P(("page", "seq")),
        P(("page", "seq"), None),
        P(("page", "seq")),
        P(("page", "seq"), None),
        P(("page", "seq")),
        P(("page", "seq")),
        P(("page", "seq")),
        P("page", "seq", None),
    )
    out_specs = (
        P("page", "seq", None),
        P("page", "seq", None),
        P(("page", "seq"), None),
        P(("page", "seq"), None),
        P(("page", "seq"), None),
        P(("page", "seq"), None),
        P(("page", "seq")),
        P(("page", "seq")),
        P(("page", "seq")),
        P(("page", "seq")),
        P(("page", "seq")),
        P(("page", "seq"), None),
        P(("page", "seq")),
        P(("page", "seq"), None),
        P(("page", "seq")),
        P(("page", "seq")),
        P(("page", "seq")),
    )
    return jax.shard_map(
        functools.partial(per_device, mesh.shape["page"]), mesh=mesh, in_specs=in_specs, out_specs=out_specs, check_vma=False
    )
```

```python
import functools
import types
import jax
import jax.numpy as jnp
from jax import lax
from jax.experimental import pallas as pl
from jax.experimental.pallas import tpu as pltpu

from jax.sharding import PartitionSpec as P

MESH = pl.DeviceIdType.MESH
VMEM = pltpu.VMEM
DMA = pltpu.SemaphoreType.DMA
BF = jnp.bfloat16
F32 = jnp.float32
AXES = PAGE, SEQ = ("page", "seq")
SMALL, PANELS, ROWS = range(3)


def page_grid(pages):
    bits = pages.bit_length() - 1
    nx = 2 ** (bits // 3)
    ny = 2 ** ((bits - bits // 3) // 2)
    return pages // (nx * ny), ny, nx


class Place:
    def __init__(self, pages):
        self.nz, self.ny, self.nx = page_grid(pages)
        self.p = lax.axis_index(PAGE)
        self.c = lax.axis_index(SEQ)
        self.x = lax.rem(self.p, self.nx)
        self.y = lax.rem(self.p // self.nx, self.ny)
        self.z = self.p // (self.nx * self.ny)

    def page(self, dz=0, dy=0, dx=0):
        z = lax.rem(self.z + dz + self.nz, self.nz)
        y = lax.rem(self.y + dy + self.ny, self.ny)
        x = lax.rem(self.x + dx + self.nx, self.nx)
        return (z * self.ny + y) * self.nx + x

    def partners(self):
        out = [(self.page(dz=d), self.c) for d in range(1, self.nz)]
        out += [(self.page(dy=d), self.c) for d in range(1, self.ny)]
        out += [(self.page(dx=d), self.c) for d in range(1, self.nx)]
        return out + [(self.p, 1 - self.c)]

    def greet(self):
        barrier = pltpu.get_barrier_semaphore()
        partners = self.partners()
        for partner in partners:
            pl.semaphore_signal(barrier, inc=1, device_id=partner, device_id_type=MESH)
        pl.semaphore_wait(barrier, len(partners))


def gather_slots(pages):
    nz, ny, nx = page_grid(pages)
    fx, fy = nx - 1, ny - 1
    base, at = {}, 0
    for name, size in (
        ("z", nz - 1), ("x", nz * fx), ("y", nz * fy), ("xa", nz * fx * fy),
        ("yb", nz * fx * fy), ("core", nz * ny * nx),
    ):
        base[name] = at
        at += size
    return base, at


class Gather:
    def __init__(self, place, ref, send, recv, kind):
        self.pl, self.ref, self.send, self.recv, self.kind = place, ref, send, recv, kind
        self.base, _ = gather_slots(place.nz * place.ny * place.nx)

    def view(self, block, part):
        ref = self.ref
        if part == "all" or self.kind == SMALL:
            return ref.at[:, block]
        half = 0 if part == "a" else 1
        if self.kind == PANELS:
            n = ref.shape[0] // 2
            return ref.at[half * n:(half + 1) * n, block]
        n = ref.shape[2] // 2
        return ref.at[:, block, half * n:(half + 1) * n]

    def copy(self, name, slot, block, part, target):
        where = self.base[name] + slot
        view = self.view(block, part)
        return pltpu.make_async_remote_copy(
            src_ref=view, dst_ref=view, send_sem=self.send.at[where], recv_sem=self.recv.at[where],
            device_id=target, device_id_type=MESH)

    def block(self, dz=0, dy=0, dx=0):
        return 2 * self.pl.page(dz, dy, dx) + self.pl.c

    def z_copy(self, dz, mine):
        p = self.pl
        return self.copy("z", dz - 1, self.block(0 if mine else -dz), "all", (p.page(dz=dz), p.c))

    def x_copy(self, dx, dz, mine):
        p = self.pl
        return self.copy("x", dz * (p.nx - 1) + dx - 1, self.block(-dz, 0, 0 if mine else -dx), "all", (p.page(dx=dx), p.c))

    def y_copy(self, dy, dz, mine):
        p = self.pl
        return self.copy("y", dz * (p.ny - 1) + dy - 1, self.block(-dz, 0 if mine else -dy, 0), "all", (p.page(dy=dy), p.c))

    def diag_slot(self, dx, dy, dz):
        p = self.pl
        return (dz * (p.ny - 1) + dy - 1) * (p.nx - 1) + dx - 1

    def xa_copy(self, dx, dy, dz, mine):
        p = self.pl
        return self.copy("xa", self.diag_slot(dx, dy, dz), self.block(-dz, -dy, 0 if mine else -dx), "a", (p.page(dx=dx), p.c))

    def yb_copy(self, dx, dy, dz, mine):
        p = self.pl
        return self.copy("yb", self.diag_slot(dx, dy, dz), self.block(-dz, 0 if mine else -dy, -dx), "b", (p.page(dy=dy), p.c))

    def core_copy(self, dz, dy, dx, mine):
        p = self.pl
        slot = (dz * p.ny + dy) * p.nx + dx
        block = 2 * p.page(-dz, -dy, -dx) + (p.c if mine else 1 - p.c)
        return self.copy("core", slot, block, "all", (p.p, 1 - p.c))

    def spread(self, dz):
        p = self.pl
        for d in range(1, p.nx):
            self.x_copy(d, dz, True).start()
        for d in range(1, p.ny):
            self.y_copy(d, dz, True).start()
        self.core_copy(dz, 0, 0, True).start()

    def begin_z(self):
        for d in range(1, self.pl.nz):
            self.z_copy(d, True).start()

    def column(self, dz):
        self.z_copy(dz, False).wait_recv()
        self.spread(dz)

    def plane(self, dz):
        p = self.pl
        for dy in range(1, p.ny):
            self.y_copy(dy, dz, False).wait_recv()
            for dx in range(1, p.nx):
                self.xa_copy(dx, dy, dz, True).start()
            self.core_copy(dz, dy, 0, True).start()
        for dx in range(1, p.nx):
            self.x_copy(dx, dz, False).wait_recv()
            if self.kind != SMALL:
                for dy in range(1, p.ny):
                    self.yb_copy(dx, dy, dz, True).start()
            self.core_copy(dz, 0, dx, True).start()

    def corner(self, dz):
        p = self.pl
        for dy in range(1, p.ny):
            for dx in range(1, p.nx):
                self.xa_copy(dx, dy, dz, False).wait_recv()
                if self.kind != SMALL:
                    self.yb_copy(dx, dy, dz, False).wait_recv()
                self.core_copy(dz, dy, dx, True).start()

    def finish_core(self):
        p = self.pl
        for dz in range(p.nz):
            for dy in range(p.ny):
                for dx in range(p.nx):
                    self.core_copy(dz, dy, dx, False).wait_recv()

    def drain(self):
        p = self.pl
        for d in range(1, p.nz):
            self.z_copy(d, True).wait_send()
        for dz in range(p.nz):
            for dx in range(1, p.nx):
                self.x_copy(dx, dz, True).wait_send()
            for dy in range(1, p.ny):
                self.y_copy(dy, dz, True).wait_send()
                for dx in range(1, p.nx):
                    self.xa_copy(dx, dy, dz, True).wait_send()
                    if self.kind != SMALL:
                        self.yb_copy(dx, dy, dz, True).wait_send()
            for dy in range(p.ny):
                for dx in range(p.nx):
                    self.core_copy(dz, dy, dx, True).wait_send()


def reduce_slots(pages):
    nz, ny, nx = page_grid(pages)
    fx, fy = nx - 1, ny - 1
    base, at = {}, 0
    for name, size in (
        ("core", nz * ny * nx), ("xa", nz * fx * fy), ("yb", nz * fx * fy), ("x", nz * fx), ("y", nz * fy), ("z", nz - 1),
    ):
        base[name] = at
        at += size
    return base, at


def reduce_scratch(pages, panels, rows, width, kind):
    nz, ny, nx = page_grid(pages)
    fx, fy = nx - 1, ny - 1
    half = (panels // 2, rows) if kind == PANELS else (panels, rows // 2)
    _, slots = reduce_slots(pages)
    return [
        VMEM((panels, nz * ny * nx, rows, width), BF),
        VMEM((nz * fx * fy,) + half + (width,), BF),
        VMEM((nz * fx * fy,) + half + (width,), BF),
        VMEM((nz * fx, panels, rows, width), BF),
        VMEM((nz * fy, panels, rows, width), BF),
        VMEM((nz - 1, panels, rows, width), BF),
        DMA((slots,)),
        DMA((slots,)),
    ]


class Reduce:
    def __init__(self, place, part, scratch, kind):
        self.pl, self.part, self.kind = place, part, kind
        self.total, self.da, self.db, self.rx, self.ry, self.rz, self.send, self.recv = scratch
        self.base, _ = reduce_slots(place.nz * place.ny * place.nx)

    def remote(self, name, slot, src, dst, target):
        where = self.base[name] + slot
        return pltpu.make_async_remote_copy(
            src_ref=src, dst_ref=dst, send_sem=self.send.at[where], recv_sem=self.recv.at[where],
            device_id=target, device_id_type=MESH)

    def half(self, page, which):
        if self.kind == PANELS:
            n = self.total.shape[0] // 2
            return self.total.at[which * n:(which + 1) * n, page]
        n = self.total.shape[2] // 2
        return self.total.at[:, page, which * n:(which + 1) * n]

    def core_copy(self, dz, dy, dx):
        p = self.pl
        page = p.page(dz, dy, dx)
        return self.remote("core", (dz * p.ny + dy) * p.nx + dx, self.part.at[:, 2 * page + 1 - p.c], self.total.at[:, page], (p.p, 1 - p.c))

    def diag(self, dz, dy, dx):
        p = self.pl
        return (dz * (p.ny - 1) + dy - 1) * (p.nx - 1) + dx - 1

    def xa_copy(self, dz, dy, dx):
        p, slot = self.pl, self.diag(dz, dy, dx)
        return self.remote("xa", slot, self.half(p.page(dz, dy, dx), 0), self.da.at[slot], (p.page(dx=dx), p.c))

    def yb_copy(self, dz, dy, dx):
        p, slot = self.pl, self.diag(dz, dy, dx)
        return self.remote("yb", slot, self.half(p.page(dz, dy, dx), 1), self.db.at[slot], (p.page(dy=dy), p.c))

    def x_copy(self, dz, dx):
        p = self.pl
        slot = dz * (p.nx - 1) + dx - 1
        return self.remote("x", slot, self.total.at[:, p.page(dz, 0, dx)], self.rx.at[slot], (p.page(dx=dx), p.c))

    def y_copy(self, dz, dy):
        p = self.pl
        slot = dz * (p.ny - 1) + dy - 1
        return self.remote("y", slot, self.total.at[:, p.page(dz, dy, 0)], self.ry.at[slot], (p.page(dy=dy), p.c))

    def z_copy(self, dz):
        p = self.pl
        return self.remote("z", dz - 1, self.total.at[:, p.page(dz, 0, 0)], self.rz.at[dz - 1], (p.page(dz=dz), p.c))

    def begin(self, dz):
        p = self.pl
        order = [(dy, dx) for dy in range(1, p.ny) for dx in range(1, p.nx)]
        order += [(0, dx) for dx in range(1, p.nx)] + [(dy, 0) for dy in range(1, p.ny)] + [(0, 0)]
        for dy, dx in order:
            self.core_copy(dz, dy, dx).start()

    def pair(self, dz, dy, dx):
        p = self.pl
        self.core_copy(dz, dy, dx).wait_recv()
        page = p.page(dz, dy, dx)
        return self.part[:, 2 * page + p.c].astype(F32) + self.total[:, page].astype(F32)

    def corner(self, dz):
        p = self.pl
        for dy in range(1, p.ny):
            for dx in range(1, p.nx):
                self.total[:, p.page(dz, dy, dx)] = self.pair(dz, dy, dx).astype(BF)
                self.xa_copy(dz, dy, dx).start()
                self.yb_copy(dz, dy, dx).start()

    def plane(self, dz):
        p = self.pl
        panels, rows = self.total.shape[0], self.total.shape[2]
        for dx in range(1, p.nx):
            total = self.pair(dz, 0, dx)
            page = p.page(dz, 0, dx)
            for dy in range(1, p.ny):
                self.yb_copy(dz, dy, dx).wait_recv()
                add = self.db[self.diag(dz, dy, dx)].astype(F32)
                if self.kind == PANELS:
                    n = panels // 2
                    total = jnp.concatenate([total[:n], total[n:] + add], axis=0)
                else:
                    n = rows // 2
                    total = jnp.concatenate([total[:, :n], total[:, n:] + add], axis=1)
            self.total[:, page] = total.astype(BF)
            self.x_copy(dz, dx).start()
        for dy in range(1, p.ny):
            total = self.pair(dz, dy, 0)
            page = p.page(dz, dy, 0)
            for dx in range(1, p.nx):
                self.xa_copy(dz, dy, dx).wait_recv()
                add = self.da[self.diag(dz, dy, dx)].astype(F32)
                if self.kind == PANELS:
                    n = panels // 2
                    total = jnp.concatenate([total[:n] + add, total[n:]], axis=0)
                else:
                    n = rows // 2
                    total = jnp.concatenate([total[:, :n] + add, total[:, n:]], axis=1)
            self.total[:, page] = total.astype(BF)
            self.y_copy(dz, dy).start()

    def column_sum(self, dz):
        p = self.pl
        total = self.pair(dz, 0, 0)
        for dx in range(1, p.nx):
            self.x_copy(dz, dx).wait_recv()
            total += self.rx[dz * (p.nx - 1) + dx - 1].astype(F32)
        for dy in range(1, p.ny):
            self.y_copy(dz, dy).wait_recv()
            total += self.ry[dz * (p.ny - 1) + dy - 1].astype(F32)
        return total

    def column(self, dz):
        self.total[:, self.pl.page(dz, 0, 0)] = self.column_sum(dz).astype(BF)
        self.z_copy(dz).start()

    def finish(self):
        total = self.column_sum(0)
        for dz in range(1, self.pl.nz):
            self.z_copy(dz).wait_recv()
            total += self.rz[dz - 1].astype(F32)
        return total

    def drain(self):
        p = self.pl

        def one(dz, _):
            for dy in range(p.ny):
                for dx in range(p.nx):
                    self.core_copy(dz, dy, dx).wait_send()
            for dy in range(1, p.ny):
                for dx in range(1, p.nx):
                    self.xa_copy(dz, dy, dx).wait_send()
                    self.yb_copy(dz, dy, dx).wait_send()
            for dx in range(1, p.nx):
                self.x_copy(dz, dx).wait_send()
            for dy in range(1, p.ny):
                self.y_copy(dz, dy).wait_send()
            return 0

        lax.fori_loop(0, p.nz, one, 0)
        for dz in range(1, p.nz):
            self.z_copy(dz).wait_send()


def vector_scratch(pages, rows, width):
    nz, ny, nx = page_grid(pages)
    n = 1 + nx - 1 + ny - 1 + nz - 1
    return [VMEM((4, rows, width), F32), VMEM((n, rows, width), F32), DMA((n,)), DMA((n,))]


class VectorSum:
    def __init__(self, place, scratch):
        self.pl = place
        self.held, self.got, self.send, self.recv = scratch

    def legs(self):
        p = self.pl
        return [
            [(p.p, 1 - p.c)],
            [(p.page(dx=d), p.c) for d in range(1, p.nx)],
            [(p.page(dy=d), p.c) for d in range(1, p.ny)],
            [(p.page(dz=d), p.c) for d in range(1, p.nz)],
        ]

    def copies(self, leg):
        legs = self.legs()
        at = sum(len(one) for one in legs[:leg])
        return [
            pltpu.make_async_remote_copy(
                src_ref=self.held.at[leg], dst_ref=self.got.at[at + i], send_sem=self.send.at[at + i],
                recv_sem=self.recv.at[at + i], device_id=target, device_id_type=MESH)
            for i, target in enumerate(legs[leg])
        ], at

    def put(self, leg, value):
        self.held[leg] = value
        for copy in self.copies(leg)[0]:
            copy.start()

    def take(self, leg):
        copies, at = self.copies(leg)
        value = self.held[leg]
        for i, copy in enumerate(copies):
            copy.wait_recv()
            value += self.got[at + i]
        return value

    def drain(self):
        for leg in range(4):
            for copy in self.copies(leg)[0]:
                copy.wait_send()


HEADS = 12


masked_value = -1e30
norm_eps = 1e-06


def layer_norm(values, norm_gain, norm_shift):
    centre = jnp.mean(values, axis=-1, keepdims=True)
    centered = values - centre
    spread = jnp.mean(centered * centered, axis=-1, keepdims=True)
    return centered * lax.rsqrt(spread + norm_eps) * norm_gain + norm_shift


def gelu_exact(values):
    return jax.nn.gelu(values, approximate=False)


def matmul(left_side, right_side):
    return jnp.dot(left_side, right_side, preferred_element_type=jnp.float32)


def column_sum(values):
    return jnp.sum(values.astype(jnp.float32), axis=0)


def usable_keys(page_lengths, seg_len):
    places = lax.broadcasted_iota(jnp.int32, (page_lengths.shape[0], seg_len), 1)
    return places < page_lengths[:, None]


def head_split(values, head_count):
    return values.reshape(
        values.shape[0], values.shape[1], head_count, values.shape[2] // head_count
    )


def page_scores(query_heads, key_piece, usable, score_scale):
    key_heads = head_split(key_piece, query_heads.shape[2])
    scores = (
        jnp.einsum("pqhd,pkhd->phqk", query_heads, key_heads, preferred_element_type=jnp.float32)
        * score_scale
    )
    return jnp.where(usable[:, None, None, :], scores, masked_value)


VECTORS = 8


def pack_vectors(vectors, inner):
    lanes = 128
    rows = [jnp.pad(v, (0, lanes - v.shape[0])) for v in (*vectors, inner)]
    rows += [jnp.zeros((lanes,), BF)] * (16 - len(rows))
    return jnp.stack(rows)


LOG2E = 1.4426950408889634
LANES = 128
VEC_ROWS = 16
NT = ((1,), (1,))
TN = ((0,), (0,))


def steps_loop(count, body, steps):
    def one(i, _):
        body(i)
        for at, todo in steps.items():
            def run(todo=todo):
                for step in todo:
                    step()
            pl.when(i == at)(run)
        return 0

    lax.fori_loop(0, count, one, 0)


def dot(left, right, dims=((1,), (0,))):
    return lax.dot_general(left, right, (dims, ((), ())), preferred_element_type=F32)


def standardize(values):
    centered = values - jnp.mean(values, axis=-1, keepdims=True)
    r = lax.rsqrt(jnp.mean(centered * centered, axis=-1, keepdims=True) + norm_eps)
    return centered * r, r


def norm_back(grad, xhat, r, gain):
    e = grad * gain
    return r * (e - jnp.mean(e, axis=-1, keepdims=True) - xhat * jnp.mean(e * xhat, axis=-1, keepdims=True))


def add_row(ref, row, values):
    ref[row:row + 1, :] += jnp.sum(values, axis=0, keepdims=True)


def spread_lanes(small, n, width, first):
    devices, vectors, lanes = small.shape
    column = (first + lax.broadcasted_iota(jnp.int32, (lanes, width), 1)).astype(F32)
    owner = jnp.floor((column + 0.5) * (1.0 / n))
    lane = lax.broadcasted_iota(jnp.int32, (lanes, width), 0).astype(F32)
    pick = jnp.where(column - owner * n == lane, 1.0, 0.0).astype(BF)
    values = dot(small.reshape(devices * vectors, lanes), pick).reshape(devices, vectors, width)
    device = lax.broadcasted_iota(jnp.int32, (devices, vectors, width), 0).astype(F32)
    return jnp.sum(jnp.where(owner[:1][None] == device, values, 0.0), axis=0)


def layer_scratch(pages, rows, width, panels, tokens, local_pages):
    devices = 2 * pages
    _, gs = gather_slots(pages)
    seg = tokens // local_pages
    own = dict(
        g_attn=VMEM((4, devices, rows, width), BF),
        g_inner=VMEM((panels, devices, rows, width), BF),
        g_outer=VMEM((1, devices, panels * rows, width), BF),
        g_small=VMEM((1, devices, VEC_ROWS, LANES), BF),
        p_one=VMEM((2, devices, rows, width), BF),
        p_two=VMEM((2, devices, rows, width), BF),
        xs=VMEM((tokens, width), BF),
        q=VMEM((tokens, width), BF),
        k=VMEM((local_pages, 2 * seg, width), BF),
        v=VMEM((local_pages, 2 * seg, width), BF),
        ctx=VMEM((tokens, width), BF),
        xhat=VMEM((tokens, width), F32),
        r_one=VMEM((tokens, 1), F32),
        low=VMEM((tokens, width), BF),
        post=VMEM((panels, tokens, width), BF),
        slope=VMEM((panels, tokens, width), BF),
        res=VMEM((tokens, width), F32),
        d_low=VMEM((tokens, width), BF),
        vec=VMEM((VEC_ROWS, width), F32),
        par=VMEM((VEC_ROWS, width), F32),
        rk=VMEM((local_pages, seg, width), BF),
        rv=VMEM((local_pages, seg, width), BF),
        x_sem=DMA((2,)),
        kv_sem=DMA((4, local_pages)),
    )
    gather = [DMA((gs,))] * 8
    reduce = []
    for count, size, kind in ((1, panels * rows, ROWS), (panels, rows, PANELS), (2, rows, PANELS), (2, rows, PANELS)):
        reduce += reduce_scratch(pages, count, size, width, kind)
    return own, gather + reduce + vector_scratch(pages, VEC_ROWS, width)


def layer_kernel(pages, heads, names, lengths, x, cot, wq, wk, wv, wo, wi, wout, small,
                 layer_out, hidden_grad, o_q, o_k, o_v, o_o, o_inner, o_outer, o_vec, *scratch):
    s = types.SimpleNamespace(**dict(zip(names, scratch)))
    s.d_ctx = s.xs
    rest = scratch[len(names):]
    place = Place(pages)
    c, nz = place.c, place.nz
    mine = 2 * place.p + c
    sibling = (place.p, 1 - c)
    tokens, width = x.shape
    panels, devices, rows = s.g_inner.shape[:3]
    local_pages, page_len = s.k.shape[:2]
    seg = tokens // local_pages
    full = (width, width)
    scale = (width // heads) ** -0.5
    q, k, v, ctx, res, par, vec = s.q, s.k, s.v, s.ctx, s.res, s.par, s.vec

    for j, ref in enumerate((wq, wk, wv, wo)):
        s.g_attn[j, mine] = ref[...]
    for j in range(panels):
        s.g_inner[j, mine] = wi[:, j * width:(j + 1) * width]
    s.g_outer[0, mine] = wout[...]
    s.g_small[0, mine] = small[...]
    place.greet()
    x_copy = pltpu.make_async_remote_copy(
        src_ref=x, dst_ref=s.xs, send_sem=s.x_sem.at[0], recv_sem=s.x_sem.at[1],
        device_id=sibling, device_id_type=MESH)
    x_copy.start()
    tiny, attn, inner, outer = (
        Gather(place, ref, rest[2 * i], rest[2 * i + 1], kind)
        for i, (ref, kind) in enumerate(((s.g_small, SMALL), (s.g_attn, PANELS), (s.g_inner, PANELS), (s.g_outer, ROWS))))
    first = (tiny, attn)
    for one in (tiny, attn, inner, outer):
        one.begin_z()
    for one in first:
        one.spread(0)
    for dz in range(1, nz):
        for one in first:
            one.column(dz)
    for dz in range(nz):
        for one in first:
            one.plane(dz)
    inner.spread(0)
    for dz in range(1, nz):
        inner.column(dz)
    for dz in range(nz):
        for one in first:
            one.corner(dz)
    for one in first:
        one.finish_core()
    x_copy.wait()

    def weight(ref, j):
        return ref[j].reshape(full)

    def outer_weight(j):
        n = devices // panels
        return s.g_outer[0, pl.ds(j * n, n)].reshape(full)

    gathered = s.g_small[0]
    par[...] = spread_lanes(gathered, rows, width, 0)
    for j in range(panels):
        par[VECTORS + j:VECTORS + j + 1, :] = spread_lanes(gathered, panels * rows, width, j * width)[VECTORS:VECTORS + 1]
    vec[...] = jnp.zeros_like(vec)

    def vector(j):
        return par[j:j + 1, :]

    q[...] = (dot(x[...], weight(s.g_attn, 0)) + vector(0)).astype(BF)
    inner.plane(0)

    def project(i, _):
        ref, half = (x, c) if i == 0 else (s.xs, 1 - c)
        rows_of = pl.ds(pl.multiple_of(half * seg, seg), seg)
        k[:, rows_of, :] = dot(ref[...], weight(s.g_attn, 1)).astype(BF).reshape(local_pages, seg, width)
        v[:, rows_of, :] = (dot(ref[...], weight(s.g_attn, 2)) + vector(1)).astype(BF).reshape(local_pages, seg, width)

    project(0, 0)
    inner.plane(1)
    project(1, 0)
    inner.plane(2)

    pairs = heads // 2
    head_dim = width // heads

    def place_of(i):
        page, pair = i // pairs, lax.rem(i, pairs)
        return page, pl.ds(pl.multiple_of(page * seg, seg), seg), pl.ds(pl.multiple_of(pair * LANES, LANES), LANES)

    low_half = lax.broadcasted_iota(jnp.int32, (1, LANES), 1) < head_dim
    key_at = lax.broadcasted_iota(jnp.int32, (1, page_len), 1)

    def one_head(values, head):
        return jnp.where(low_half if head == 0 else jnp.logical_not(low_half), values, jnp.zeros_like(values))

    def probabilities(q2, k2, head, usable):
        t = jnp.where(usable, dot(q2, one_head(k2, head), NT) * (scale * LOG2E), masked_value)
        e = jnp.exp2(t - jnp.max(t, axis=-1, keepdims=True))
        return e * (1.0 / jnp.sum(e, axis=-1, keepdims=True))

    def attend(i):
        page, rows_of, cols = place_of(i)
        q2, k2, v2 = q[rows_of, cols], k[page, :, cols], v[page, :, cols]
        usable = key_at < lengths[page]
        parts = [dot(probabilities(q2, k2, head, usable).astype(BF), v2) for head in range(2)]
        ctx[rows_of, cols] = jnp.where(low_half, *parts).astype(BF)

    steps_loop(local_pages * pairs, attend, {
        0: [lambda: inner.plane(3), lambda: outer.spread(0)],
        1: [lambda: outer.column(1)],
        2: [lambda: outer.column(2)],
        3: [lambda: outer.column(3)],
        4: [lambda: inner.corner(0)],
        5: [lambda: inner.corner(1)],
        6: [lambda: inner.corner(2)],
        7: [lambda: inner.corner(3)],
        8: [lambda: outer.plane(0)],
        9: [lambda: outer.plane(1)],
        10: [lambda: outer.plane(2)],
        11: [lambda: outer.plane(3)],
    })

    res[...] = dot(ctx[...], weight(s.g_attn, 3))
    chunk = 128

    def chunks(body):
        def one(i, _):
            body(pl.ds(pl.multiple_of(i * chunk, chunk), chunk))
            return 0
        lax.fori_loop(0, tokens // chunk, one, 0)

    def norm_one(at):
        xhat, r = standardize(x[at, :].astype(F32) + res[at, :] + vector(2))
        s.xhat[at, :] = xhat
        s.r_one[at, :] = r
        normed = xhat * vector(3) + vector(4)
        s.low[at, :] = normed.astype(BF)
        res[at, :] = normed + vector(5)

    chunks(norm_one)

    inner.finish_core()
    root_half = 0.7071067811865476

    def expand(j):
        pre = dot(s.low[...], weight(s.g_inner, j)) + par[pl.ds(VECTORS + j, 1), :]
        half_one = 0.5 * (1.0 + lax.erf(pre * root_half))
        bell = jnp.exp2(pre * pre * (-0.5 * LOG2E)) * 0.3989422804014327
        s.post[j] = (pre * half_one).astype(BF)
        s.slope[j] = (half_one + pre * bell).astype(BF)

    steps_loop(panels, expand, {j: [lambda j=j: outer.corner(j)] for j in range(nz)})
    outer.finish_core()

    def contract(j, _):
        res[...] += dot(s.post[j], outer_weight(j))
        return 0

    lax.fori_loop(0, panels, contract, 0)

    def norm_two(at):
        xhat, r = standardize(res[at, :])
        layer_out[at, :] = (xhat * vector(6) + vector(7)).astype(BF)
        grad = cot[at, :].astype(F32)
        add_row(vec, 6, grad * xhat)
        add_row(vec, 7, grad)
        d_res = norm_back(grad, xhat, r, vector(6))
        res[at, :] = d_res
        d_low = d_res.astype(BF)
        s.d_low[at, :] = d_low
        add_row(vec, 5, d_low.astype(F32))

    chunks(norm_two)

    reducers = [
        Reduce(place, part, rest[8 + 8 * i:16 + 8 * i], kind)
        for i, (part, kind) in enumerate(((s.g_outer, ROWS), (s.g_inner, PANELS), (s.p_one, PANELS), (s.p_two, PANELS)))]
    r_outer, r_inner, r_first, r_second = reducers
    outer.drain()

    def outer_back(dz):
        j = lax.rem(place.z + dz, nz)
        d_low = s.d_low[...]
        d_pre = (dot(d_low, outer_weight(j), NT) * s.slope[j].astype(F32)).astype(BF)
        n = devices // panels
        s.g_outer[0, pl.ds(j * n, n)] = dot(s.post[j], d_low, TN).reshape(n, panels * rows, width).astype(BF)
        r_outer.begin(dz)
        s.slope[j] = d_pre
        vec[pl.ds(VECTORS + j, 1), :] = jnp.sum(d_pre.astype(F32), axis=0, keepdims=True)

    steps_loop(nz, outer_back, {
        1: [lambda: r_outer.corner(0)],
        2: [lambda: r_outer.corner(1)],
        3: [lambda: r_outer.corner(2)],
    })
    inner.drain()

    def inner_back(j):
        d_pre = s.slope[j]
        res[...] += dot(d_pre, weight(s.g_inner, j), NT)
        s.g_inner[j] = dot(s.low[...], d_pre, TN).reshape(devices, rows, width).astype(BF)

    steps_loop(panels, inner_back, {
        0: [lambda: r_outer.corner(3), lambda: r_outer.plane(0)],
        1: [lambda: r_outer.plane(1)],
        2: [lambda: r_outer.plane(2)],
        3: [lambda: r_outer.plane(3)],
    })
    for dz in range(nz):
        r_inner.begin(dz)

    def norm_one_back(at):
        grad, xhat = res[at, :], s.xhat[at, :]
        add_row(vec, 3, grad * xhat)
        add_row(vec, 4, grad)
        d_res = norm_back(grad, xhat, s.r_one[at, :], vector(3))
        res[at, :] = d_res
        d_low = d_res.astype(BF)
        s.d_low[at, :] = d_low
        add_row(vec, 2, d_low.astype(F32))

    chunks(norm_one_back)
    s.d_ctx[...] = dot(s.d_low[...], weight(s.g_attn, 3), NT).astype(BF)
    s.p_one[0] = dot(ctx[...], s.d_low[...], TN).reshape(devices, rows, width).astype(BF)
    r_inner.corner(0)
    r_inner.corner(1)

    d_q, d_k, d_v = s.post.at[0], s.post.at[1:1 + local_pages], s.slope.at[0:local_pages]

    def kv_copies(page):
        theirs = pl.ds(pl.multiple_of((1 - c) * seg, seg), seg)
        return [
            pltpu.make_async_remote_copy(
                src_ref=grad.at[page, theirs], dst_ref=got.at[page], send_sem=s.kv_sem.at[2 * n, page],
                recv_sem=s.kv_sem.at[2 * n + 1, page], device_id=sibling, device_id_type=MESH)
            for n, (grad, got) in enumerate(((d_k, s.rk), (d_v, s.rv)))]

    def attend_back(i):
        page, rows_of, cols = place_of(i)
        q2, k2, v2 = q[rows_of, cols], k[page, :, cols], v[page, :, cols]
        c2 = s.d_ctx[rows_of, cols]
        usable = key_at < lengths[page]
        parts = []
        for head in range(2):
            p = probabilities(q2, k2, head, usable)
            d_p = dot(c2, one_head(v2, head), NT)
            d_s = (p * (d_p - jnp.sum(p * d_p, axis=-1, keepdims=True))).astype(BF)
            parts.append((dot(d_s, k2), dot(d_s, q2, TN), dot(p.astype(BF), c2, TN)))
        both = [jnp.where(low_half, one, two) for one, two in zip(*parts)]
        d_q[rows_of, cols] = (both[0] * scale).astype(BF)
        d_k[page, :, cols] = (both[1] * scale).astype(BF)
        d_v[page, :, cols] = both[2].astype(BF)

    def send_kv(page):
        for copy in kv_copies(page):
            copy.start()

    def finish_outer():
        o_outer[...] = r_outer.finish()[0]

    steps_loop(local_pages * pairs, attend_back, {
        0: [lambda: r_inner.corner(2)],
        1: [lambda: r_inner.corner(3)],
        2: [lambda: r_outer.column(1)],
        3: [lambda: r_outer.column(2)],
        4: [lambda: r_outer.column(3)],
        5: [lambda: r_inner.plane(0)],
        6: [lambda: r_inner.plane(1)],
        7: [lambda: r_inner.plane(2)],
        8: [lambda: r_inner.plane(3)],
        9: [finish_outer],
    })
    for page in range(local_pages):
        send_kv(page)
    s.p_one[1] = dot(x[...], d_q[...], TN).reshape(devices, rows, width).astype(BF)
    for dz in range(nz):
        r_first.begin(dz)
    add_row(vec, 0, d_q[...].astype(F32))
    for page in range(local_pages):
        for copy in kv_copies(page):
            copy.wait()
    ours = pl.ds(pl.multiple_of(c * seg, seg), seg)
    for j, (grad, got) in enumerate(((d_k, s.rk), (d_v, s.rv))):
        total = (grad[:, ours, :].astype(F32) + got[...].astype(F32)).astype(BF)
        got[...] = total
        total = total.reshape(tokens, width)
        if j == 1:
            add_row(vec, 1, total.astype(F32))
        s.p_two[j] = dot(x[...], total, TN).reshape(devices, rows, width).astype(BF)
    vectors = VectorSum(place, rest[40:44])
    vectors.put(0, vec[...])
    for dz in range(nz):
        r_second.begin(dz)

    def loop(start, body):
        def one(dz, _):
            body(dz)
            return 0
        lax.fori_loop(start, nz, one, 0)

    loop(0, r_first.corner)
    loop(1, r_inner.column)
    vectors.put(1, vectors.take(0))
    loop(0, r_second.corner)
    vectors.put(2, vectors.take(1))
    loop(0, r_first.plane)
    vectors.put(3, vectors.take(2))
    loop(0, r_second.plane)
    d_keys, d_values = s.rk[...].reshape(tokens, width), s.rv[...].reshape(tokens, width)
    res[...] += dot(d_q[...], weight(s.g_attn, 0), NT)
    res[...] += dot(d_keys, weight(s.g_attn, 1), NT)
    hidden_grad[...] = (res[...] + dot(d_values, weight(s.g_attn, 2), NT)).astype(BF)
    total = r_inner.finish()
    for j in range(panels):
        o_inner[:, j * width:(j + 1) * width] = total[j]
    loop(1, r_first.column)
    loop(1, r_second.column)
    o_vec[...] = vectors.take(3)
    total = r_first.finish()
    o_o[...] = total[0]
    o_q[...] = total[1]
    total = r_second.finish()
    o_k[...] = total[0]
    o_v[...] = total[1]
    tiny.drain()
    attn.drain()
    for one in reducers:
        one.drain()
    vectors.drain()


def whole_layer(pages, heads, lengths, x, cot, wq, wk, wv, wo, wi, wout, small, local_pages):
    tokens, width = x.shape
    rows, panels = wq.shape[0], wi.shape[1] // width
    own, scratch = layer_scratch(pages, rows, width, panels, tokens, local_pages)
    vm = pl.BlockSpec(memory_space=VMEM)
    row_shape = jax.ShapeDtypeStruct((tokens, width), BF)
    square = jax.ShapeDtypeStruct((rows, width), F32)
    return pl.pallas_call(
        functools.partial(layer_kernel, pages, heads, tuple(own)),
        name="whole_layer",
        out_shape=(row_shape, row_shape, square, square, square, square,
                   jax.ShapeDtypeStruct((rows, panels * width), F32),
                   jax.ShapeDtypeStruct((panels * rows, width), F32),
                   jax.ShapeDtypeStruct((VEC_ROWS, width), F32)),
        in_specs=[pl.BlockSpec(memory_space=pltpu.SMEM)] + [vm] * 9,
        out_specs=(vm,) * 9,
        scratch_shapes=[*own.values(), *scratch],
        compiler_params=pltpu.CompilerParams(collective_id=0, has_side_effects=True, vmem_limit_bytes=61 << 20),
    )(lengths, x, cot, wq, wk, wv, wo, wi, wout, small)


def plain_layer(
    hidden,
    lengths,
    w_query,
    w_key,
    w_value,
    w_output,
    b_query,
    b_value,
    b_output,
    attn_gain,
    attn_shift,
    w_inner,
    b_inner,
    w_outer,
    b_outer,
    ffn_gain,
    ffn_shift,
    cotangent,
):
    model_width = hidden.shape[2]
    head_count = HEADS
    score_scale = (model_width // head_count) ** (-0.5)
    f32 = jnp.float32
    bf16 = jnp.bfloat16
    work_hidden, work_cot = (hidden, cotangent)
    local_pages, local_tokens = (work_hidden.shape[0], work_hidden.shape[1])
    row_count = local_pages * local_tokens
    (
        query_full,
        key_full,
        value_full,
        output_full,
        query_bias,
        value_bias,
        output_bias,
        gain_one,
        shift_one,
    ) = (
        lax.all_gather(w_query, AXES, axis=0, tiled=True),
        lax.all_gather(w_key, AXES, axis=0, tiled=True),
        lax.all_gather(w_value, AXES, axis=0, tiled=True),
        lax.all_gather(w_output, AXES, axis=0, tiled=True),
        lax.all_gather(b_query, AXES, axis=0, tiled=True),
        lax.all_gather(b_value, AXES, axis=0, tiled=True),
        lax.all_gather(b_output, AXES, axis=0, tiled=True),
        lax.all_gather(attn_gain, AXES, axis=0, tiled=True),
        lax.all_gather(attn_shift, AXES, axis=0, tiled=True),
    )
    flat_rows = work_hidden.reshape(row_count, model_width)
    queries = (matmul(flat_rows, query_full) + query_bias.astype(f32)).astype(bf16)
    key_rows = matmul(flat_rows, key_full).astype(bf16)
    value_rows = (matmul(flat_rows, value_full) + value_bias.astype(f32)).astype(bf16)
    query_heads = head_split(queries.reshape(local_pages, local_tokens, model_width), head_count)
    key_pages = key_rows.reshape(local_pages, local_tokens, model_width)
    value_pages = value_rows.reshape(local_pages, local_tokens, model_width)
    stat_shape = (local_pages, head_count, local_tokens)
    stat_start = (jnp.full(stat_shape, masked_value, f32), jnp.zeros(stat_shape, f32))
    key_piece = lax.all_gather(key_pages, SEQ, axis=1, tiled=True)
    usable = usable_keys(lengths, key_piece.shape[1])

    def merged():
        run_peak, run_total = stat_start
        scores = page_scores(query_heads, key_piece, usable, score_scale)
        new_peak = jnp.maximum(run_peak, jnp.max(scores, axis=-1))
        summed = jnp.sum(jnp.exp(scores - new_peak[..., None]), axis=-1)
        return (new_peak, summed)

    run_peak, run_total = merged()
    log_norm = run_peak + jnp.log(run_total)
    add_key_piece = lax.all_gather(key_pages, SEQ, axis=1, tiled=True)
    value_piece = lax.all_gather(value_pages, SEQ, axis=1, tiled=True)
    add_usable = usable_keys(lengths, add_key_piece.shape[1])

    def merged():
        scores = page_scores(query_heads, add_key_piece, add_usable, score_scale)
        attn_probs = jnp.exp(scores - log_norm[..., None]).astype(bf16)
        addend = jnp.einsum(
            "phqk,pkhd->pqhd",
            attn_probs,
            head_split(value_piece, head_count),
            preferred_element_type=f32,
        )
        return addend.reshape(local_pages, local_tokens, model_width)

    context = merged()
    context_low = context.astype(bf16).reshape(row_count, model_width)
    residual_one = (
        flat_rows.astype(f32) + matmul(context_low, output_full) + output_bias.astype(f32)
    )
    normed_one, pull_one = jax.vjp(
        layer_norm, residual_one, gain_one.astype(f32), shift_one.astype(f32)
    )
    inner_full, outer_full, inner_bias, outer_bias, gain_two, shift_two = (
        lax.all_gather(w_inner, AXES, axis=0, tiled=True),
        lax.all_gather(w_outer, AXES, axis=0, tiled=True),
        lax.all_gather(b_inner, AXES, axis=0, tiled=True),
        lax.all_gather(b_outer, AXES, axis=0, tiled=True),
        lax.all_gather(ffn_gain, AXES, axis=0, tiled=True),
        lax.all_gather(ffn_shift, AXES, axis=0, tiled=True),
    )
    normed_low = normed_one.astype(bf16)
    pre_gelu = matmul(normed_low, inner_full) + inner_bias.astype(f32)
    post_gelu, pull_gelu = jax.vjp(gelu_exact, pre_gelu)
    post_low = post_gelu.astype(bf16)
    residual_two = normed_one + matmul(post_low, outer_full) + outer_bias.astype(f32)
    layer_out, pull_two = jax.vjp(
        layer_norm, residual_two, gain_two.astype(f32), shift_two.astype(f32)
    )
    cot_rows = work_cot.reshape(row_count, model_width).astype(f32)
    d_res_two, gain_two_grad, shift_two_grad = pull_two(cot_rows)
    d_outer = d_res_two.astype(bf16)
    outer_w_grad = matmul(post_low.T, d_outer)
    outer_b_grad = column_sum(d_outer)
    (d_pre_full,) = pull_gelu(matmul(d_outer, outer_full.T))
    d_pre = d_pre_full.astype(bf16)
    inner_w_grad = matmul(normed_low.T, d_pre)
    inner_b_grad = column_sum(d_pre)
    d_normed = d_res_two + matmul(d_pre, inner_full.T)
    d_res_one, gain_one_grad, shift_one_grad = pull_one(d_normed)
    ffn_owned = (
        lax.psum_scatter(inner_w_grad, AXES, scatter_dimension=0, tiled=True),
        lax.psum_scatter(outer_w_grad, AXES, scatter_dimension=0, tiled=True),
        lax.psum_scatter(inner_b_grad, AXES, scatter_dimension=0, tiled=True),
        lax.psum_scatter(outer_b_grad, AXES, scatter_dimension=0, tiled=True),
        lax.psum_scatter(gain_two_grad, AXES, scatter_dimension=0, tiled=True),
        lax.psum_scatter(shift_two_grad, AXES, scatter_dimension=0, tiled=True),
    )
    d_attn = d_res_one.astype(bf16)
    output_w_grad = matmul(context_low.T, d_attn)
    output_b_grad = column_sum(d_attn)
    d_context = matmul(d_attn, output_full.T).astype(bf16)
    d_context_heads = head_split(
        d_context.reshape(local_pages, local_tokens, model_width), head_count
    )
    context_heads = head_split(context, head_count)
    row_delta = jnp.transpose(
        jnp.sum(d_context_heads.astype(f32) * context_heads, axis=-1), (0, 2, 1)
    )

    def add_grads(segment):
        key_piece, value_piece = segment
        seg_len = key_piece.shape[1]
        usable = usable_keys(lengths, seg_len)

        def merged():
            scores = page_scores(query_heads, key_piece, usable, score_scale)
            attn_probs = jnp.exp(scores - log_norm[..., None])
            key_heads = head_split(key_piece, head_count)
            value_heads = head_split(value_piece, head_count)
            d_probs = jnp.einsum(
                "pqhd,pkhd->phqk", d_context_heads, value_heads, preferred_element_type=f32
            )
            d_scores = (attn_probs * (d_probs - row_delta[..., None])).astype(bf16)
            query_part = jnp.einsum(
                "phqk,pkhd->pqhd", d_scores, key_heads, preferred_element_type=f32
            )
            key_part = jnp.einsum(
                "phqk,pqhd->pkhd", d_scores, query_heads, preferred_element_type=f32
            )
            value_part = jnp.einsum(
                "phqk,pqhd->pkhd",
                attn_probs.astype(bf16),
                d_context_heads,
                preferred_element_type=f32,
            )
            query_grad = query_part.reshape(local_pages, local_tokens, model_width) * score_scale
            key_grads = key_part.reshape(local_pages, seg_len, model_width) * score_scale
            value_grads = value_part.reshape(local_pages, seg_len, model_width)
            return (query_grad, key_grads, value_grads)

        return merged()

    query_grad, key_grads, value_grads = add_grads(
        (
            lax.all_gather(key_pages, SEQ, axis=1, tiled=True),
            lax.all_gather(value_pages, SEQ, axis=1, tiled=True),
        )
    )
    key_owned, value_owned = (
        lax.psum_scatter(
            key_grads.astype(jnp.bfloat16), SEQ, scatter_dimension=1, tiled=True
        ).astype(jnp.float32),
        lax.psum_scatter(
            value_grads.astype(jnp.bfloat16), SEQ, scatter_dimension=1, tiled=True
        ).astype(jnp.float32),
    )
    d_queries = query_grad.astype(bf16).reshape(row_count, model_width)
    d_keys = key_owned.astype(bf16).reshape(row_count, model_width)
    d_values = value_owned.astype(bf16).reshape(row_count, model_width)
    query_w_grad = matmul(flat_rows.T, d_queries)
    key_w_grad = matmul(flat_rows.T, d_keys)
    value_w_grad = matmul(flat_rows.T, d_values)
    query_b_grad = column_sum(d_queries)
    value_b_grad = column_sum(d_values)
    hidden_grad = (
        d_res_one
        + matmul(d_queries, query_full.T)
        + matmul(d_keys, key_full.T)
        + matmul(d_values, value_full.T)
    ).astype(bf16)
    attn_owned = (
        lax.psum_scatter(query_w_grad, AXES, scatter_dimension=0, tiled=True),
        lax.psum_scatter(key_w_grad, AXES, scatter_dimension=0, tiled=True),
        lax.psum_scatter(value_w_grad, AXES, scatter_dimension=0, tiled=True),
        lax.psum_scatter(output_w_grad, AXES, scatter_dimension=0, tiled=True),
        lax.psum_scatter(query_b_grad, AXES, scatter_dimension=0, tiled=True),
        lax.psum_scatter(value_b_grad, AXES, scatter_dimension=0, tiled=True),
        lax.psum_scatter(output_b_grad, AXES, scatter_dimension=0, tiled=True),
        lax.psum_scatter(gain_one_grad, AXES, scatter_dimension=0, tiled=True),
        lax.psum_scatter(shift_one_grad, AXES, scatter_dimension=0, tiled=True),
    )
    out_pages = layer_out.astype(bf16).reshape(local_pages, local_tokens, model_width)
    grad_pages = hidden_grad.reshape(local_pages, local_tokens, model_width)
    return (
        out_pages,
        grad_pages,
        attn_owned[0],
        attn_owned[1],
        attn_owned[2],
        attn_owned[3],
        attn_owned[4],
        attn_owned[5],
        attn_owned[6],
        attn_owned[7],
        attn_owned[8],
        ffn_owned[0],
        ffn_owned[2],
        ffn_owned[1],
        ffn_owned[3],
        ffn_owned[4],
        ffn_owned[5],
    )


def per_device(pages, hidden, lengths, w_query, w_key, w_value, w_output, b_query, b_value, b_output, attn_gain, attn_shift,
               w_inner, b_inner, w_outer, b_outer, ffn_gain, ffn_shift, cotangent):
    local_pages, seg, width = hidden.shape
    rows, panels = w_query.shape[0], w_inner.shape[1] // width
    nz, _, _ = page_grid(pages)
    if rows % 8 or nz != panels or local_pages * seg != 2 * seg or 4 * rows > 128:
        return plain_layer(hidden, lengths, w_query, w_key, w_value, w_output, b_query, b_value, b_output, attn_gain, attn_shift,
                           w_inner, b_inner, w_outer, b_outer, ffn_gain, ffn_shift, cotangent)
    small = pack_vectors((b_query, b_value, b_output, attn_gain, attn_shift, b_outer, ffn_gain, ffn_shift), b_inner)
    flat = local_pages * seg, width
    out, grad, g_q, g_k, g_v, g_o, g_inner, g_outer, total = whole_layer(
        pages, HEADS, lengths, hidden.reshape(flat), cotangent.reshape(flat), w_query, w_key, w_value, w_output, w_inner, w_outer,
        small, local_pages)
    at = lax.axis_index(PAGE) * 2 + lax.axis_index(SEQ)
    own = [lax.dynamic_slice(total, (j, rows * at), (1, rows))[0] for j in range(VECTORS)]
    wide = lax.dynamic_slice(total[VECTORS:VECTORS + panels].reshape(-1), (panels * rows * at,), (panels * rows,))
    return (out.reshape(hidden.shape), grad.reshape(hidden.shape), g_q, g_k, g_v, g_o, own[0], own[1], own[2], own[3], own[4],
            g_inner, wide, g_outer, own[5], own[6], own[7])


def solution(mesh):
    in_specs = (
        P(PAGE, SEQ, None),
        P(PAGE),
        P(AXES, None),
        P(AXES, None),
        P(AXES, None),
        P(AXES, None),
        P(AXES),
        P(AXES),
        P(AXES),
        P(AXES),
        P(AXES),
        P(AXES, None),
        P(AXES),
        P(AXES, None),
        P(AXES),
        P(AXES),
        P(AXES),
        P(PAGE, SEQ, None),
    )
    out_specs = (
        P(PAGE, SEQ, None),
        P(PAGE, SEQ, None),
        P(AXES, None),
        P(AXES, None),
        P(AXES, None),
        P(AXES, None),
        P(AXES),
        P(AXES),
        P(AXES),
        P(AXES),
        P(AXES),
        P(AXES, None),
        P(AXES),
        P(AXES, None),
        P(AXES),
        P(AXES),
        P(AXES),
    )
    return jax.shard_map(
        functools.partial(per_device, mesh.shape[PAGE]), mesh=mesh, in_specs=in_specs, out_specs=out_specs, check_vma=False
    )
```

```python
import functools
import types
import jax
import jax.numpy as jnp
from jax import lax
from jax.experimental import pallas as pl
from jax.experimental.pallas import tpu as pltpu

from jax.sharding import PartitionSpec as P

MESH = pl.DeviceIdType.MESH
VMEM = pltpu.VMEM
DMA = pltpu.SemaphoreType.DMA
BF = jnp.bfloat16
F32 = jnp.float32
LANES = 128
AXES = PAGE, SEQ = ("page", "seq")
SMALL, PANELS, ROWS = range(3)
SPREAD_RELAY = 128
RELAY = 0


def page_grid(pages):
    bits = pages.bit_length() - 1
    nx = 2 ** (bits // 3)
    ny = 2 ** ((bits - bits // 3) // 2)
    return pages // (nx * ny), ny, nx


class Place:
    def __init__(self, pages):
        self.nz, self.ny, self.nx = page_grid(pages)
        self.plane = self.ny * self.nx
        self.p = lax.axis_index(PAGE)
        self.c = lax.axis_index(SEQ)
        self.x = lax.rem(self.p, self.nx)
        self.y = lax.rem(self.p // self.nx, self.ny)
        self.z = self.p // self.plane
        self.sibling = (self.p, 1 - self.c)
        self.others = [(dy, dx) for dy in range(self.ny) for dx in range(self.nx) if dy or dx]

    def page(self, dz=0, dy=0, dx=0):
        z = lax.rem(self.z + dz + self.nz, self.nz)
        y = lax.rem(self.y + dy + self.ny, self.ny)
        x = lax.rem(self.x + dx + self.nx, self.nx)
        return (z * self.ny + y) * self.nx + x

    def level(self, dz):
        return lax.rem(self.z + dz + self.nz, self.nz) * self.plane

    def there(self, dz=0, dy=0, dx=0):
        return self.page(dz, dy, dx), self.c

    def signal(self):
        barrier = pltpu.get_barrier_semaphore()
        partners = [self.there(dz=d) for d in range(1, self.nz)] + [self.there(0, *d) for d in self.others] + [self.sibling]
        for partner in partners:
            pl.semaphore_signal(barrier, inc=1, device_id=partner, device_id_type=MESH)
        return lambda: pl.semaphore_wait(barrier, len(partners))


def slots(sizes):
    base, at = [], 0
    for size in sizes:
        base.append(at)
        at += size
    return base, at


def gather_slots(pages):
    nz, ny, nx = page_grid(pages)
    return slots((1, 1, 1, nz, nz)), slots((nz - 1, nz * (nx - 1), nz * (ny - 1), nz * (nx - 1) * (ny - 1), 1, nz, 1))


class Gather:
    def __init__(self, place, ref, send, recv, kind):
        self.pl, self.ref, self.send, self.recv, self.kind = place, ref, send, recv, kind
        (self.sbase, _), (self.rbase, _) = gather_slots(place.nz * place.plane)
        self.low = 0 if kind == SMALL else SPREAD_RELAY

    def view(self, page, part, core=None, count=None):
        ref, low = self.ref, self.low
        core = self.pl.c if core is None else core
        pages = page if count is None else pl.ds(page, count)
        if part == 3:
            return ref.at[:, pages, core, :, 0:low]
        if part == 4:
            return ref.at[:, pages, core]
        if part == 0 or self.kind == SMALL:
            return ref.at[:, pages, core, :, low:]
        if self.kind == PANELS:
            n = ref.shape[0] // 2
            return ref.at[(part - 1) * n:part * n, pages, core, :, low:]
        n = ref.shape[3] // 2
        return ref.at[:, pages, core, (part - 1) * n:part * n, low:]

    def copy(self, view, send, recv, target):
        return pltpu.make_async_remote_copy(
            src_ref=view, dst_ref=view, send_sem=self.send.at[send], recv_sem=self.recv.at[recv],
            device_id=target, device_id_type=MESH)

    def plain(self, group, slot, page, part, target):
        return self.copy(self.view(page, part), self.sbase[0], self.rbase[group] + slot, target)

    def corner_slot(self, dx, dy, dz):
        return (dz * (self.pl.ny - 1) + dy - 1) * (self.pl.nx - 1) + dx - 1

    def z_copy(self, dz, mine):
        p = self.pl
        return self.plain(0, dz - 1, p.page(0 if mine else -dz), 0, p.there(dz=dz))

    def x_copy(self, dx, dz, mine):
        p = self.pl
        return self.plain(1, dz * (p.nx - 1) + dx - 1, p.page(-dz, 0, 0 if mine else -dx), 0, p.there(dx=dx))

    def y_copy(self, dy, dz, mine):
        p = self.pl
        return self.plain(2, dz * (p.ny - 1) + dy - 1, p.page(-dz, 0 if mine else -dy, 0), 0, p.there(dy=dy))

    def xa_copy(self, dx, dy, dz):
        p = self.pl
        return self.plain(3, self.corner_slot(dx, dy, dz), p.page(-dz, -dy, 0), 1, p.there(dx=dx))

    def yb_copy(self, dx, dy, dz):
        p = self.pl
        return self.plain(3, self.corner_slot(dx, dy, dz), p.page(-dz, 0, -dx), 2, p.there(dy=dy))

    def core_copy(self, page, part, count=None):
        return self.copy(self.view(page, part, None, count), self.sbase[1], self.rbase[6], self.pl.sibling)

    def relay_copy(self, level, up):
        p = self.pl
        group = level // p.plane
        target = p.there(dz=1 if up else p.nz - 1)
        return self.copy(self.view(level, 3, None, p.plane), self.sbase[3 if up else 4] + group, self.rbase[5] + group, target)

    def wait(self, view, sem):
        pltpu.make_async_copy(view, view, sem).wait()

    def begin(self):
        p = self.pl
        if self.low:
            for dy, dx in p.others:
                self.copy(self.view(p.page(), 3), self.sbase[2], self.rbase[4], p.there(0, dy, dx)).start()
        for d in range(1, p.nz):
            self.z_copy(d, True).start()

    def spread(self, dz):
        p = self.pl
        for d in range(1, p.nx):
            self.x_copy(d, dz, True).start()
        for d in range(1, p.ny):
            self.y_copy(d, dz, True).start()
        self.core_copy(p.page(-dz), 0).start()

    def column(self, dz):
        self.z_copy(dz, False).wait_recv()
        self.spread(dz)

    def rise(self):
        p = self.pl
        if not self.low:
            return
        level = p.level(0)
        self.wait(self.view(level, 3, None, p.plane - 1), self.recv.at[self.rbase[4]])
        pl.when(p.z < p.nz - 1)(lambda: self.relay_copy(level, True).start())
        pl.when(p.z > 0)(lambda: self.relay_copy(level, False).start())
        self.core_copy(level, 3, p.plane).start()

    def relay(self, d):
        p = self.pl
        if not self.low:
            return

        def step(up):
            level = (p.z - d if up else p.z + d) * p.plane
            self.relay_copy(level, up).wait_recv()
            pl.when(p.z < p.nz - 1 if up else p.z > 0)(lambda: self.relay_copy(level, up).start())
            self.core_copy(level, 3, p.plane).start()

        pl.when(p.z >= d)(lambda: step(True))
        pl.when(p.z + d < p.nz)(lambda: step(False))

    def plane(self, dz):
        p = self.pl
        for dy in range(1, p.ny):
            self.y_copy(dy, dz, False).wait_recv()
            for dx in range(1, p.nx):
                self.xa_copy(dx, dy, dz).start()
            self.core_copy(p.page(-dz, -dy), 0).start()
        for dx in range(1, p.nx):
            self.x_copy(dx, dz, False).wait_recv()
            if self.kind != SMALL:
                for dy in range(1, p.ny):
                    self.yb_copy(dx, dy, dz).start()
            self.core_copy(p.page(-dz, 0, -dx), 0).start()

    def corner(self, dz):
        p = self.pl
        for dy in range(1, p.ny):
            for dx in range(1, p.nx):
                page = p.page(-dz, -dy, -dx)
                self.wait(self.view(page, 0), self.recv.at[self.rbase[3] + self.corner_slot(dx, dy, dz)])
                self.core_copy(page, 0).start()

    def finish_core(self):
        self.wait(self.view(0, 4, 1 - self.pl.c, self.pl.nz * self.pl.plane), self.recv.at[self.rbase[6]])

    def drain(self):
        p = self.pl
        pages = p.nz * p.plane
        self.wait(self.view(0, 4, None, pages), self.send.at[self.sbase[1]])
        corners = p.nz * (p.ny - 1) * (p.nx - 1)
        blocks = p.nz - 1 + p.nz * (p.nx - 1) + p.nz * (p.ny - 1) + corners
        if self.low:
            self.wait(self.view(0, 3, None, p.plane - 1), self.send.at[self.sbase[2]])
        self.wait(self.view(0, 0, None, blocks), self.send.at[self.sbase[0]])
        if self.low:
            def group(g):
                pl.when(jnp.logical_and(p.z < p.nz - 1, g <= p.z))(lambda: self.relay_copy(g * p.plane, True).wait_send())
                pl.when(jnp.logical_and(p.z > 0, g >= p.z))(lambda: self.relay_copy(g * p.plane, False).wait_send())
            for g in range(p.nz):
                group(g)


def reduce_slots(pages):
    nz, ny, nx = page_grid(pages)
    corners = nz * (nx - 1) * (ny - 1)
    return slots((1, 1, 1, nz, nz)), slots((nz, corners, corners, nz * (nx - 1), nz * (ny - 1), nz - 1, 1, nz, nz))


def reduce_scratch(pages, panels, rows, width, kind):
    nz, ny, nx = page_grid(pages)
    fx, fy = nx - 1, ny - 1
    half = (panels // 2, rows) if kind == PANELS else (panels, rows // 2)
    rest = width - RELAY
    (_, sends), (_, recvs) = reduce_slots(pages)
    return [
        VMEM((panels, nz * ny * nx, rows, width), BF),
        VMEM((nz * fx * fy,) + half + (rest,), BF),
        VMEM((nz * fx * fy,) + half + (rest,), BF),
        VMEM((nz * fx, panels, rows, rest), BF),
        VMEM((nz * fy, panels, rows, rest), BF),
        VMEM((nz - 1, panels, rows, rest), BF),
        VMEM((ny * nx - 1, panels, rows, RELAY) if RELAY else (8, LANES), BF),
        VMEM((2, nz, panels, ny * nx, rows, RELAY) if RELAY else (8, LANES), BF),
        DMA((sends,)),
        DMA((recvs,)),
    ]


REDUCE_REFS = 10


class Reduce:
    def __init__(self, place, part, scratch, kind):
        self.pl, self.part, self.kind = place, part, kind
        self.total, self.da, self.db, self.rx, self.ry, self.rz, self.rp, self.rr, self.send, self.recv = scratch
        (self.sbase, _), (self.rbase, _) = reduce_slots(place.nz * place.plane)

    def remote(self, send, recv, src, dst, target):
        return pltpu.make_async_remote_copy(
            src_ref=src, dst_ref=dst, send_sem=self.send.at[send], recv_sem=self.recv.at[recv],
            device_id=target, device_id_type=MESH)

    def plain(self, group, slot, src, dst, target):
        return self.remote(self.sbase[0], self.rbase[group] + slot, src, dst, target)

    def wait(self, view, sem):
        pltpu.make_async_copy(view, view, sem).wait()

    def half(self, page, which):
        if self.kind == PANELS:
            n = self.total.shape[0] // 2
            return self.total.at[which * n:(which + 1) * n, page, :, RELAY:]
        n = self.total.shape[2] // 2
        return self.total.at[:, page, which * n:(which + 1) * n, RELAY:]

    def corner_slot(self, dz, dy, dx):
        return (dz * (self.pl.ny - 1) + dy - 1) * (self.pl.nx - 1) + dx - 1

    def core_copy(self, dz):
        p = self.pl
        pages = pl.ds(p.level(dz), p.plane)
        return self.remote(
            self.sbase[1], self.rbase[0] + dz, self.part.at[:, pages, 1 - p.c], self.total.at[:, pages], p.sibling)

    def xa_copy(self, dz, dy, dx):
        p, slot = self.pl, self.corner_slot(dz, dy, dx)
        return self.plain(1, slot, self.half(p.page(dz, dy, dx), 0), self.da.at[slot], p.there(dx=dx))

    def yb_copy(self, dz, dy, dx):
        p, slot = self.pl, self.corner_slot(dz, dy, dx)
        return self.plain(2, slot, self.half(p.page(dz, dy, dx), 1), self.db.at[slot], p.there(dy=dy))

    def x_copy(self, dz, dx):
        p = self.pl
        slot = dz * (p.nx - 1) + dx - 1
        return self.plain(3, slot, self.total.at[:, p.page(dz, 0, dx), :, RELAY:], self.rx.at[slot], p.there(dx=dx))

    def y_copy(self, dz, dy):
        p = self.pl
        slot = dz * (p.ny - 1) + dy - 1
        return self.plain(4, slot, self.total.at[:, p.page(dz, dy, 0), :, RELAY:], self.ry.at[slot], p.there(dy=dy))

    def z_copy(self, dz):
        p = self.pl
        return self.plain(5, dz - 1, self.total.at[:, p.page(dz), :, RELAY:], self.rz.at[dz - 1], p.there(dz=dz))

    def relay_copy(self, level, up):
        p = self.pl
        group, way = level // p.plane, 0 if up else 1
        return self.remote(
            self.sbase[3 + way] + group, self.rbase[7 + way] + group,
            self.total.at[:, pl.ds(level, p.plane), :, 0:RELAY], self.rr.at[way, group], p.there(dz=1 if up else p.nz - 1))

    def plane_copy(self, k, dy, dx):
        p = self.pl
        return self.remote(
            self.sbase[2], self.rbase[6], self.total.at[:, p.page(0, dy, dx), :, 0:RELAY], self.rp.at[k], p.there(0, dy, dx))

    def begin(self, dz):
        self.core_copy(dz).start()

    def arrive(self, dz):
        self.core_copy(dz).wait_recv()

    def pair(self, page):
        return self.part[:, page, self.pl.c, :, RELAY:].astype(F32) + self.total[:, page, :, RELAY:].astype(F32)

    def corner(self, dz):
        p = self.pl
        for dy in range(1, p.ny):
            for dx in range(1, p.nx):
                page = p.page(dz, dy, dx)
                self.total[:, page, :, RELAY:] = self.pair(page).astype(BF)
                self.xa_copy(dz, dy, dx).start()
                self.yb_copy(dz, dy, dx).start()

    def level_sum(self, level):
        p = self.pl
        pages, group = pl.ds(level, p.plane), level // p.plane
        total = self.part[:, pages, p.c, :, 0:RELAY].astype(F32) + self.total[:, pages, :, 0:RELAY].astype(F32)
        return total, pages, group

    def relay(self, d):
        p = self.pl
        if not RELAY:
            return

        def step(up):
            total, pages, group = self.level_sum((p.z + d if up else p.z - d) * p.plane)
            self.total[:, pages, :, 0:RELAY] = total.astype(BF)

            def add():
                self.relay_copy(group * p.plane, up).wait_recv()
                got = self.rr[0 if up else 1, group].astype(F32)
                self.total[:, pages, :, 0:RELAY] = (total + got).astype(BF)

            pl.when(p.z > 0 if up else p.z < p.nz - 1)(add)
            self.relay_copy(group * p.plane, up).start()

        pl.when(p.z + d < p.nz)(lambda: step(True))
        pl.when(p.z >= d)(lambda: step(False))

    def settle(self):
        p = self.pl
        if not RELAY:
            return
        total, pages, group = self.level_sum(p.level(0))
        self.total[:, pages, :, 0:RELAY] = total.astype(BF)
        for way in range(2):
            def add(way=way):
                self.relay_copy(group * p.plane, way == 0).wait_recv()
                self.total[:, pages, :, 0:RELAY] = (
                    self.total[:, pages, :, 0:RELAY].astype(F32) + self.rr[way, group].astype(F32)).astype(BF)
            pl.when(p.z > 0 if way == 0 else p.z < p.nz - 1)(add)
        for k, (dy, dx) in enumerate(p.others):
            self.plane_copy(k, dy, dx).start()

    def owned(self):
        p = self.pl
        self.wait(self.rp, self.recv.at[self.rbase[6]])
        total = self.total[:, p.page(), :, 0:RELAY].astype(F32)
        for k in range(len(p.others)):
            total += self.rp[k].astype(F32)
        return total

    def plane(self, dz):
        p = self.pl
        panels, rows = self.total.shape[0], self.total.shape[2]

        def with_half(total, add, which):
            axis, n = (0, panels // 2) if self.kind == PANELS else (1, rows // 2)
            first, second = (total[:n], total[n:]) if axis == 0 else (total[:, :n], total[:, n:])
            return jnp.concatenate([first + add, second] if which == 0 else [first, second + add], axis=axis)

        for dx in range(1, p.nx):
            page = p.page(dz, 0, dx)
            total = self.pair(page)
            for dy in range(1, p.ny):
                self.yb_copy(dz, dy, dx).wait_recv()
                total = with_half(total, self.db[self.corner_slot(dz, dy, dx)].astype(F32), 1)
            self.total[:, page, :, RELAY:] = total.astype(BF)
            self.x_copy(dz, dx).start()
        for dy in range(1, p.ny):
            page = p.page(dz, dy, 0)
            total = self.pair(page)
            for dx in range(1, p.nx):
                self.xa_copy(dz, dy, dx).wait_recv()
                total = with_half(total, self.da[self.corner_slot(dz, dy, dx)].astype(F32), 0)
            self.total[:, page, :, RELAY:] = total.astype(BF)
            self.y_copy(dz, dy).start()

    def column_sum(self, dz):
        p = self.pl
        total = self.pair(p.page(dz))
        for dx in range(1, p.nx):
            self.x_copy(dz, dx).wait_recv()
            total += self.rx[dz * (p.nx - 1) + dx - 1].astype(F32)
        for dy in range(1, p.ny):
            self.y_copy(dz, dy).wait_recv()
            total += self.ry[dz * (p.ny - 1) + dy - 1].astype(F32)
        return total

    def column(self, dz):
        self.total[:, self.pl.page(dz), :, RELAY:] = self.column_sum(dz).astype(BF)
        self.z_copy(dz).start()

    def finish(self):
        total = self.column_sum(0)
        for dz in range(1, self.pl.nz):
            self.z_copy(dz).wait_recv()
            total += self.rz[dz - 1].astype(F32)
        return jnp.concatenate([self.owned(), total], axis=2) if RELAY else total

    def drain(self):
        p = self.pl
        pages = p.nz * p.plane
        self.wait(self.part.at[:, :, 0], self.send.at[self.sbase[1]])
        self.wait(self.total.at[:, 0:pages - 1, :, RELAY:], self.send.at[self.sbase[0]])
        if not RELAY:
            return
        self.wait(self.rp, self.send.at[self.sbase[2]])

        def group(g):
            pl.when(g > p.z)(lambda: self.relay_copy(g * p.plane, True).wait_send())
            pl.when(g < p.z)(lambda: self.relay_copy(g * p.plane, False).wait_send())

        for g in range(p.nz):
            group(g)


def vector_scratch(pages, rows, width):
    nz, ny, nx = page_grid(pages)
    n = 1 + nx - 1 + ny - 1 + nz - 1
    return [VMEM((4, rows, width), F32), VMEM((n, rows, width), F32), DMA((n,)), DMA((n,))]


class VectorSum:
    def __init__(self, place, scratch):
        self.pl = place
        self.held, self.got, self.send, self.recv = scratch

    def legs(self):
        p = self.pl
        return [
            [p.sibling],
            [p.there(dx=d) for d in range(1, p.nx)],
            [p.there(dy=d) for d in range(1, p.ny)],
            [p.there(dz=d) for d in range(1, p.nz)],
        ]

    def copies(self, leg):
        legs = self.legs()
        at = sum(len(one) for one in legs[:leg])
        return [
            pltpu.make_async_remote_copy(
                src_ref=self.held.at[leg], dst_ref=self.got.at[at + i], send_sem=self.send.at[at + i],
                recv_sem=self.recv.at[at + i], device_id=target, device_id_type=MESH)
            for i, target in enumerate(legs[leg])
        ], at

    def put(self, leg, value):
        self.held[leg] = value
        for copy in self.copies(leg)[0]:
            copy.start()

    def take(self, leg):
        copies, at = self.copies(leg)
        value = self.held[leg]
        for i, copy in enumerate(copies):
            copy.wait_recv()
            value += self.got[at + i]
        return value

    def drain(self):
        for leg in range(4):
            for copy in self.copies(leg)[0]:
                copy.wait_send()


HEADS = 12


masked_value = -1e30
norm_eps = 1e-06


def layer_norm(values, norm_gain, norm_shift):
    centre = jnp.mean(values, axis=-1, keepdims=True)
    centered = values - centre
    spread = jnp.mean(centered * centered, axis=-1, keepdims=True)
    return centered * lax.rsqrt(spread + norm_eps) * norm_gain + norm_shift


def gelu_exact(values):
    return jax.nn.gelu(values, approximate=False)


def matmul(left_side, right_side):
    return jnp.dot(left_side, right_side, preferred_element_type=jnp.float32)


def column_sum(values):
    return jnp.sum(values.astype(jnp.float32), axis=0)


def usable_keys(page_lengths, seg_len):
    places = lax.broadcasted_iota(jnp.int32, (page_lengths.shape[0], seg_len), 1)
    return places < page_lengths[:, None]


def head_split(values, head_count):
    return values.reshape(
        values.shape[0], values.shape[1], head_count, values.shape[2] // head_count
    )


def page_scores(query_heads, key_piece, usable, score_scale):
    key_heads = head_split(key_piece, query_heads.shape[2])
    scores = (
        jnp.einsum("pqhd,pkhd->phqk", query_heads, key_heads, preferred_element_type=jnp.float32)
        * score_scale
    )
    return jnp.where(usable[:, None, None, :], scores, masked_value)


VECTORS = 8


def pack_vectors(vectors, inner):
    rows = [jnp.pad(v[None], ((j, 15 - j), (0, 128 - v.shape[0]))) for j, v in enumerate((*vectors, inner))]
    return functools.reduce(jnp.add, rows)


LOG2E = 1.4426950408889634
VEC_ROWS = 16
NT = ((1,), (1,))
TN = ((0,), (0,))


def steps_loop(count, body, steps):
    def one(i, _):
        body(i)
        for at, todo in steps.items():
            def run(todo=todo):
                for step in todo:
                    step()
            pl.when(i == at)(run)
        return 0

    lax.fori_loop(0, count, one, 0)


def dot(left, right, dims=((1,), (0,))):
    return lax.dot_general(left, right, (dims, ((), ())), preferred_element_type=F32)


def standardize(values):
    centered = values - jnp.mean(values, axis=-1, keepdims=True)
    r = lax.rsqrt(jnp.mean(centered * centered, axis=-1, keepdims=True) + norm_eps)
    return centered * r, r


def norm_back(grad, xhat, r, gain):
    e = grad * gain
    return r * (e - jnp.mean(e, axis=-1, keepdims=True) - xhat * jnp.mean(e * xhat, axis=-1, keepdims=True))


def add_row(ref, row, values):
    ref[row:row + 1, :] += jnp.sum(values, axis=0, keepdims=True)


def spread_lanes(small, n, width, first):
    devices, vectors, lanes = small.shape
    column = (first + lax.broadcasted_iota(jnp.int32, (lanes, width), 1)).astype(F32)
    owner = jnp.floor((column + 0.5) * (1.0 / n))
    lane = lax.broadcasted_iota(jnp.int32, (lanes, width), 0).astype(F32)
    pick = jnp.where(column - owner * n == lane, 1.0, 0.0).astype(BF)
    values = dot(small.reshape(devices * vectors, lanes), pick).reshape(devices, vectors, width)
    device = lax.broadcasted_iota(jnp.int32, (devices, vectors, width), 0).astype(F32)
    return jnp.sum(jnp.where(owner[:1][None] == device, values, 0.0), axis=0)


def layer_scratch(pages, rows, width, panels, tokens, local_pages):
    (_, gather_sends), (_, gather_recvs) = gather_slots(pages)
    seg = tokens // local_pages
    own = dict(
        g_attn=VMEM((4, pages, 2, rows, width), BF),
        g_inner=VMEM((panels, pages, 2, rows, width), BF),
        g_outer=VMEM((1, pages, 2, panels * rows, width), BF),
        g_small=VMEM((1, pages, 2, VEC_ROWS, LANES), BF),
        p_one=VMEM((2, pages, 2, rows, width), BF),
        p_two=VMEM((2, pages, 2, rows, width), BF),
        xs=VMEM((tokens, width), BF),
        q=VMEM((tokens, width), BF),
        k=VMEM((local_pages, 2 * seg, width), BF),
        v=VMEM((local_pages, 2 * seg, width), BF),
        ctx=VMEM((tokens, width), BF),
        xhat=VMEM((tokens, width), F32),
        r_one=VMEM((tokens, 1), F32),
        low=VMEM((tokens, width), BF),
        post=VMEM((panels, tokens, width), BF),
        slope=VMEM((panels, tokens, width), BF),
        res=VMEM((tokens, width), F32),
        d_low=VMEM((tokens, width), BF),
        vec=VMEM((VEC_ROWS, width), F32),
        par=VMEM((VEC_ROWS, width), F32),
        rk=VMEM((local_pages, seg, width), BF),
        rv=VMEM((local_pages, seg, width), BF),
        x=VMEM((tokens, width), BF),
        cot=VMEM((tokens, width), BF),
        out=VMEM((tokens, width), BF),
        squares=VMEM((4, rows, width), F32),
        wide=VMEM((rows, panels * width), F32),
        tall=VMEM((panels * rows, width), F32),
        total=VMEM((VEC_ROWS, width), F32),
        in_sem=DMA((8 + panels,)),
        out_sem=DMA((9,)),
        x_sem=DMA((2,)),
        kv_sem=DMA((4, local_pages)),
    )
    gather = [DMA((gather_sends,)), DMA((gather_recvs,))] * 4
    reduce = []
    for count, size, kind in ((1, panels * rows, ROWS), (panels, rows, PANELS), (2, rows, PANELS), (2, rows, PANELS)):
        reduce += reduce_scratch(pages, count, size, width, kind)
    return own, gather + reduce + vector_scratch(pages, VEC_ROWS, width)


def layer_kernel(pages, heads, names, lengths, x_in, cot_in, wq, wk, wv, wo, wi, wout, small,
                 layer_out, hidden_grad, o_q, o_k, o_v, o_o, o_inner, o_outer, o_vec, *scratch):
    s = types.SimpleNamespace(**dict(zip(names, scratch)))
    s.d_ctx, s.grad = s.xs, s.cot
    rest = scratch[len(names):]
    place = Place(pages)
    c, nz = place.c, place.nz
    mine = place.p, c
    sibling = place.sibling
    x, cot = s.x, s.cot
    tokens, width = x.shape
    panels, _, _, rows = s.g_inner.shape[:4]
    blocks = (pages, 2, rows, width)
    local_pages, page_len = s.k.shape[:2]
    seg = tokens // local_pages
    full = (width, width)
    scale = (width // heads) ** -0.5
    q, k, v, ctx, res, par, vec = s.q, s.k, s.v, s.ctx, s.res, s.par, s.vec

    arrived = place.signal()
    moves = [(x_in, x), (small, s.g_small.at[0, *mine])]
    moves += [(ref, s.g_attn.at[j, *mine]) for j, ref in enumerate((wq, wk, wv, wo))]
    moves += [(wi.at[:, j * width:(j + 1) * width], s.g_inner.at[j, *mine]) for j in range(panels)]
    moves += [(wout, s.g_outer.at[0, *mine]), (cot_in, cot)]
    moves = [pltpu.make_async_copy(src, dst, s.in_sem.at[i]) for i, (src, dst) in enumerate(moves)]
    for move in moves:
        move.start()
    for move in moves[:-1]:
        move.wait()
    arrived()

    def emit(i, src, dst):
        return pltpu.make_async_copy(src, dst, s.out_sem.at[i])

    results = [
        emit(i, src, dst) for i, (src, dst) in enumerate((
            (s.out, layer_out), (s.grad, hidden_grad), (s.squares.at[0], o_q), (s.squares.at[1], o_k), (s.squares.at[2], o_v),
            (s.squares.at[3], o_o), (s.wide, o_inner), (s.tall, o_outer), (s.total, o_vec)))]
    x_copy = pltpu.make_async_remote_copy(
        src_ref=x, dst_ref=s.xs, send_sem=s.x_sem.at[0], recv_sem=s.x_sem.at[1],
        device_id=sibling, device_id_type=MESH)
    x_copy.start()
    tiny, attn, inner, outer = (
        Gather(place, ref, rest[2 * i], rest[2 * i + 1], kind)
        for i, (ref, kind) in enumerate(((s.g_small, SMALL), (s.g_attn, PANELS), (s.g_inner, PANELS), (s.g_outer, ROWS))))
    first = (attn, tiny)
    for one in first:
        one.begin()
    for one in first:
        one.spread(0)
    for dz in range(1, nz):
        for one in first:
            one.column(dz)
    attn.rise()
    inner.begin()
    for dz in range(nz):
        for one in first:
            one.plane(dz)
    attn.relay(1)
    inner.spread(0)
    attn.relay(2)
    for dz in range(1, nz):
        inner.column(dz)
    attn.relay(3)
    inner.rise()
    for dz in range(nz):
        for one in first:
            one.corner(dz)
    outer.begin()
    for one in first:
        one.finish_core()
    x_copy.wait()

    def weight(ref, j):
        return ref[j].reshape(full)

    def outer_weight(j):
        n = pages // panels
        return s.g_outer[0, pl.ds(j * n, n)].reshape(full)

    gathered = s.g_small[0].reshape(2 * pages, VEC_ROWS, LANES)
    par[...] = spread_lanes(gathered, rows, width, 0)
    for j in range(panels):
        par[VECTORS + j:VECTORS + j + 1, :] = spread_lanes(gathered, panels * rows, width, j * width)[VECTORS:VECTORS + 1]
    vec[...] = jnp.zeros_like(vec)

    def vector(j):
        return par[j:j + 1, :]

    q[...] = (dot(x[...], weight(s.g_attn, 0)) + vector(0)).astype(BF)
    inner.plane(0)

    def project(i, _):
        ref, half = (x, c) if i == 0 else (s.xs, 1 - c)
        rows_of = pl.ds(pl.multiple_of(half * seg, seg), seg)
        k[:, rows_of, :] = dot(ref[...], weight(s.g_attn, 1)).astype(BF).reshape(local_pages, seg, width)
        v[:, rows_of, :] = (dot(ref[...], weight(s.g_attn, 2)) + vector(1)).astype(BF).reshape(local_pages, seg, width)

    project(0, 0)
    inner.plane(1)
    project(1, 0)
    inner.plane(2)

    pairs = heads // 2
    head_dim = width // heads

    def place_of(i):
        page, pair = i // pairs, lax.rem(i, pairs)
        return page, pl.ds(pl.multiple_of(page * seg, seg), seg), pl.ds(pl.multiple_of(pair * LANES, LANES), LANES)

    low_half = lax.broadcasted_iota(jnp.int32, (1, LANES), 1) < head_dim
    key_at = lax.broadcasted_iota(jnp.int32, (1, page_len), 1)

    def one_head(values, head):
        return jnp.where(low_half if head == 0 else jnp.logical_not(low_half), values, jnp.zeros_like(values))

    def probabilities(q2, k2, head, usable):
        t = jnp.where(usable, dot(q2, one_head(k2, head), NT) * (scale * LOG2E), masked_value)
        e = jnp.exp2(t - jnp.max(t, axis=-1, keepdims=True))
        return e * (1.0 / jnp.sum(e, axis=-1, keepdims=True))

    def attend(i):
        page, rows_of, cols = place_of(i)
        q2, k2, v2 = q[rows_of, cols], k[page, :, cols], v[page, :, cols]
        usable = key_at < lengths[page]
        parts = [dot(probabilities(q2, k2, head, usable).astype(BF), v2) for head in range(2)]
        ctx[rows_of, cols] = jnp.where(low_half, *parts).astype(BF)

    steps_loop(local_pages * pairs, attend, {
        0: [lambda: inner.plane(3), lambda: inner.relay(1), lambda: outer.spread(0)],
        1: [lambda: outer.column(1), lambda: inner.relay(2)],
        2: [lambda: outer.column(2), outer.rise],
        3: [lambda: outer.column(3), lambda: inner.relay(3)],
        4: [lambda: inner.corner(0)],
        5: [lambda: inner.corner(1)],
        6: [lambda: inner.corner(2), lambda: outer.relay(1)],
        7: [lambda: inner.corner(3)],
        8: [lambda: outer.plane(0), lambda: outer.relay(2)],
        9: [lambda: outer.plane(1)],
        10: [lambda: outer.plane(2), lambda: outer.relay(3)],
        11: [lambda: outer.plane(3)],
    })

    res[...] = dot(ctx[...], weight(s.g_attn, 3))
    chunk = 128

    def chunks(body):
        def one(i, _):
            body(pl.ds(pl.multiple_of(i * chunk, chunk), chunk))
            return 0
        lax.fori_loop(0, tokens // chunk, one, 0)

    def norm_one(at):
        xhat, r = standardize(x[at, :].astype(F32) + res[at, :] + vector(2))
        s.xhat[at, :] = xhat
        s.r_one[at, :] = r
        normed = xhat * vector(3) + vector(4)
        s.low[at, :] = normed.astype(BF)
        res[at, :] = normed + vector(5)

    chunks(norm_one)

    inner.finish_core()
    root_half = 0.7071067811865476

    def expand(j):
        pre = dot(s.low[...], weight(s.g_inner, j)) + par[pl.ds(VECTORS + j, 1), :]
        half_one = 0.5 * (1.0 + lax.erf(pre * root_half))
        bell = jnp.exp2(pre * pre * (-0.5 * LOG2E)) * 0.3989422804014327
        s.post[j] = (pre * half_one).astype(BF)
        s.slope[j] = (half_one + pre * bell).astype(BF)

    steps_loop(panels, expand, {j: [lambda j=j: outer.corner(j)] for j in range(nz)})
    outer.finish_core()

    def contract(j, _):
        res[...] += dot(s.post[j], outer_weight(j))
        return 0

    lax.fori_loop(0, panels, contract, 0)

    def norm_two(at):
        xhat, r = standardize(res[at, :])
        s.out[at, :] = (xhat * vector(6) + vector(7)).astype(BF)
        grad = cot[at, :].astype(F32)
        add_row(vec, 6, grad * xhat)
        add_row(vec, 7, grad)
        d_res = norm_back(grad, xhat, r, vector(6))
        res[at, :] = d_res
        d_low = d_res.astype(BF)
        s.d_low[at, :] = d_low
        add_row(vec, 5, d_low.astype(F32))

    moves[-1].wait()
    chunks(norm_two)
    results[0].start()

    reducers = [
        Reduce(place, part, rest[8 + REDUCE_REFS * i:8 + REDUCE_REFS * (i + 1)], kind)
        for i, (part, kind) in enumerate(((s.g_outer, ROWS), (s.g_inner, PANELS), (s.p_one, PANELS), (s.p_two, PANELS)))]
    r_outer, r_inner, r_first, r_second = reducers
    outer.drain()

    def outer_back(dz):
        j = lax.rem(place.z + dz, nz)
        d_low = s.d_low[...]
        d_pre = (dot(d_low, outer_weight(j), NT) * s.slope[j].astype(F32)).astype(BF)
        n = pages // panels
        s.g_outer[0, pl.ds(j * n, n)] = dot(s.post[j], d_low, TN).reshape(n, 2, panels * rows, width).astype(BF)
        r_outer.begin(dz)
        s.slope[j] = d_pre
        vec[pl.ds(VECTORS + j, 1), :] = jnp.sum(d_pre.astype(F32), axis=0, keepdims=True)

    steps_loop(nz, outer_back, {
        1: [lambda: r_outer.arrive(0), lambda: r_outer.corner(0)],
        2: [lambda: r_outer.arrive(1), lambda: r_outer.corner(1)],
        3: [lambda: r_outer.arrive(2), lambda: r_outer.corner(2)],
    })
    inner.drain()

    def inner_back(j):
        d_pre = s.slope[j]
        res[...] += dot(d_pre, weight(s.g_inner, j), NT)
        s.g_inner[j] = dot(s.low[...], d_pre, TN).reshape(blocks).astype(BF)

    steps_loop(panels, inner_back, {
        0: [lambda: r_outer.arrive(3), lambda: r_outer.corner(3), lambda: r_outer.relay(3), lambda: r_outer.plane(0)],
        1: [lambda: r_outer.plane(1), lambda: r_outer.relay(2)],
        2: [lambda: r_outer.plane(2), lambda: r_outer.relay(1)],
        3: [lambda: r_outer.plane(3), r_outer.settle],
    })
    for dz in range(nz):
        r_inner.begin(dz)

    def norm_one_back(at):
        grad, xhat = res[at, :], s.xhat[at, :]
        add_row(vec, 3, grad * xhat)
        add_row(vec, 4, grad)
        d_res = norm_back(grad, xhat, s.r_one[at, :], vector(3))
        res[at, :] = d_res
        d_low = d_res.astype(BF)
        s.d_low[at, :] = d_low
        add_row(vec, 2, d_low.astype(F32))

    chunks(norm_one_back)
    s.d_ctx[...] = dot(s.d_low[...], weight(s.g_attn, 3), NT).astype(BF)
    s.p_one[0] = dot(ctx[...], s.d_low[...], TN).reshape(blocks).astype(BF)
    for dz in range(nz):
        r_inner.arrive(dz)
    r_inner.corner(0)
    r_inner.corner(1)

    d_q, d_k, d_v = s.post.at[0], s.post.at[1:1 + local_pages], s.slope.at[0:local_pages]

    def kv_copies(page):
        theirs = pl.ds(pl.multiple_of((1 - c) * seg, seg), seg)
        return [
            pltpu.make_async_remote_copy(
                src_ref=grad.at[page, theirs], dst_ref=got.at[page], send_sem=s.kv_sem.at[2 * n, page],
                recv_sem=s.kv_sem.at[2 * n + 1, page], device_id=sibling, device_id_type=MESH)
            for n, (grad, got) in enumerate(((d_k, s.rk), (d_v, s.rv)))]

    def attend_back(i):
        page, rows_of, cols = place_of(i)
        q2, k2, v2 = q[rows_of, cols], k[page, :, cols], v[page, :, cols]
        c2 = s.d_ctx[rows_of, cols]
        usable = key_at < lengths[page]
        parts = []
        for head in range(2):
            p = probabilities(q2, k2, head, usable)
            d_p = dot(c2, one_head(v2, head), NT)
            d_s = (p * (d_p - jnp.sum(p * d_p, axis=-1, keepdims=True))).astype(BF)
            parts.append((dot(d_s, k2), dot(d_s, q2, TN), dot(p.astype(BF), c2, TN)))
        both = [jnp.where(low_half, one, two) for one, two in zip(*parts)]
        d_q[rows_of, cols] = (both[0] * scale).astype(BF)
        d_k[page, :, cols] = (both[1] * scale).astype(BF)
        d_v[page, :, cols] = both[2].astype(BF)

    def send_kv(page):
        for copy in kv_copies(page):
            copy.start()

    def finish_outer():
        s.tall[...] = r_outer.finish()[0]
        results[7].start()

    steps_loop(local_pages * pairs, attend_back, {
        0: [lambda: r_inner.corner(2)],
        1: [lambda: r_inner.corner(3)],
        2: [lambda: r_outer.column(1), lambda: r_inner.relay(3)],
        3: [lambda: r_outer.column(2)],
        4: [lambda: r_outer.column(3)],
        5: [lambda: r_inner.plane(0), lambda: r_inner.relay(2)],
        6: [lambda: r_inner.plane(1)],
        7: [lambda: r_inner.plane(2), lambda: r_inner.relay(1)],
        8: [lambda: r_inner.plane(3)],
        9: [finish_outer, r_inner.settle],
    })
    for page in range(local_pages):
        send_kv(page)
    s.p_one[1] = dot(x[...], d_q[...], TN).reshape(blocks).astype(BF)
    for dz in range(nz):
        r_first.begin(dz)
    add_row(vec, 0, d_q[...].astype(F32))
    for page in range(local_pages):
        for copy in kv_copies(page):
            copy.wait()
    ours = pl.ds(pl.multiple_of(c * seg, seg), seg)
    for j, (grad, got) in enumerate(((d_k, s.rk), (d_v, s.rv))):
        total = (grad[:, ours, :].astype(F32) + got[...].astype(F32)).astype(BF)
        got[...] = total
        total = total.reshape(tokens, width)
        if j == 1:
            add_row(vec, 1, total.astype(F32))
        s.p_two[j] = dot(x[...], total, TN).reshape(blocks).astype(BF)
    vectors = VectorSum(place, rest[8 + 4 * REDUCE_REFS:])
    vectors.put(0, vec[...])
    for dz in range(nz):
        r_second.begin(dz)

    def loop(start, body):
        def one(dz, _):
            body(dz)
            return 0
        lax.fori_loop(start, nz, one, 0)

    loop(0, r_first.arrive)
    loop(0, r_first.corner)
    r_first.relay(3)
    loop(1, r_inner.column)
    vectors.put(1, vectors.take(0))
    loop(0, r_second.arrive)
    loop(0, r_second.corner)
    r_first.relay(2)
    r_second.relay(3)
    vectors.put(2, vectors.take(1))
    loop(0, r_first.plane)
    r_first.relay(1)
    r_second.relay(2)
    vectors.put(3, vectors.take(2))
    loop(0, r_second.plane)
    r_second.relay(1)
    r_first.settle()
    d_keys, d_values = s.rk[...].reshape(tokens, width), s.rv[...].reshape(tokens, width)
    res[...] += dot(d_q[...], weight(s.g_attn, 0), NT)
    res[...] += dot(d_keys, weight(s.g_attn, 1), NT)
    s.grad[...] = (res[...] + dot(d_values, weight(s.g_attn, 2), NT)).astype(BF)
    r_second.settle()
    total = r_inner.finish()
    for j in range(panels):
        s.wide[:, j * width:(j + 1) * width] = total[j]
    results[1].start()
    results[6].start()
    loop(1, r_first.column)
    loop(1, r_second.column)
    s.total[...] = vectors.take(3)
    results[8].start()
    total = r_first.finish()
    s.squares[3] = total[0]
    s.squares[0] = total[1]
    results[2].start()
    results[5].start()
    total = r_second.finish()
    s.squares[1] = total[0]
    s.squares[2] = total[1]
    results[3].start()
    results[4].start()
    tiny.drain()
    attn.drain()
    for one in reducers:
        one.drain()
    vectors.drain()
    for result in results:
        result.wait()


def finish_kernel(rows, panels, out, grad, g_q, g_k, g_v, g_o, g_inner, g_outer, total, *refs):
    outs, owned, held, sems = refs[:8], refs[8:8 + VECTORS + 1], refs[8 + VECTORS + 1:-1], refs[-1]
    copies = [
        (pltpu.make_async_copy(src, way, sems.at[i, 0]), pltpu.make_async_copy(way, dst, sems.at[i, 1]))
        for i, (src, way, dst) in enumerate(zip((out, grad, g_q, g_k, g_v, g_o, g_inner, g_outer), held, outs))]
    for copy, _ in copies:
        copy.start()
    for copy, onward in copies:
        copy.wait()
        onward.start()
    at = lax.axis_index(PAGE) * 2 + lax.axis_index(SEQ)
    width = total.shape[1]
    mine = pltpu.roll(total[0:VECTORS, :], width - rows * at, 1)
    for j, ref in enumerate(owned[:VECTORS]):
        ref[...] = mine[j, :rows]
    per_row = width // (panels * rows)
    row = total[pl.ds(VECTORS + at // per_row, 1), :]
    mine = pltpu.roll(row, width - panels * rows * lax.rem(at, per_row), 1)
    owned[VECTORS][...] = mine[0, :panels * rows]
    for _, onward in copies:
        onward.wait()


def finish(rows, panels, arrays):
    hbm, vm = pl.BlockSpec(memory_space=pl.ANY), pl.BlockSpec(memory_space=VMEM)
    return pl.pallas_call(
        functools.partial(finish_kernel, rows, panels),
        name="finish",
        out_shape=tuple(jax.ShapeDtypeStruct(a.shape, a.dtype) for a in arrays[:8])
        + (jax.ShapeDtypeStruct((rows,), F32),) * VECTORS + (jax.ShapeDtypeStruct((panels * rows,), F32),),
        in_specs=[hbm] * 8 + [vm],
        out_specs=(hbm,) * 8 + (vm,) * (VECTORS + 1),
        scratch_shapes=[VMEM(a.shape, a.dtype) for a in arrays[:8]] + [DMA((8, 2))],
    )(*arrays)


def whole_layer(pages, heads, lengths, x, cot, wq, wk, wv, wo, wi, wout, small, local_pages):
    tokens, width = x.shape
    rows, panels = wq.shape[0], wi.shape[1] // width
    own, scratch = layer_scratch(pages, rows, width, panels, tokens, local_pages)
    hbm = pl.BlockSpec(memory_space=pl.ANY)
    row_shape = jax.ShapeDtypeStruct((tokens, width), BF)
    square = jax.ShapeDtypeStruct((rows, width), F32)
    return pl.pallas_call(
        functools.partial(layer_kernel, pages, heads, tuple(own)),
        name="whole_layer",
        out_shape=(row_shape, row_shape, square, square, square, square,
                   jax.ShapeDtypeStruct((rows, panels * width), F32),
                   jax.ShapeDtypeStruct((panels * rows, width), F32),
                   jax.ShapeDtypeStruct((VEC_ROWS, width), F32)),
        in_specs=[pl.BlockSpec(memory_space=pltpu.SMEM)] + [hbm] * 9,
        out_specs=(hbm,) * 9,
        scratch_shapes=[*own.values(), *scratch],
        compiler_params=pltpu.CompilerParams(collective_id=0, has_side_effects=True, vmem_limit_bytes=61 << 20),
    )(lengths, x, cot, wq, wk, wv, wo, wi, wout, small)


def plain_layer(
    hidden,
    lengths,
    w_query,
    w_key,
    w_value,
    w_output,
    b_query,
    b_value,
    b_output,
    attn_gain,
    attn_shift,
    w_inner,
    b_inner,
    w_outer,
    b_outer,
    ffn_gain,
    ffn_shift,
    cotangent,
):
    model_width = hidden.shape[2]
    head_count = HEADS
    score_scale = (model_width // head_count) ** (-0.5)
    f32 = jnp.float32
    bf16 = jnp.bfloat16
    work_hidden, work_cot = (hidden, cotangent)
    local_pages, local_tokens = (work_hidden.shape[0], work_hidden.shape[1])
    row_count = local_pages * local_tokens
    (
        query_full,
        key_full,
        value_full,
        output_full,
        query_bias,
        value_bias,
        output_bias,
        gain_one,
        shift_one,
    ) = (
        lax.all_gather(w_query, AXES, axis=0, tiled=True),
        lax.all_gather(w_key, AXES, axis=0, tiled=True),
        lax.all_gather(w_value, AXES, axis=0, tiled=True),
        lax.all_gather(w_output, AXES, axis=0, tiled=True),
        lax.all_gather(b_query, AXES, axis=0, tiled=True),
        lax.all_gather(b_value, AXES, axis=0, tiled=True),
        lax.all_gather(b_output, AXES, axis=0, tiled=True),
        lax.all_gather(attn_gain, AXES, axis=0, tiled=True),
        lax.all_gather(attn_shift, AXES, axis=0, tiled=True),
    )
    flat_rows = work_hidden.reshape(row_count, model_width)
    queries = (matmul(flat_rows, query_full) + query_bias.astype(f32)).astype(bf16)
    key_rows = matmul(flat_rows, key_full).astype(bf16)
    value_rows = (matmul(flat_rows, value_full) + value_bias.astype(f32)).astype(bf16)
    query_heads = head_split(queries.reshape(local_pages, local_tokens, model_width), head_count)
    key_pages = key_rows.reshape(local_pages, local_tokens, model_width)
    value_pages = value_rows.reshape(local_pages, local_tokens, model_width)
    stat_shape = (local_pages, head_count, local_tokens)
    stat_start = (jnp.full(stat_shape, masked_value, f32), jnp.zeros(stat_shape, f32))
    key_piece = lax.all_gather(key_pages, SEQ, axis=1, tiled=True)
    usable = usable_keys(lengths, key_piece.shape[1])

    def merged():
        run_peak, run_total = stat_start
        scores = page_scores(query_heads, key_piece, usable, score_scale)
        new_peak = jnp.maximum(run_peak, jnp.max(scores, axis=-1))
        summed = jnp.sum(jnp.exp(scores - new_peak[..., None]), axis=-1)
        return (new_peak, summed)

    run_peak, run_total = merged()
    log_norm = run_peak + jnp.log(run_total)
    add_key_piece = lax.all_gather(key_pages, SEQ, axis=1, tiled=True)
    value_piece = lax.all_gather(value_pages, SEQ, axis=1, tiled=True)
    add_usable = usable_keys(lengths, add_key_piece.shape[1])

    def merged():
        scores = page_scores(query_heads, add_key_piece, add_usable, score_scale)
        attn_probs = jnp.exp(scores - log_norm[..., None]).astype(bf16)
        addend = jnp.einsum(
            "phqk,pkhd->pqhd",
            attn_probs,
            head_split(value_piece, head_count),
            preferred_element_type=f32,
        )
        return addend.reshape(local_pages, local_tokens, model_width)

    context = merged()
    context_low = context.astype(bf16).reshape(row_count, model_width)
    residual_one = (
        flat_rows.astype(f32) + matmul(context_low, output_full) + output_bias.astype(f32)
    )
    normed_one, pull_one = jax.vjp(
        layer_norm, residual_one, gain_one.astype(f32), shift_one.astype(f32)
    )
    inner_full, outer_full, inner_bias, outer_bias, gain_two, shift_two = (
        lax.all_gather(w_inner, AXES, axis=0, tiled=True),
        lax.all_gather(w_outer, AXES, axis=0, tiled=True),
        lax.all_gather(b_inner, AXES, axis=0, tiled=True),
        lax.all_gather(b_outer, AXES, axis=0, tiled=True),
        lax.all_gather(ffn_gain, AXES, axis=0, tiled=True),
        lax.all_gather(ffn_shift, AXES, axis=0, tiled=True),
    )
    normed_low = normed_one.astype(bf16)
    pre_gelu = matmul(normed_low, inner_full) + inner_bias.astype(f32)
    post_gelu, pull_gelu = jax.vjp(gelu_exact, pre_gelu)
    post_low = post_gelu.astype(bf16)
    residual_two = normed_one + matmul(post_low, outer_full) + outer_bias.astype(f32)
    layer_out, pull_two = jax.vjp(
        layer_norm, residual_two, gain_two.astype(f32), shift_two.astype(f32)
    )
    cot_rows = work_cot.reshape(row_count, model_width).astype(f32)
    d_res_two, gain_two_grad, shift_two_grad = pull_two(cot_rows)
    d_outer = d_res_two.astype(bf16)
    outer_w_grad = matmul(post_low.T, d_outer)
    outer_b_grad = column_sum(d_outer)
    (d_pre_full,) = pull_gelu(matmul(d_outer, outer_full.T))
    d_pre = d_pre_full.astype(bf16)
    inner_w_grad = matmul(normed_low.T, d_pre)
    inner_b_grad = column_sum(d_pre)
    d_normed = d_res_two + matmul(d_pre, inner_full.T)
    d_res_one, gain_one_grad, shift_one_grad = pull_one(d_normed)
    ffn_owned = (
        lax.psum_scatter(inner_w_grad, AXES, scatter_dimension=0, tiled=True),
        lax.psum_scatter(outer_w_grad, AXES, scatter_dimension=0, tiled=True),
        lax.psum_scatter(inner_b_grad, AXES, scatter_dimension=0, tiled=True),
        lax.psum_scatter(outer_b_grad, AXES, scatter_dimension=0, tiled=True),
        lax.psum_scatter(gain_two_grad, AXES, scatter_dimension=0, tiled=True),
        lax.psum_scatter(shift_two_grad, AXES, scatter_dimension=0, tiled=True),
    )
    d_attn = d_res_one.astype(bf16)
    output_w_grad = matmul(context_low.T, d_attn)
    output_b_grad = column_sum(d_attn)
    d_context = matmul(d_attn, output_full.T).astype(bf16)
    d_context_heads = head_split(
        d_context.reshape(local_pages, local_tokens, model_width), head_count
    )
    context_heads = head_split(context, head_count)
    row_delta = jnp.transpose(
        jnp.sum(d_context_heads.astype(f32) * context_heads, axis=-1), (0, 2, 1)
    )

    def add_grads(segment):
        key_piece, value_piece = segment
        seg_len = key_piece.shape[1]
        usable = usable_keys(lengths, seg_len)

        def merged():
            scores = page_scores(query_heads, key_piece, usable, score_scale)
            attn_probs = jnp.exp(scores - log_norm[..., None])
            key_heads = head_split(key_piece, head_count)
            value_heads = head_split(value_piece, head_count)
            d_probs = jnp.einsum(
                "pqhd,pkhd->phqk", d_context_heads, value_heads, preferred_element_type=f32
            )
            d_scores = (attn_probs * (d_probs - row_delta[..., None])).astype(bf16)
            query_part = jnp.einsum(
                "phqk,pkhd->pqhd", d_scores, key_heads, preferred_element_type=f32
            )
            key_part = jnp.einsum(
                "phqk,pqhd->pkhd", d_scores, query_heads, preferred_element_type=f32
            )
            value_part = jnp.einsum(
                "phqk,pqhd->pkhd",
                attn_probs.astype(bf16),
                d_context_heads,
                preferred_element_type=f32,
            )
            query_grad = query_part.reshape(local_pages, local_tokens, model_width) * score_scale
            key_grads = key_part.reshape(local_pages, seg_len, model_width) * score_scale
            value_grads = value_part.reshape(local_pages, seg_len, model_width)
            return (query_grad, key_grads, value_grads)

        return merged()

    query_grad, key_grads, value_grads = add_grads(
        (
            lax.all_gather(key_pages, SEQ, axis=1, tiled=True),
            lax.all_gather(value_pages, SEQ, axis=1, tiled=True),
        )
    )
    key_owned, value_owned = (
        lax.psum_scatter(
            key_grads.astype(jnp.bfloat16), SEQ, scatter_dimension=1, tiled=True
        ).astype(jnp.float32),
        lax.psum_scatter(
            value_grads.astype(jnp.bfloat16), SEQ, scatter_dimension=1, tiled=True
        ).astype(jnp.float32),
    )
    d_queries = query_grad.astype(bf16).reshape(row_count, model_width)
    d_keys = key_owned.astype(bf16).reshape(row_count, model_width)
    d_values = value_owned.astype(bf16).reshape(row_count, model_width)
    query_w_grad = matmul(flat_rows.T, d_queries)
    key_w_grad = matmul(flat_rows.T, d_keys)
    value_w_grad = matmul(flat_rows.T, d_values)
    query_b_grad = column_sum(d_queries)
    value_b_grad = column_sum(d_values)
    hidden_grad = (
        d_res_one
        + matmul(d_queries, query_full.T)
        + matmul(d_keys, key_full.T)
        + matmul(d_values, value_full.T)
    ).astype(bf16)
    attn_owned = (
        lax.psum_scatter(query_w_grad, AXES, scatter_dimension=0, tiled=True),
        lax.psum_scatter(key_w_grad, AXES, scatter_dimension=0, tiled=True),
        lax.psum_scatter(value_w_grad, AXES, scatter_dimension=0, tiled=True),
        lax.psum_scatter(output_w_grad, AXES, scatter_dimension=0, tiled=True),
        lax.psum_scatter(query_b_grad, AXES, scatter_dimension=0, tiled=True),
        lax.psum_scatter(value_b_grad, AXES, scatter_dimension=0, tiled=True),
        lax.psum_scatter(output_b_grad, AXES, scatter_dimension=0, tiled=True),
        lax.psum_scatter(gain_one_grad, AXES, scatter_dimension=0, tiled=True),
        lax.psum_scatter(shift_one_grad, AXES, scatter_dimension=0, tiled=True),
    )
    out_pages = layer_out.astype(bf16).reshape(local_pages, local_tokens, model_width)
    grad_pages = hidden_grad.reshape(local_pages, local_tokens, model_width)
    return (
        out_pages,
        grad_pages,
        attn_owned[0],
        attn_owned[1],
        attn_owned[2],
        attn_owned[3],
        attn_owned[4],
        attn_owned[5],
        attn_owned[6],
        attn_owned[7],
        attn_owned[8],
        ffn_owned[0],
        ffn_owned[2],
        ffn_owned[1],
        ffn_owned[3],
        ffn_owned[4],
        ffn_owned[5],
    )


def per_device(pages, hidden, lengths, w_query, w_key, w_value, w_output, b_query, b_value, b_output, attn_gain, attn_shift,
               w_inner, b_inner, w_outer, b_outer, ffn_gain, ffn_shift, cotangent):
    local_pages, seg, width = hidden.shape
    rows, panels = w_query.shape[0], w_inner.shape[1] // width
    nz, _, _ = page_grid(pages)
    if rows % 8 or nz != panels or local_pages * seg != 2 * seg or 4 * rows > 128:
        return plain_layer(hidden, lengths, w_query, w_key, w_value, w_output, b_query, b_value, b_output, attn_gain, attn_shift,
                           w_inner, b_inner, w_outer, b_outer, ffn_gain, ffn_shift, cotangent)
    small = pack_vectors((b_query, b_value, b_output, attn_gain, attn_shift, b_outer, ffn_gain, ffn_shift), b_inner)
    flat = local_pages * seg, width
    arrays = whole_layer(
        pages, HEADS, lengths, hidden.reshape(flat), cotangent.reshape(flat), w_query, w_key, w_value, w_output, w_inner, w_outer,
        small, local_pages)
    out, grad, g_q, g_k, g_v, g_o, g_inner, g_outer, *own = finish(rows, panels, arrays)
    return (out.reshape(hidden.shape), grad.reshape(hidden.shape), g_q, g_k, g_v, g_o, own[0], own[1], own[2], own[3], own[4],
            g_inner, own[8], g_outer, own[5], own[6], own[7])


def solution(mesh):
    in_specs = (
        P(PAGE, SEQ, None),
        P(PAGE),
        P(AXES, None),
        P(AXES, None),
        P(AXES, None),
        P(AXES, None),
        P(AXES),
        P(AXES),
        P(AXES),
        P(AXES),
        P(AXES),
        P(AXES, None),
        P(AXES),
        P(AXES, None),
        P(AXES),
        P(AXES),
        P(AXES),
        P(PAGE, SEQ, None),
    )
    out_specs = (
        P(PAGE, SEQ, None),
        P(PAGE, SEQ, None),
        P(AXES, None),
        P(AXES, None),
        P(AXES, None),
        P(AXES, None),
        P(AXES),
        P(AXES),
        P(AXES),
        P(AXES),
        P(AXES),
        P(AXES, None),
        P(AXES),
        P(AXES, None),
        P(AXES),
        P(AXES),
        P(AXES),
    )
    return jax.shard_map(
        functools.partial(per_device, mesh.shape[PAGE]), mesh=mesh, in_specs=in_specs, out_specs=out_specs, check_vma=False
    )
```

```python
import functools
import types
import jax
import jax.numpy as jnp
from jax import lax
from jax.experimental import pallas as pl
from jax.experimental.pallas import tpu as pltpu

from jax.sharding import PartitionSpec as P

MESH = pl.DeviceIdType.MESH
VMEM = pltpu.VMEM
DMA = pltpu.SemaphoreType.DMA
BF = jnp.bfloat16
F32 = jnp.float32
LANES = 128
AXES = PAGE, SEQ = ("page", "seq")
SMALL, PANELS, ROWS = range(3)
SPREAD_RELAY = 128
REDUCE_RELAY = 128


def page_grid(pages):
    bits = pages.bit_length() - 1
    nx = 2 ** (bits // 3)
    ny = 2 ** ((bits - bits // 3) // 2)
    return pages // (nx * ny), ny, nx


class Place:
    def __init__(self, pages):
        self.nz, self.ny, self.nx = page_grid(pages)
        self.plane = self.ny * self.nx
        self.p = lax.axis_index(PAGE)
        self.c = lax.axis_index(SEQ)
        self.x = lax.rem(self.p, self.nx)
        self.y = lax.rem(self.p // self.nx, self.ny)
        self.z = self.p // self.plane
        self.sibling = (self.p, 1 - self.c)
        self.others = [(dy, dx) for dy in range(self.ny) for dx in range(self.nx) if dy or dx]

    def page(self, dz=0, dy=0, dx=0):
        z = lax.rem(self.z + dz + self.nz, self.nz)
        y = lax.rem(self.y + dy + self.ny, self.ny)
        x = lax.rem(self.x + dx + self.nx, self.nx)
        return (z * self.ny + y) * self.nx + x

    def level(self, dz):
        return lax.rem(self.z + dz + self.nz, self.nz) * self.plane

    def there(self, dz=0, dy=0, dx=0):
        return self.page(dz, dy, dx), self.c

    def signal(self):
        barrier = pltpu.get_barrier_semaphore()
        partners = [self.there(dz=d) for d in range(1, self.nz)] + [self.there(0, *d) for d in self.others] + [self.sibling]
        for partner in partners:
            pl.semaphore_signal(barrier, inc=1, device_id=partner, device_id_type=MESH)
        return lambda: pl.semaphore_wait(barrier, len(partners))


def slots(sizes):
    base, at = [], 0
    for size in sizes:
        base.append(at)
        at += size
    return base, at


def gather_slots(pages):
    nz, ny, nx = page_grid(pages)
    return slots((1, 1, 1, nz, nz)), slots((nz - 1, nz * (nx - 1), nz * (ny - 1), nz * (nx - 1) * (ny - 1), 1, nz, 1))


class Gather:
    def __init__(self, place, ref, send, recv, kind):
        self.pl, self.ref, self.send, self.recv, self.kind = place, ref, send, recv, kind
        (self.sbase, _), (self.rbase, _) = gather_slots(place.nz * place.plane)
        self.low = 0 if kind == SMALL else SPREAD_RELAY

    def view(self, page, part, core=None, count=None):
        ref, low = self.ref, self.low
        core = self.pl.c if core is None else core
        pages = page if count is None else pl.ds(page, count)
        if part == 3:
            return ref.at[:, pages, core, :, 0:low]
        if part == 4:
            return ref.at[:, pages, core]
        if part == 0 or self.kind == SMALL:
            return ref.at[:, pages, core, :, low:]
        if self.kind == PANELS:
            n = ref.shape[0] // 2
            return ref.at[(part - 1) * n:part * n, pages, core, :, low:]
        n = ref.shape[3] // 2
        return ref.at[:, pages, core, (part - 1) * n:part * n, low:]

    def copy(self, view, send, recv, target):
        return pltpu.make_async_remote_copy(
            src_ref=view, dst_ref=view, send_sem=self.send.at[send], recv_sem=self.recv.at[recv],
            device_id=target, device_id_type=MESH)

    def plain(self, group, slot, page, part, target):
        return self.copy(self.view(page, part), self.sbase[0], self.rbase[group] + slot, target)

    def corner_slot(self, dx, dy, dz):
        return (dz * (self.pl.ny - 1) + dy - 1) * (self.pl.nx - 1) + dx - 1

    def z_copy(self, dz, mine):
        p = self.pl
        return self.plain(0, dz - 1, p.page(0 if mine else -dz), 0, p.there(dz=dz))

    def x_copy(self, dx, dz, mine):
        p = self.pl
        return self.plain(1, dz * (p.nx - 1) + dx - 1, p.page(-dz, 0, 0 if mine else -dx), 0, p.there(dx=dx))

    def y_copy(self, dy, dz, mine):
        p = self.pl
        return self.plain(2, dz * (p.ny - 1) + dy - 1, p.page(-dz, 0 if mine else -dy, 0), 0, p.there(dy=dy))

    def xa_copy(self, dx, dy, dz):
        p = self.pl
        return self.plain(3, self.corner_slot(dx, dy, dz), p.page(-dz, -dy, 0), 1, p.there(dx=dx))

    def yb_copy(self, dx, dy, dz):
        p = self.pl
        return self.plain(3, self.corner_slot(dx, dy, dz), p.page(-dz, 0, -dx), 2, p.there(dy=dy))

    def core_copy(self, page, part, count=None):
        return self.copy(self.view(page, part, None, count), self.sbase[1], self.rbase[6], self.pl.sibling)

    def relay_copy(self, level, up):
        p = self.pl
        group = level // p.plane
        target = p.there(dz=1 if up else p.nz - 1)
        return self.copy(self.view(level, 3, None, p.plane), self.sbase[3 if up else 4] + group, self.rbase[5] + group, target)

    def wait(self, view, sem):
        pltpu.make_async_copy(view, view, sem).wait()

    def begin(self):
        p = self.pl
        if self.low:
            for dy, dx in p.others:
                self.copy(self.view(p.page(), 3), self.sbase[2], self.rbase[4], p.there(0, dy, dx)).start()
        for d in range(1, p.nz):
            self.z_copy(d, True).start()

    def spread(self, dz):
        p = self.pl
        for d in range(1, p.nx):
            self.x_copy(d, dz, True).start()
        for d in range(1, p.ny):
            self.y_copy(d, dz, True).start()
        self.core_copy(p.page(-dz), 0).start()

    def column(self, dz):
        self.z_copy(dz, False).wait_recv()
        self.spread(dz)

    def rise(self):
        p = self.pl
        if not self.low:
            return
        level = p.level(0)
        self.wait(self.view(level, 3, None, p.plane - 1), self.recv.at[self.rbase[4]])
        pl.when(p.z < p.nz - 1)(lambda: self.relay_copy(level, True).start())
        pl.when(p.z > 0)(lambda: self.relay_copy(level, False).start())
        self.core_copy(level, 3, p.plane).start()

    def relay(self, d):
        p = self.pl
        if not self.low:
            return

        def step(up):
            level = (p.z - d if up else p.z + d) * p.plane
            self.relay_copy(level, up).wait_recv()
            pl.when(p.z < p.nz - 1 if up else p.z > 0)(lambda: self.relay_copy(level, up).start())
            self.core_copy(level, 3, p.plane).start()

        pl.when(p.z >= d)(lambda: step(True))
        pl.when(p.z + d < p.nz)(lambda: step(False))

    def plane(self, dz):
        p = self.pl
        for dy in range(1, p.ny):
            self.y_copy(dy, dz, False).wait_recv()
            for dx in range(1, p.nx):
                self.xa_copy(dx, dy, dz).start()
            self.core_copy(p.page(-dz, -dy), 0).start()
        for dx in range(1, p.nx):
            self.x_copy(dx, dz, False).wait_recv()
            if self.kind != SMALL:
                for dy in range(1, p.ny):
                    self.yb_copy(dx, dy, dz).start()
            self.core_copy(p.page(-dz, 0, -dx), 0).start()

    def corner(self, dz):
        p = self.pl
        for dy in range(1, p.ny):
            for dx in range(1, p.nx):
                page = p.page(-dz, -dy, -dx)
                self.wait(self.view(page, 0), self.recv.at[self.rbase[3] + self.corner_slot(dx, dy, dz)])
                self.core_copy(page, 0).start()

    def finish_core(self):
        self.wait(self.view(0, 4, 1 - self.pl.c, self.pl.nz * self.pl.plane), self.recv.at[self.rbase[6]])

    def drain(self):
        p = self.pl
        pages = p.nz * p.plane
        self.wait(self.view(0, 4, None, pages), self.send.at[self.sbase[1]])
        corners = p.nz * (p.ny - 1) * (p.nx - 1)
        blocks = p.nz - 1 + p.nz * (p.nx - 1) + p.nz * (p.ny - 1) + corners
        if self.low:
            self.wait(self.view(0, 3, None, p.plane - 1), self.send.at[self.sbase[2]])
        self.wait(self.view(0, 0, None, blocks), self.send.at[self.sbase[0]])
        if self.low:
            def group(g):
                pl.when(jnp.logical_and(p.z < p.nz - 1, g <= p.z))(lambda: self.relay_copy(g * p.plane, True).wait_send())
                pl.when(jnp.logical_and(p.z > 0, g >= p.z))(lambda: self.relay_copy(g * p.plane, False).wait_send())
            for g in range(p.nz):
                group(g)


def reduce_slots(pages, low):
    nz, ny, nx = page_grid(pages)
    corners = nz * (nx - 1) * (ny - 1)
    n = nz if low else 0
    return slots((1, 1, 1, n, n)), slots((nz, corners, corners, nz * (nx - 1), nz * (ny - 1), nz - 1, 1, n, n))


def reduce_scratch(pages, panels, rows, width, kind, low):
    nz, ny, nx = page_grid(pages)
    fx, fy = nx - 1, ny - 1
    half = (panels // 2, rows) if kind == PANELS else (panels, rows // 2)
    rest = width - low
    (_, sends), (_, recvs) = reduce_slots(pages, low)
    return [
        VMEM((panels, nz * ny * nx, rows, width), BF),
        VMEM((nz * fx * fy,) + half + (rest,), BF),
        VMEM((nz * fx * fy,) + half + (rest,), BF),
        VMEM((nz * fx, panels, rows, rest), BF),
        VMEM((nz * fy, panels, rows, rest), BF),
        VMEM((nz - 1, panels, rows, rest), BF),
        VMEM((ny * nx - 1, panels, rows, low) if low else (8, LANES), BF),
        VMEM((2, nz, panels, ny * nx, rows, low) if low else (8, LANES), BF),
        DMA((sends,)),
        DMA((recvs,)),
    ]


REDUCE_REFS = 10


class Reduce:
    def __init__(self, place, part, scratch, kind, low):
        self.pl, self.part, self.kind, self.low = place, part, kind, low
        self.total, self.da, self.db, self.rx, self.ry, self.rz, self.rp, self.rr, self.send, self.recv = scratch
        (self.sbase, _), (self.rbase, _) = reduce_slots(place.nz * place.plane, low)

    def remote(self, send, recv, src, dst, target):
        return pltpu.make_async_remote_copy(
            src_ref=src, dst_ref=dst, send_sem=self.send.at[send], recv_sem=self.recv.at[recv],
            device_id=target, device_id_type=MESH)

    def plain(self, group, slot, src, dst, target):
        return self.remote(self.sbase[0], self.rbase[group] + slot, src, dst, target)

    def wait(self, view, sem):
        pltpu.make_async_copy(view, view, sem).wait()

    def half(self, page, which):
        if self.kind == PANELS:
            n = self.total.shape[0] // 2
            return self.total.at[which * n:(which + 1) * n, page, :, self.low:]
        n = self.total.shape[2] // 2
        return self.total.at[:, page, which * n:(which + 1) * n, self.low:]

    def corner_slot(self, dz, dy, dx):
        return (dz * (self.pl.ny - 1) + dy - 1) * (self.pl.nx - 1) + dx - 1

    def core_copy(self, dz):
        p = self.pl
        pages = pl.ds(p.level(dz), p.plane)
        return self.remote(
            self.sbase[1], self.rbase[0] + dz, self.part.at[:, pages, 1 - p.c], self.total.at[:, pages], p.sibling)

    def xa_copy(self, dz, dy, dx):
        p, slot = self.pl, self.corner_slot(dz, dy, dx)
        return self.plain(1, slot, self.half(p.page(dz, dy, dx), 0), self.da.at[slot], p.there(dx=dx))

    def yb_copy(self, dz, dy, dx):
        p, slot = self.pl, self.corner_slot(dz, dy, dx)
        return self.plain(2, slot, self.half(p.page(dz, dy, dx), 1), self.db.at[slot], p.there(dy=dy))

    def x_copy(self, dz, dx):
        p = self.pl
        slot = dz * (p.nx - 1) + dx - 1
        return self.plain(3, slot, self.total.at[:, p.page(dz, 0, dx), :, self.low:], self.rx.at[slot], p.there(dx=dx))

    def y_copy(self, dz, dy):
        p = self.pl
        slot = dz * (p.ny - 1) + dy - 1
        return self.plain(4, slot, self.total.at[:, p.page(dz, dy, 0), :, self.low:], self.ry.at[slot], p.there(dy=dy))

    def z_copy(self, dz):
        p = self.pl
        return self.plain(5, dz - 1, self.total.at[:, p.page(dz), :, self.low:], self.rz.at[dz - 1], p.there(dz=dz))

    def relay_copy(self, level, up):
        p = self.pl
        group, way = level // p.plane, 0 if up else 1
        return self.remote(
            self.sbase[3 + way] + group, self.rbase[7 + way] + group,
            self.total.at[:, pl.ds(level, p.plane), :, 0:self.low], self.rr.at[way, group], p.there(dz=1 if up else p.nz - 1))

    def plane_copy(self, k, dy, dx):
        p = self.pl
        return self.remote(
            self.sbase[2], self.rbase[6], self.total.at[:, p.page(0, dy, dx), :, 0:self.low], self.rp.at[k], p.there(0, dy, dx))

    def begin(self, dz):
        self.core_copy(dz).start()

    def arrive(self, dz):
        self.core_copy(dz).wait_recv()

    def pair(self, page):
        return self.part[:, page, self.pl.c, :, self.low:].astype(F32) + self.total[:, page, :, self.low:].astype(F32)

    def corner(self, dz):
        p = self.pl
        for dy in range(1, p.ny):
            for dx in range(1, p.nx):
                page = p.page(dz, dy, dx)
                self.total[:, page, :, self.low:] = self.pair(page).astype(BF)
                self.xa_copy(dz, dy, dx).start()
                self.yb_copy(dz, dy, dx).start()

    def level_sum(self, level):
        p = self.pl
        pages, group = pl.ds(level, p.plane), level // p.plane
        total = self.part[:, pages, p.c, :, 0:self.low].astype(F32) + self.total[:, pages, :, 0:self.low].astype(F32)
        return total, pages, group

    def relay(self, d):
        p = self.pl
        if not self.low:
            return

        def step(up):
            total, pages, group = self.level_sum((p.z + d if up else p.z - d) * p.plane)
            self.total[:, pages, :, 0:self.low] = total.astype(BF)

            def add():
                self.relay_copy(group * p.plane, up).wait_recv()
                got = self.rr[0 if up else 1, group].astype(F32)
                self.total[:, pages, :, 0:self.low] = (total + got).astype(BF)

            pl.when(p.z > 0 if up else p.z < p.nz - 1)(add)
            self.relay_copy(group * p.plane, up).start()

        pl.when(p.z + d < p.nz)(lambda: step(True))
        pl.when(p.z >= d)(lambda: step(False))

    def settle(self):
        p = self.pl
        if not self.low:
            return
        total, pages, group = self.level_sum(p.level(0))
        self.total[:, pages, :, 0:self.low] = total.astype(BF)
        for way in range(2):
            def add(way=way):
                self.relay_copy(group * p.plane, way == 0).wait_recv()
                self.total[:, pages, :, 0:self.low] = (
                    self.total[:, pages, :, 0:self.low].astype(F32) + self.rr[way, group].astype(F32)).astype(BF)
            pl.when(p.z > 0 if way == 0 else p.z < p.nz - 1)(add)
        for k, (dy, dx) in enumerate(p.others):
            self.plane_copy(k, dy, dx).start()

    def owned(self):
        p = self.pl
        self.wait(self.rp, self.recv.at[self.rbase[6]])
        total = self.total[:, p.page(), :, 0:self.low].astype(F32)
        for k in range(len(p.others)):
            total += self.rp[k].astype(F32)
        return total

    def plane(self, dz):
        p = self.pl
        panels, rows = self.total.shape[0], self.total.shape[2]

        def with_half(total, add, which):
            axis, n = (0, panels // 2) if self.kind == PANELS else (1, rows // 2)
            first, second = (total[:n], total[n:]) if axis == 0 else (total[:, :n], total[:, n:])
            return jnp.concatenate([first + add, second] if which == 0 else [first, second + add], axis=axis)

        for dx in range(1, p.nx):
            page = p.page(dz, 0, dx)
            total = self.pair(page)
            for dy in range(1, p.ny):
                self.yb_copy(dz, dy, dx).wait_recv()
                total = with_half(total, self.db[self.corner_slot(dz, dy, dx)].astype(F32), 1)
            self.total[:, page, :, self.low:] = total.astype(BF)
            self.x_copy(dz, dx).start()
        for dy in range(1, p.ny):
            page = p.page(dz, dy, 0)
            total = self.pair(page)
            for dx in range(1, p.nx):
                self.xa_copy(dz, dy, dx).wait_recv()
                total = with_half(total, self.da[self.corner_slot(dz, dy, dx)].astype(F32), 0)
            self.total[:, page, :, self.low:] = total.astype(BF)
            self.y_copy(dz, dy).start()

    def column_sum(self, dz):
        p = self.pl
        total = self.pair(p.page(dz))
        for dx in range(1, p.nx):
            self.x_copy(dz, dx).wait_recv()
            total += self.rx[dz * (p.nx - 1) + dx - 1].astype(F32)
        for dy in range(1, p.ny):
            self.y_copy(dz, dy).wait_recv()
            total += self.ry[dz * (p.ny - 1) + dy - 1].astype(F32)
        return total

    def column(self, dz):
        self.total[:, self.pl.page(dz), :, self.low:] = self.column_sum(dz).astype(BF)
        self.z_copy(dz).start()

    def finish(self):
        total = self.column_sum(0)
        for dz in range(1, self.pl.nz):
            self.z_copy(dz).wait_recv()
            total += self.rz[dz - 1].astype(F32)
        return jnp.concatenate([self.owned(), total], axis=2) if self.low else total

    def drain(self):
        p = self.pl
        pages = p.nz * p.plane
        self.wait(self.part.at[:, :, 0], self.send.at[self.sbase[1]])
        self.wait(self.total.at[:, 0:pages - 1, :, self.low:], self.send.at[self.sbase[0]])
        if not self.low:
            return
        self.wait(self.rp, self.send.at[self.sbase[2]])

        def group(g):
            pl.when(g > p.z)(lambda: self.relay_copy(g * p.plane, True).wait_send())
            pl.when(g < p.z)(lambda: self.relay_copy(g * p.plane, False).wait_send())

        for g in range(p.nz):
            group(g)


def vector_scratch(pages, rows, width):
    nz, ny, nx = page_grid(pages)
    n = 1 + nx - 1 + ny - 1 + nz - 1
    return [VMEM((4, rows, width), F32), VMEM((n, rows, width), F32), DMA((n,)), DMA((n,))]


class VectorSum:
    def __init__(self, place, scratch):
        self.pl = place
        self.held, self.got, self.send, self.recv = scratch

    def legs(self):
        p = self.pl
        return [
            [p.sibling],
            [p.there(dx=d) for d in range(1, p.nx)],
            [p.there(dy=d) for d in range(1, p.ny)],
            [p.there(dz=d) for d in range(1, p.nz)],
        ]

    def copies(self, leg):
        legs = self.legs()
        at = sum(len(one) for one in legs[:leg])
        return [
            pltpu.make_async_remote_copy(
                src_ref=self.held.at[leg], dst_ref=self.got.at[at + i], send_sem=self.send.at[at + i],
                recv_sem=self.recv.at[at + i], device_id=target, device_id_type=MESH)
            for i, target in enumerate(legs[leg])
        ], at

    def put(self, leg, value):
        self.held[leg] = value
        for copy in self.copies(leg)[0]:
            copy.start()

    def take(self, leg):
        copies, at = self.copies(leg)
        value = self.held[leg]
        for i, copy in enumerate(copies):
            copy.wait_recv()
            value += self.got[at + i]
        return value

    def drain(self):
        for leg in range(4):
            for copy in self.copies(leg)[0]:
                copy.wait_send()


HEADS = 12


masked_value = -1e30
norm_eps = 1e-06


def layer_norm(values, norm_gain, norm_shift):
    centre = jnp.mean(values, axis=-1, keepdims=True)
    centered = values - centre
    spread = jnp.mean(centered * centered, axis=-1, keepdims=True)
    return centered * lax.rsqrt(spread + norm_eps) * norm_gain + norm_shift


def gelu_exact(values):
    return jax.nn.gelu(values, approximate=False)


def matmul(left_side, right_side):
    return jnp.dot(left_side, right_side, preferred_element_type=jnp.float32)


def column_sum(values):
    return jnp.sum(values.astype(jnp.float32), axis=0)


def usable_keys(page_lengths, seg_len):
    places = lax.broadcasted_iota(jnp.int32, (page_lengths.shape[0], seg_len), 1)
    return places < page_lengths[:, None]


def head_split(values, head_count):
    return values.reshape(
        values.shape[0], values.shape[1], head_count, values.shape[2] // head_count
    )


def page_scores(query_heads, key_piece, usable, score_scale):
    key_heads = head_split(key_piece, query_heads.shape[2])
    scores = (
        jnp.einsum("pqhd,pkhd->phqk", query_heads, key_heads, preferred_element_type=jnp.float32)
        * score_scale
    )
    return jnp.where(usable[:, None, None, :], scores, masked_value)


VECTORS = 8


def pack_vectors(vectors, inner):
    rows = [jnp.pad(v[None], ((j, 15 - j), (0, 128 - v.shape[0]))) for j, v in enumerate((*vectors, inner))]
    return functools.reduce(jnp.add, rows)


LOG2E = 1.4426950408889634
VEC_ROWS = 16
NT = ((1,), (1,))
TN = ((0,), (0,))


def steps_loop(count, body, steps):
    def one(i, _):
        body(i)
        for at, todo in steps.items():
            def run(todo=todo):
                for step in todo:
                    step()
            pl.when(i == at)(run)
        return 0

    lax.fori_loop(0, count, one, 0)


def dot(left, right, dims=((1,), (0,))):
    return lax.dot_general(left, right, (dims, ((), ())), preferred_element_type=F32)


def standardize(values):
    centered = values - jnp.mean(values, axis=-1, keepdims=True)
    r = lax.rsqrt(jnp.mean(centered * centered, axis=-1, keepdims=True) + norm_eps)
    return centered * r, r


def norm_back(grad, xhat, r, gain):
    e = grad * gain
    return r * (e - jnp.mean(e, axis=-1, keepdims=True) - xhat * jnp.mean(e * xhat, axis=-1, keepdims=True))


def add_row(ref, row, values):
    ref[row:row + 1, :] += jnp.sum(values, axis=0, keepdims=True)


def spread_lanes(small, n, width, first):
    devices, vectors, lanes = small.shape
    column = (first + lax.broadcasted_iota(jnp.int32, (lanes, width), 1)).astype(F32)
    owner = jnp.floor((column + 0.5) * (1.0 / n))
    lane = lax.broadcasted_iota(jnp.int32, (lanes, width), 0).astype(F32)
    pick = jnp.where(column - owner * n == lane, 1.0, 0.0).astype(BF)
    values = dot(small.reshape(devices * vectors, lanes), pick).reshape(devices, vectors, width)
    device = lax.broadcasted_iota(jnp.int32, (devices, vectors, width), 0).astype(F32)
    return jnp.sum(jnp.where(owner[:1][None] == device, values, 0.0), axis=0)


def layer_scratch(pages, rows, width, panels, tokens, local_pages):
    (_, gather_sends), (_, gather_recvs) = gather_slots(pages)
    seg = tokens // local_pages
    groups = width // (2 * LANES)
    own = dict(
        g_attn=VMEM((4, pages, 2, rows, width), BF),
        g_inner=VMEM((panels, pages, 2, rows, width), BF),
        g_outer=VMEM((1, pages, 2, panels * rows, width), BF),
        g_small=VMEM((1, pages, 2, VEC_ROWS, LANES), BF),
        p_output=VMEM((2, pages, 2, rows, width // 2), BF),
        p_groups=VMEM((groups, 6, pages, 2, rows, LANES), BF),
        xs=VMEM((tokens, width), BF),
        q=VMEM((tokens, width), BF),
        k=VMEM((local_pages, 2 * seg, width), BF),
        v=VMEM((local_pages, 2 * seg, width), BF),
        ctx=VMEM((tokens, width), BF),
        xhat=VMEM((tokens, width), F32),
        r_one=VMEM((tokens, 1), F32),
        low=VMEM((tokens, width), BF),
        post=VMEM((panels, tokens, width), BF),
        slope=VMEM((panels, tokens, width), BF),
        res=VMEM((tokens, width), F32),
        d_low=VMEM((tokens, width), BF),
        vec=VMEM((VEC_ROWS, width), F32),
        par=VMEM((VEC_ROWS, width), F32),
        rk=VMEM((local_pages, seg, width), BF),
        rv=VMEM((local_pages, seg, width), BF),
        x=VMEM((tokens, width), BF),
        cot=VMEM((tokens, width), BF),
        out=VMEM((tokens, width), BF),
        squares=VMEM((4, rows, width), F32),
        wide=VMEM((rows, panels * width), F32),
        tall=VMEM((panels * rows, width), F32),
        total=VMEM((VEC_ROWS, width), F32),
        in_sem=DMA((8 + panels,)),
        out_sem=DMA((9,)),
        x_sem=DMA((2,)),
        kv_sem=DMA((4, groups)),
    )
    gather = [DMA((gather_sends,)), DMA((gather_recvs,))] * 4
    reduce = []
    parts = [(1, panels * rows, width, ROWS, REDUCE_RELAY), (panels, rows, width, PANELS, REDUCE_RELAY)]
    parts += [(2, rows, width // 2, PANELS, 0)] + [(6, rows, LANES, PANELS, 0)] * groups
    for part in parts:
        reduce += reduce_scratch(pages, *part)
    return own, gather + reduce + vector_scratch(pages, VEC_ROWS, width)


def layer_kernel(pages, heads, names, lengths, x_in, cot_in, wq, wk, wv, wo, wi, wout, small,
                 layer_out, hidden_grad, o_q, o_k, o_v, o_o, o_inner, o_outer, o_vec, *scratch):
    s = types.SimpleNamespace(**dict(zip(names, scratch)))
    s.d_ctx, s.grad = s.xs, s.cot
    rest = scratch[len(names):]
    place = Place(pages)
    c, nz = place.c, place.nz
    mine = place.p, c
    sibling = place.sibling
    x, cot = s.x, s.cot
    tokens, width = x.shape
    panels, _, _, rows = s.g_inner.shape[:4]
    blocks = (pages, 2, rows, width)
    local_pages, page_len = s.k.shape[:2]
    seg = tokens // local_pages
    full = (width, width)
    scale = (width // heads) ** -0.5
    q, k, v, ctx, res, par, vec = s.q, s.k, s.v, s.ctx, s.res, s.par, s.vec

    arrived = place.signal()
    moves = [(x_in, x), (small, s.g_small.at[0, *mine])]
    moves += [(ref, s.g_attn.at[j, *mine]) for j, ref in enumerate((wq, wk, wv, wo))]
    moves += [(wi.at[:, j * width:(j + 1) * width], s.g_inner.at[j, *mine]) for j in range(panels)]
    moves += [(wout, s.g_outer.at[0, *mine]), (cot_in, cot)]
    moves = [pltpu.make_async_copy(src, dst, s.in_sem.at[i]) for i, (src, dst) in enumerate(moves)]
    for move in moves:
        move.start()
    for move in moves[:-1]:
        move.wait()
    arrived()

    def emit(i, src, dst):
        return pltpu.make_async_copy(src, dst, s.out_sem.at[i])

    results = [
        emit(i, src, dst) for i, (src, dst) in enumerate((
            (s.out, layer_out), (s.grad, hidden_grad), (s.squares.at[0], o_q), (s.squares.at[1], o_k), (s.squares.at[2], o_v),
            (s.squares.at[3], o_o), (s.wide, o_inner), (s.tall, o_outer), (s.total, o_vec)))]
    x_copy = pltpu.make_async_remote_copy(
        src_ref=x, dst_ref=s.xs, send_sem=s.x_sem.at[0], recv_sem=s.x_sem.at[1],
        device_id=sibling, device_id_type=MESH)
    x_copy.start()
    tiny, attn, inner, outer = (
        Gather(place, ref, rest[2 * i], rest[2 * i + 1], kind)
        for i, (ref, kind) in enumerate(((s.g_small, SMALL), (s.g_attn, PANELS), (s.g_inner, PANELS), (s.g_outer, ROWS))))
    first = (attn, tiny)
    for one in first:
        one.begin()
    for one in first:
        one.spread(0)
    for dz in range(1, nz):
        for one in first:
            one.column(dz)
    attn.rise()
    inner.begin()
    for dz in range(nz):
        for one in first:
            one.plane(dz)
    attn.relay(1)
    inner.spread(0)
    attn.relay(2)
    for dz in range(1, nz):
        inner.column(dz)
    attn.relay(3)
    inner.rise()
    for dz in range(nz):
        for one in first:
            one.corner(dz)
    outer.begin()
    for one in first:
        one.finish_core()
    x_copy.wait()

    def begin_all(one):
        for dz in range(nz):
            one.begin(dz)

    def corners(one):
        loop(0, one.arrive)
        loop(0, one.corner)

    def weight(ref, j):
        return ref[j].reshape(full)

    def loop(start, body):
        def one(dz, _):
            body(dz)
            return 0
        lax.fori_loop(start, nz, one, 0)

    def outer_weight(j):
        n = pages // panels
        return s.g_outer[0, pl.ds(j * n, n)].reshape(full)

    gathered = s.g_small[0].reshape(2 * pages, VEC_ROWS, LANES)
    par[...] = spread_lanes(gathered, rows, width, 0)
    for j in range(panels):
        par[VECTORS + j:VECTORS + j + 1, :] = spread_lanes(gathered, panels * rows, width, j * width)[VECTORS:VECTORS + 1]
    vec[...] = jnp.zeros_like(vec)

    def vector(j):
        return par[j:j + 1, :]

    q[...] = (dot(x[...], weight(s.g_attn, 0)) + vector(0)).astype(BF)
    inner.plane(0)

    def project(i, _):
        ref, half = (x, c) if i == 0 else (s.xs, 1 - c)
        rows_of = pl.ds(pl.multiple_of(half * seg, seg), seg)
        k[:, rows_of, :] = dot(ref[...], weight(s.g_attn, 1)).astype(BF).reshape(local_pages, seg, width)
        v[:, rows_of, :] = (dot(ref[...], weight(s.g_attn, 2)) + vector(1)).astype(BF).reshape(local_pages, seg, width)

    project(0, 0)
    inner.plane(1)
    project(1, 0)
    inner.plane(2)

    pairs = heads // 2
    head_dim = width // heads

    def place_of(i):
        page, pair = i // pairs, lax.rem(i, pairs)
        return page, pl.ds(pl.multiple_of(page * seg, seg), seg), pl.ds(pl.multiple_of(pair * LANES, LANES), LANES)

    low_half = lax.broadcasted_iota(jnp.int32, (1, LANES), 1) < head_dim
    key_at = lax.broadcasted_iota(jnp.int32, (1, page_len), 1)

    def one_head(values, head):
        return jnp.where(low_half if head == 0 else jnp.logical_not(low_half), values, jnp.zeros_like(values))

    def probabilities(q2, k2, head, usable):
        t = jnp.where(usable, dot(q2, one_head(k2, head), NT) * (scale * LOG2E), masked_value)
        e = jnp.exp2(t - jnp.max(t, axis=-1, keepdims=True))
        return e * (1.0 / jnp.sum(e, axis=-1, keepdims=True))

    def attend(i):
        page, rows_of, cols = place_of(i)
        q2, k2, v2 = q[rows_of, cols], k[page, :, cols], v[page, :, cols]
        usable = key_at < lengths[page]
        parts = [dot(probabilities(q2, k2, head, usable).astype(BF), v2) for head in range(2)]
        ctx[rows_of, cols] = jnp.where(low_half, *parts).astype(BF)

    steps_loop(local_pages * pairs, attend, {
        0: [lambda: inner.plane(3), lambda: inner.relay(1), lambda: outer.spread(0)],
        1: [lambda: outer.column(1), lambda: inner.relay(2)],
        2: [lambda: outer.column(2), outer.rise],
        3: [lambda: outer.column(3), lambda: inner.relay(3)],
        4: [lambda: inner.corner(0)],
        5: [lambda: inner.corner(1)],
        6: [lambda: inner.corner(2), lambda: outer.relay(1)],
        7: [lambda: inner.corner(3)],
        8: [lambda: outer.plane(0), lambda: outer.relay(2)],
        9: [lambda: outer.plane(1)],
        10: [lambda: outer.plane(2), lambda: outer.relay(3)],
        11: [lambda: outer.plane(3)],
    })

    res[...] = dot(ctx[...], weight(s.g_attn, 3))
    chunk = 128

    def chunks(body):
        def one(i, _):
            body(pl.ds(pl.multiple_of(i * chunk, chunk), chunk))
            return 0
        lax.fori_loop(0, tokens // chunk, one, 0)

    def norm_one(at):
        xhat, r = standardize(x[at, :].astype(F32) + res[at, :] + vector(2))
        s.xhat[at, :] = xhat
        s.r_one[at, :] = r
        normed = xhat * vector(3) + vector(4)
        s.low[at, :] = normed.astype(BF)
        res[at, :] = normed + vector(5)

    chunks(norm_one)

    inner.finish_core()
    root_half = 0.7071067811865476

    def expand(j):
        pre = dot(s.low[...], weight(s.g_inner, j)) + par[pl.ds(VECTORS + j, 1), :]
        half_one = 0.5 * (1.0 + lax.erf(pre * root_half))
        bell = jnp.exp2(pre * pre * (-0.5 * LOG2E)) * 0.3989422804014327
        s.post[j] = (pre * half_one).astype(BF)
        s.slope[j] = (half_one + pre * bell).astype(BF)

    steps_loop(panels, expand, {j: [lambda j=j: outer.corner(j)] for j in range(nz)})
    outer.finish_core()

    def contract(j, _):
        res[...] += dot(s.post[j], outer_weight(j))
        return 0

    lax.fori_loop(0, panels, contract, 0)

    def norm_two(at):
        xhat, r = standardize(res[at, :])
        s.out[at, :] = (xhat * vector(6) + vector(7)).astype(BF)
        grad = cot[at, :].astype(F32)
        add_row(vec, 6, grad * xhat)
        add_row(vec, 7, grad)
        d_res = norm_back(grad, xhat, r, vector(6))
        res[at, :] = d_res
        d_low = d_res.astype(BF)
        s.d_low[at, :] = d_low
        add_row(vec, 5, d_low.astype(F32))

    moves[-1].wait()
    chunks(norm_two)
    results[0].start()

    parts = [(s.g_outer, ROWS, REDUCE_RELAY), (s.g_inner, PANELS, REDUCE_RELAY), (s.p_output, PANELS, 0)]
    parts += [(s.p_groups.at[g], PANELS, 0) for g in range(s.p_groups.shape[0])]
    reducers = [
        Reduce(place, part, rest[8 + REDUCE_REFS * i:8 + REDUCE_REFS * (i + 1)], kind, low)
        for i, (part, kind, low) in enumerate(parts)]
    r_outer, r_inner, r_output, *r_groups = reducers
    outer.drain()

    def outer_back(dz):
        j = lax.rem(place.z + dz, nz)
        d_low = s.d_low[...]
        d_pre = (dot(d_low, outer_weight(j), NT) * s.slope[j].astype(F32)).astype(BF)
        n = pages // panels
        s.g_outer[0, pl.ds(j * n, n)] = dot(s.post[j], d_low, TN).reshape(n, 2, panels * rows, width).astype(BF)
        r_outer.begin(dz)
        s.slope[j] = d_pre
        vec[pl.ds(VECTORS + j, 1), :] = jnp.sum(d_pre.astype(F32), axis=0, keepdims=True)

    steps_loop(nz, outer_back, {
        1: [lambda: r_outer.arrive(0), lambda: r_outer.corner(0)],
        2: [lambda: r_outer.arrive(1), lambda: r_outer.corner(1)],
        3: [lambda: r_outer.arrive(2), lambda: r_outer.corner(2)],
    })
    inner.drain()

    def inner_back(j):
        d_pre = s.slope[j]
        res[...] += dot(d_pre, weight(s.g_inner, j), NT)
        s.g_inner[j] = dot(s.low[...], d_pre, TN).reshape(blocks).astype(BF)

    steps_loop(panels, inner_back, {
        0: [lambda: r_outer.arrive(3), lambda: r_outer.corner(3), lambda: r_outer.plane(0), lambda: r_outer.relay(3)],
        1: [lambda: r_outer.plane(1)],
        2: [lambda: r_outer.plane(2), lambda: r_outer.relay(2)],
        3: [lambda: r_outer.plane(3)],
    })
    begin_all(r_inner)

    def norm_one_back(at):
        grad, xhat = res[at, :], s.xhat[at, :]
        add_row(vec, 3, grad * xhat)
        add_row(vec, 4, grad)
        d_res = norm_back(grad, xhat, s.r_one[at, :], vector(3))
        res[at, :] = d_res
        d_low = d_res.astype(BF)
        s.d_low[at, :] = d_low
        add_row(vec, 2, d_low.astype(F32))

    chunks(norm_one_back)
    s.d_ctx[...] = dot(s.d_low[...], weight(s.g_attn, 3), NT).astype(BF)
    grad = dot(ctx[...], s.d_low[...], TN).reshape(blocks)
    half = width // 2
    for j in range(2):
        s.p_output[j] = grad[..., j * half:(j + 1) * half].astype(BF)
    begin_all(r_output)
    r_outer.relay(1)
    r_inner.arrive(0)
    r_inner.corner(0)
    r_inner.arrive(3)
    r_inner.corner(3)
    r_inner.arrive(1)
    r_inner.corner(1)
    r_inner.arrive(2)
    r_inner.corner(2)
    r_inner.relay(3)

    d_q, d_k, d_v = s.post.at[0], s.post.at[1:1 + local_pages], s.slope.at[0:local_pages]

    def kv_copies(g):
        theirs = pl.ds(pl.multiple_of((1 - c) * seg, seg), seg)
        cols = slice(2 * LANES * g, 2 * LANES * (g + 1))
        return [
            pltpu.make_async_remote_copy(
                src_ref=grad.at[:, theirs, cols], dst_ref=got.at[:, :, cols], send_sem=s.kv_sem.at[2 * n, g],
                recv_sem=s.kv_sem.at[2 * n + 1, g], device_id=sibling, device_id_type=MESH)
            for n, (grad, got) in enumerate(((d_k, s.rk), (d_v, s.rv)))]

    def exchange(g):
        for copy in kv_copies(g):
            copy.start()

    def group_grads(g):
        cols = slice(2 * LANES * g, 2 * LANES * (g + 1))
        for copy in kv_copies(g):
            copy.wait_recv()
        ours = pl.ds(pl.multiple_of(c * seg, seg), seg)
        for j in range(3):
            if j == 0:
                total = d_q[:, cols]
            else:
                mine_k, got = ((d_k, s.rk), (d_v, s.rv))[j - 1]
                total = (mine_k[:, ours, cols].astype(F32) + got[:, :, cols].astype(F32)).astype(BF)
                got[:, :, cols] = total
                total = total.reshape(tokens, 2 * LANES)
            if j != 1:
                vec[j // 2:j // 2 + 1, cols] = jnp.sum(total.astype(F32), axis=0, keepdims=True)
            grad = dot(x[...], total, TN).reshape(pages, 2, rows, 2 * LANES)
            for n in range(2):
                s.p_groups[g, 2 * j + n] = grad[..., n * LANES:(n + 1) * LANES].astype(BF)
        for dz in range(nz):
            r_groups[g].begin(dz)

    def attend_back(i):
        page, rows_of, cols = place_of(lax.rem(i, local_pages) * pairs + i // local_pages)
        q2, k2, v2 = q[rows_of, cols], k[page, :, cols], v[page, :, cols]
        c2 = s.d_ctx[rows_of, cols]
        usable = key_at < lengths[page]
        found = []
        for head in range(2):
            p = probabilities(q2, k2, head, usable)
            d_p = dot(c2, one_head(v2, head), NT)
            d_s = (p * (d_p - jnp.sum(p * d_p, axis=-1, keepdims=True))).astype(BF)
            found.append((dot(d_s, k2), dot(d_s, q2, TN), dot(p.astype(BF), c2, TN)))
        both = [jnp.where(low_half, one, two) for one, two in zip(*found)]
        d_q[rows_of, cols] = (both[0] * scale).astype(BF)
        d_k[page, :, cols] = (both[1] * scale).astype(BF)
        d_v[page, :, cols] = both[2].astype(BF)

    def finish_outer():
        s.tall[...] = r_outer.finish()[0]
        results[7].start()

    def finish_inner():
        total = r_inner.finish()
        for j in range(panels):
            s.wide[:, j * width:(j + 1) * width] = total[j]
        results[6].start()

    def finish_output():
        total = r_output.finish()
        for j in range(2):
            s.squares[3, :, j * half:(j + 1) * half] = total[j]
        results[5].start()

    def finish_group(g):
        total = r_groups[g].finish()
        for j in range(3):
            for n in range(2):
                at = (2 * g + n) * LANES
                s.squares[j, :, at:at + LANES] = total[2 * j + n]

    vectors = VectorSum(place, rest[8 + len(reducers) * REDUCE_REFS:])
    steps_loop(local_pages * pairs, attend_back, {
        0: [lambda: r_outer.column(1)],
        1: [lambda: r_outer.column(2), lambda: r_outer.column(3), lambda: r_outer.settle()],
        2: [lambda: corners(r_output)],
        3: [lambda: r_inner.plane(0), lambda: exchange(0)],
        4: [lambda: r_inner.relay(2), lambda: r_inner.plane(1)],
        5: [lambda: finish_outer(), lambda: r_inner.plane(2), lambda: r_inner.plane(3), lambda: group_grads(0)],
        6: [lambda: r_inner.relay(1), lambda: loop(0, r_output.plane)],
        7: [lambda: exchange(1), lambda: corners(r_groups[0])],
        8: [lambda: r_inner.column(1), lambda: r_inner.column(2), lambda: r_inner.column(3)],
        9: [lambda: r_inner.settle(), lambda: group_grads(1)],
        10: [lambda: loop(0, r_groups[0].plane)],
        11: [lambda: exchange(2), lambda: corners(r_groups[1])],
    })
    loop(1, r_output.column)
    res[...] += dot(d_q[...], weight(s.g_attn, 0), NT)
    group_grads(2)
    vectors.put(0, vec[...])
    loop(0, r_groups[1].plane)
    loop(1, r_groups[0].column)
    corners(r_groups[2])
    vectors.put(1, vectors.take(0))
    res[...] += dot(s.rk[...].reshape(tokens, width), weight(s.g_attn, 1), NT)
    vectors.put(2, vectors.take(1))
    loop(0, r_groups[2].plane)
    loop(1, r_groups[1].column)
    s.grad[...] = (res[...] + dot(s.rv[...].reshape(tokens, width), weight(s.g_attn, 2), NT)).astype(BF)
    results[1].start()
    vectors.put(3, vectors.take(2))
    finish_inner()
    finish_output()
    loop(1, r_groups[2].column)
    finish_group(1)
    finish_group(2)
    finish_group(0)
    s.total[...] = vectors.take(3)
    results[8].start()
    for i in (2, 3, 4):
        results[i].start()
    tiny.drain()
    attn.drain()
    for one in reducers:
        one.drain()
    vectors.drain()
    for g in range(len(r_groups)):
        for copy in kv_copies(g):
            copy.wait_send()
    for result in results:
        result.wait()


def finish_kernel(rows, panels, out, grad, g_q, g_k, g_v, g_o, g_inner, g_outer, total, *refs):
    outs, owned, held, sems = refs[:8], refs[8:8 + VECTORS + 1], refs[8 + VECTORS + 1:-1], refs[-1]
    copies = [
        (pltpu.make_async_copy(src, way, sems.at[i, 0]), pltpu.make_async_copy(way, dst, sems.at[i, 1]))
        for i, (src, way, dst) in enumerate(zip((out, grad, g_q, g_k, g_v, g_o, g_inner, g_outer), held, outs))]
    for copy, _ in copies:
        copy.start()
    for copy, onward in copies:
        copy.wait()
        onward.start()
    at = lax.axis_index(PAGE) * 2 + lax.axis_index(SEQ)
    width = total.shape[1]
    mine = pltpu.roll(total[0:VECTORS, :], width - rows * at, 1)
    for j, ref in enumerate(owned[:VECTORS]):
        ref[...] = mine[j, :rows]
    per_row = width // (panels * rows)
    row = total[pl.ds(VECTORS + at // per_row, 1), :]
    mine = pltpu.roll(row, width - panels * rows * lax.rem(at, per_row), 1)
    owned[VECTORS][...] = mine[0, :panels * rows]
    for _, onward in copies:
        onward.wait()


def finish(rows, panels, arrays):
    hbm, vm = pl.BlockSpec(memory_space=pl.ANY), pl.BlockSpec(memory_space=VMEM)
    return pl.pallas_call(
        functools.partial(finish_kernel, rows, panels),
        name="finish",
        out_shape=tuple(jax.ShapeDtypeStruct(a.shape, a.dtype) for a in arrays[:8])
        + (jax.ShapeDtypeStruct((rows,), F32),) * VECTORS + (jax.ShapeDtypeStruct((panels * rows,), F32),),
        in_specs=[hbm] * 8 + [vm],
        out_specs=(hbm,) * 8 + (vm,) * (VECTORS + 1),
        scratch_shapes=[VMEM(a.shape, a.dtype) for a in arrays[:8]] + [DMA((8, 2))],
    )(*arrays)


def whole_layer(pages, heads, lengths, x, cot, wq, wk, wv, wo, wi, wout, small, local_pages):
    tokens, width = x.shape
    rows, panels = wq.shape[0], wi.shape[1] // width
    own, scratch = layer_scratch(pages, rows, width, panels, tokens, local_pages)
    hbm = pl.BlockSpec(memory_space=pl.ANY)
    row_shape = jax.ShapeDtypeStruct((tokens, width), BF)
    square = jax.ShapeDtypeStruct((rows, width), F32)
    return pl.pallas_call(
        functools.partial(layer_kernel, pages, heads, tuple(own)),
        name="whole_layer",
        out_shape=(row_shape, row_shape, square, square, square, square,
                   jax.ShapeDtypeStruct((rows, panels * width), F32),
                   jax.ShapeDtypeStruct((panels * rows, width), F32),
                   jax.ShapeDtypeStruct((VEC_ROWS, width), F32)),
        in_specs=[pl.BlockSpec(memory_space=pltpu.SMEM)] + [hbm] * 9,
        out_specs=(hbm,) * 9,
        scratch_shapes=[*own.values(), *scratch],
        compiler_params=pltpu.CompilerParams(collective_id=0, has_side_effects=True, vmem_limit_bytes=61 << 20),
    )(lengths, x, cot, wq, wk, wv, wo, wi, wout, small)


def plain_layer(
    hidden,
    lengths,
    w_query,
    w_key,
    w_value,
    w_output,
    b_query,
    b_value,
    b_output,
    attn_gain,
    attn_shift,
    w_inner,
    b_inner,
    w_outer,
    b_outer,
    ffn_gain,
    ffn_shift,
    cotangent,
):
    model_width = hidden.shape[2]
    head_count = HEADS
    score_scale = (model_width // head_count) ** (-0.5)
    f32 = jnp.float32
    bf16 = jnp.bfloat16
    work_hidden, work_cot = (hidden, cotangent)
    local_pages, local_tokens = (work_hidden.shape[0], work_hidden.shape[1])
    row_count = local_pages * local_tokens
    (
        query_full,
        key_full,
        value_full,
        output_full,
        query_bias,
        value_bias,
        output_bias,
        gain_one,
        shift_one,
    ) = (
        lax.all_gather(w_query, AXES, axis=0, tiled=True),
        lax.all_gather(w_key, AXES, axis=0, tiled=True),
        lax.all_gather(w_value, AXES, axis=0, tiled=True),
        lax.all_gather(w_output, AXES, axis=0, tiled=True),
        lax.all_gather(b_query, AXES, axis=0, tiled=True),
        lax.all_gather(b_value, AXES, axis=0, tiled=True),
        lax.all_gather(b_output, AXES, axis=0, tiled=True),
        lax.all_gather(attn_gain, AXES, axis=0, tiled=True),
        lax.all_gather(attn_shift, AXES, axis=0, tiled=True),
    )
    flat_rows = work_hidden.reshape(row_count, model_width)
    queries = (matmul(flat_rows, query_full) + query_bias.astype(f32)).astype(bf16)
    key_rows = matmul(flat_rows, key_full).astype(bf16)
    value_rows = (matmul(flat_rows, value_full) + value_bias.astype(f32)).astype(bf16)
    query_heads = head_split(queries.reshape(local_pages, local_tokens, model_width), head_count)
    key_pages = key_rows.reshape(local_pages, local_tokens, model_width)
    value_pages = value_rows.reshape(local_pages, local_tokens, model_width)
    stat_shape = (local_pages, head_count, local_tokens)
    stat_start = (jnp.full(stat_shape, masked_value, f32), jnp.zeros(stat_shape, f32))
    key_piece = lax.all_gather(key_pages, SEQ, axis=1, tiled=True)
    usable = usable_keys(lengths, key_piece.shape[1])

    def merged():
        run_peak, run_total = stat_start
        scores = page_scores(query_heads, key_piece, usable, score_scale)
        new_peak = jnp.maximum(run_peak, jnp.max(scores, axis=-1))
        summed = jnp.sum(jnp.exp(scores - new_peak[..., None]), axis=-1)
        return (new_peak, summed)

    run_peak, run_total = merged()
    log_norm = run_peak + jnp.log(run_total)
    add_key_piece = lax.all_gather(key_pages, SEQ, axis=1, tiled=True)
    value_piece = lax.all_gather(value_pages, SEQ, axis=1, tiled=True)
    add_usable = usable_keys(lengths, add_key_piece.shape[1])

    def merged():
        scores = page_scores(query_heads, add_key_piece, add_usable, score_scale)
        attn_probs = jnp.exp(scores - log_norm[..., None]).astype(bf16)
        addend = jnp.einsum(
            "phqk,pkhd->pqhd",
            attn_probs,
            head_split(value_piece, head_count),
            preferred_element_type=f32,
        )
        return addend.reshape(local_pages, local_tokens, model_width)

    context = merged()
    context_low = context.astype(bf16).reshape(row_count, model_width)
    residual_one = (
        flat_rows.astype(f32) + matmul(context_low, output_full) + output_bias.astype(f32)
    )
    normed_one, pull_one = jax.vjp(
        layer_norm, residual_one, gain_one.astype(f32), shift_one.astype(f32)
    )
    inner_full, outer_full, inner_bias, outer_bias, gain_two, shift_two = (
        lax.all_gather(w_inner, AXES, axis=0, tiled=True),
        lax.all_gather(w_outer, AXES, axis=0, tiled=True),
        lax.all_gather(b_inner, AXES, axis=0, tiled=True),
        lax.all_gather(b_outer, AXES, axis=0, tiled=True),
        lax.all_gather(ffn_gain, AXES, axis=0, tiled=True),
        lax.all_gather(ffn_shift, AXES, axis=0, tiled=True),
    )
    normed_low = normed_one.astype(bf16)
    pre_gelu = matmul(normed_low, inner_full) + inner_bias.astype(f32)
    post_gelu, pull_gelu = jax.vjp(gelu_exact, pre_gelu)
    post_low = post_gelu.astype(bf16)
    residual_two = normed_one + matmul(post_low, outer_full) + outer_bias.astype(f32)
    layer_out, pull_two = jax.vjp(
        layer_norm, residual_two, gain_two.astype(f32), shift_two.astype(f32)
    )
    cot_rows = work_cot.reshape(row_count, model_width).astype(f32)
    d_res_two, gain_two_grad, shift_two_grad = pull_two(cot_rows)
    d_outer = d_res_two.astype(bf16)
    outer_w_grad = matmul(post_low.T, d_outer)
    outer_b_grad = column_sum(d_outer)
    (d_pre_full,) = pull_gelu(matmul(d_outer, outer_full.T))
    d_pre = d_pre_full.astype(bf16)
    inner_w_grad = matmul(normed_low.T, d_pre)
    inner_b_grad = column_sum(d_pre)
    d_normed = d_res_two + matmul(d_pre, inner_full.T)
    d_res_one, gain_one_grad, shift_one_grad = pull_one(d_normed)
    ffn_owned = (
        lax.psum_scatter(inner_w_grad, AXES, scatter_dimension=0, tiled=True),
        lax.psum_scatter(outer_w_grad, AXES, scatter_dimension=0, tiled=True),
        lax.psum_scatter(inner_b_grad, AXES, scatter_dimension=0, tiled=True),
        lax.psum_scatter(outer_b_grad, AXES, scatter_dimension=0, tiled=True),
        lax.psum_scatter(gain_two_grad, AXES, scatter_dimension=0, tiled=True),
        lax.psum_scatter(shift_two_grad, AXES, scatter_dimension=0, tiled=True),
    )
    d_attn = d_res_one.astype(bf16)
    output_w_grad = matmul(context_low.T, d_attn)
    output_b_grad = column_sum(d_attn)
    d_context = matmul(d_attn, output_full.T).astype(bf16)
    d_context_heads = head_split(
        d_context.reshape(local_pages, local_tokens, model_width), head_count
    )
    context_heads = head_split(context, head_count)
    row_delta = jnp.transpose(
        jnp.sum(d_context_heads.astype(f32) * context_heads, axis=-1), (0, 2, 1)
    )

    def add_grads(segment):
        key_piece, value_piece = segment
        seg_len = key_piece.shape[1]
        usable = usable_keys(lengths, seg_len)

        def merged():
            scores = page_scores(query_heads, key_piece, usable, score_scale)
            attn_probs = jnp.exp(scores - log_norm[..., None])
            key_heads = head_split(key_piece, head_count)
            value_heads = head_split(value_piece, head_count)
            d_probs = jnp.einsum(
                "pqhd,pkhd->phqk", d_context_heads, value_heads, preferred_element_type=f32
            )
            d_scores = (attn_probs * (d_probs - row_delta[..., None])).astype(bf16)
            query_part = jnp.einsum(
                "phqk,pkhd->pqhd", d_scores, key_heads, preferred_element_type=f32
            )
            key_part = jnp.einsum(
                "phqk,pqhd->pkhd", d_scores, query_heads, preferred_element_type=f32
            )
            value_part = jnp.einsum(
                "phqk,pqhd->pkhd",
                attn_probs.astype(bf16),
                d_context_heads,
                preferred_element_type=f32,
            )
            query_grad = query_part.reshape(local_pages, local_tokens, model_width) * score_scale
            key_grads = key_part.reshape(local_pages, seg_len, model_width) * score_scale
            value_grads = value_part.reshape(local_pages, seg_len, model_width)
            return (query_grad, key_grads, value_grads)

        return merged()

    query_grad, key_grads, value_grads = add_grads(
        (
            lax.all_gather(key_pages, SEQ, axis=1, tiled=True),
            lax.all_gather(value_pages, SEQ, axis=1, tiled=True),
        )
    )
    key_owned, value_owned = (
        lax.psum_scatter(
            key_grads.astype(jnp.bfloat16), SEQ, scatter_dimension=1, tiled=True
        ).astype(jnp.float32),
        lax.psum_scatter(
            value_grads.astype(jnp.bfloat16), SEQ, scatter_dimension=1, tiled=True
        ).astype(jnp.float32),
    )
    d_queries = query_grad.astype(bf16).reshape(row_count, model_width)
    d_keys = key_owned.astype(bf16).reshape(row_count, model_width)
    d_values = value_owned.astype(bf16).reshape(row_count, model_width)
    query_w_grad = matmul(flat_rows.T, d_queries)
    key_w_grad = matmul(flat_rows.T, d_keys)
    value_w_grad = matmul(flat_rows.T, d_values)
    query_b_grad = column_sum(d_queries)
    value_b_grad = column_sum(d_values)
    hidden_grad = (
        d_res_one
        + matmul(d_queries, query_full.T)
        + matmul(d_keys, key_full.T)
        + matmul(d_values, value_full.T)
    ).astype(bf16)
    attn_owned = (
        lax.psum_scatter(query_w_grad, AXES, scatter_dimension=0, tiled=True),
        lax.psum_scatter(key_w_grad, AXES, scatter_dimension=0, tiled=True),
        lax.psum_scatter(value_w_grad, AXES, scatter_dimension=0, tiled=True),
        lax.psum_scatter(output_w_grad, AXES, scatter_dimension=0, tiled=True),
        lax.psum_scatter(query_b_grad, AXES, scatter_dimension=0, tiled=True),
        lax.psum_scatter(value_b_grad, AXES, scatter_dimension=0, tiled=True),
        lax.psum_scatter(output_b_grad, AXES, scatter_dimension=0, tiled=True),
        lax.psum_scatter(gain_one_grad, AXES, scatter_dimension=0, tiled=True),
        lax.psum_scatter(shift_one_grad, AXES, scatter_dimension=0, tiled=True),
    )
    out_pages = layer_out.astype(bf16).reshape(local_pages, local_tokens, model_width)
    grad_pages = hidden_grad.reshape(local_pages, local_tokens, model_width)
    return (
        out_pages,
        grad_pages,
        attn_owned[0],
        attn_owned[1],
        attn_owned[2],
        attn_owned[3],
        attn_owned[4],
        attn_owned[5],
        attn_owned[6],
        attn_owned[7],
        attn_owned[8],
        ffn_owned[0],
        ffn_owned[2],
        ffn_owned[1],
        ffn_owned[3],
        ffn_owned[4],
        ffn_owned[5],
    )


def per_device(pages, hidden, lengths, w_query, w_key, w_value, w_output, b_query, b_value, b_output, attn_gain, attn_shift,
               w_inner, b_inner, w_outer, b_outer, ffn_gain, ffn_shift, cotangent):
    local_pages, seg, width = hidden.shape
    rows, panels = w_query.shape[0], w_inner.shape[1] // width
    nz, _, _ = page_grid(pages)
    if rows % 8 or nz != panels or local_pages * seg != 2 * seg or 4 * rows > 128:
        return plain_layer(hidden, lengths, w_query, w_key, w_value, w_output, b_query, b_value, b_output, attn_gain, attn_shift,
                           w_inner, b_inner, w_outer, b_outer, ffn_gain, ffn_shift, cotangent)
    small = pack_vectors((b_query, b_value, b_output, attn_gain, attn_shift, b_outer, ffn_gain, ffn_shift), b_inner)
    flat = local_pages * seg, width
    arrays = whole_layer(
        pages, HEADS, lengths, hidden.reshape(flat), cotangent.reshape(flat), w_query, w_key, w_value, w_output, w_inner, w_outer,
        small, local_pages)
    out, grad, g_q, g_k, g_v, g_o, g_inner, g_outer, *own = finish(rows, panels, arrays)
    return (out.reshape(hidden.shape), grad.reshape(hidden.shape), g_q, g_k, g_v, g_o, own[0], own[1], own[2], own[3], own[4],
            g_inner, own[8], g_outer, own[5], own[6], own[7])


def solution(mesh):
    in_specs = (
        P(PAGE, SEQ, None),
        P(PAGE),
        P(AXES, None),
        P(AXES, None),
        P(AXES, None),
        P(AXES, None),
        P(AXES),
        P(AXES),
        P(AXES),
        P(AXES),
        P(AXES),
        P(AXES, None),
        P(AXES),
        P(AXES, None),
        P(AXES),
        P(AXES),
        P(AXES),
        P(PAGE, SEQ, None),
    )
    out_specs = (
        P(PAGE, SEQ, None),
        P(PAGE, SEQ, None),
        P(AXES, None),
        P(AXES, None),
        P(AXES, None),
        P(AXES, None),
        P(AXES),
        P(AXES),
        P(AXES),
        P(AXES),
        P(AXES),
        P(AXES, None),
        P(AXES),
        P(AXES, None),
        P(AXES),
        P(AXES),
        P(AXES),
    )
    return jax.shard_map(
        functools.partial(per_device, mesh.shape[PAGE]), mesh=mesh, in_specs=in_specs, out_specs=out_specs, check_vma=False
    )
```

```python
import functools
import types
import jax
import jax.numpy as jnp
from jax import lax
from jax.experimental import pallas as pl
from jax.experimental.pallas import tpu as pltpu

from jax.sharding import PartitionSpec as P

MESH = pl.DeviceIdType.MESH
VMEM = pltpu.VMEM
DMA = pltpu.SemaphoreType.DMA
BF = jnp.bfloat16
F32 = jnp.float32
LANES = 128
AXES = PAGE, SEQ = ("page", "seq")
SMALL, PANELS, ROWS = range(3)
SPREAD_RELAY = 128
REDUCE_RELAY = 128


def page_grid(pages):
    bits = pages.bit_length() - 1
    nx = 2 ** (bits // 3)
    ny = 2 ** ((bits - bits // 3) // 2)
    return pages // (nx * ny), ny, nx


class Place:
    def __init__(self, pages):
        self.nz, self.ny, self.nx = page_grid(pages)
        self.plane = self.ny * self.nx
        self.p = lax.axis_index(PAGE)
        self.c = lax.axis_index(SEQ)
        self.x = lax.rem(self.p, self.nx)
        self.y = lax.rem(self.p // self.nx, self.ny)
        self.z = self.p // self.plane
        self.sibling = (self.p, 1 - self.c)
        ys = [lax.rem(self.y + d, self.ny) * self.nx for d in range(self.ny)]
        xs = [lax.rem(self.x + d, self.nx) for d in range(self.nx)]
        self.levels = [lax.rem(self.z + d, self.nz) * self.plane for d in range(self.nz)]
        self.pages = [[[level + y + x for x in xs] for y in ys] for level in self.levels]
        self.others = [(dy, dx) for dy in range(self.ny) for dx in range(self.nx) if dy or dx]

    def page(self, dz=0, dy=0, dx=0):
        return self.pages[dz % self.nz][dy % self.ny][dx % self.nx]

    def level(self, dz):
        return self.levels[dz % self.nz]

    def there(self, dz=0, dy=0, dx=0):
        return self.page(dz, dy, dx), self.c

    def signal(self):
        barrier = pltpu.get_barrier_semaphore()
        partners = [self.there(dz=d) for d in range(1, self.nz)] + [self.there(0, *d) for d in self.others] + [self.sibling]
        for partner in partners:
            pl.semaphore_signal(barrier, inc=1, device_id=partner, device_id_type=MESH)
        return lambda: pl.semaphore_wait(barrier, len(partners))


def slots(sizes):
    base, at = [], 0
    for size in sizes:
        base.append(at)
        at += size
    return base, at


def gather_slots(pages):
    nz, ny, nx = page_grid(pages)
    return slots((1, 1, 1, nz, nz)), slots((nz - 1, nz * (nx - 1), nz * (ny - 1), nz * (nx - 1) * (ny - 1), 1, nz, 1))


class Gather:
    def __init__(self, place, ref, send, recv, kind):
        self.pl, self.ref, self.send, self.recv, self.kind = place, ref, send, recv, kind
        (self.sbase, _), (self.rbase, _) = gather_slots(place.nz * place.plane)
        self.low = 0 if kind == SMALL else SPREAD_RELAY

    def view(self, page, part, core=None, count=None):
        ref, low = self.ref, self.low
        core = self.pl.c if core is None else core
        pages = page if count is None else pl.ds(page, count)
        if part == 3:
            return ref.at[:, pages, core, :, 0:low]
        if part == 4:
            return ref.at[:, pages, core]
        if part == 0 or self.kind == SMALL:
            return ref.at[:, pages, core, :, low:]
        if self.kind == PANELS:
            n = ref.shape[0] // 2
            return ref.at[(part - 1) * n:part * n, pages, core, :, low:]
        n = ref.shape[3] // 2
        return ref.at[:, pages, core, (part - 1) * n:part * n, low:]

    def copy(self, view, send, recv, target):
        return pltpu.make_async_remote_copy(
            src_ref=view, dst_ref=view, send_sem=self.send.at[send], recv_sem=self.recv.at[recv],
            device_id=target, device_id_type=MESH)

    def plain(self, group, slot, page, part, target):
        return self.copy(self.view(page, part), self.sbase[0], self.rbase[group] + slot, target)

    def corner_slot(self, dx, dy, dz):
        return (dz * (self.pl.ny - 1) + dy - 1) * (self.pl.nx - 1) + dx - 1

    def z_copy(self, dz, mine):
        p = self.pl
        return self.plain(0, dz - 1, p.page(0 if mine else -dz), 0, p.there(dz=dz))

    def x_copy(self, dx, dz, mine):
        p = self.pl
        return self.plain(1, dz * (p.nx - 1) + dx - 1, p.page(-dz, 0, 0 if mine else -dx), 0, p.there(dx=dx))

    def y_copy(self, dy, dz, mine):
        p = self.pl
        return self.plain(2, dz * (p.ny - 1) + dy - 1, p.page(-dz, 0 if mine else -dy, 0), 0, p.there(dy=dy))

    def xa_copy(self, dx, dy, dz):
        p = self.pl
        return self.plain(3, self.corner_slot(dx, dy, dz), p.page(-dz, -dy, 0), 1, p.there(dx=dx))

    def yb_copy(self, dx, dy, dz):
        p = self.pl
        return self.plain(3, self.corner_slot(dx, dy, dz), p.page(-dz, 0, -dx), 2, p.there(dy=dy))

    def core_copy(self, page, part, count=None):
        return self.copy(self.view(page, part, None, count), self.sbase[1], self.rbase[6], self.pl.sibling)

    def relay_copy(self, group, up):
        p = self.pl
        level = group * p.plane
        target = p.there(dz=1 if up else p.nz - 1)
        return self.copy(self.view(level, 3, None, p.plane), self.sbase[3 if up else 4] + group, self.rbase[5] + group, target)

    def wait(self, view, sem):
        pltpu.make_async_copy(view, view, sem).wait()

    def begin(self):
        p = self.pl
        if self.low:
            for dy, dx in p.others:
                self.copy(self.view(p.page(), 3), self.sbase[2], self.rbase[4], p.there(0, dy, dx)).start()
        for d in range(1, p.nz):
            self.z_copy(d, True).start()

    def spread(self, dz):
        p = self.pl
        for d in range(1, p.nx):
            self.x_copy(d, dz, True).start()
        for d in range(1, p.ny):
            self.y_copy(d, dz, True).start()
        self.core_copy(p.page(-dz), 0).start()

    def column(self, dz):
        self.z_copy(dz, False).wait_recv()
        self.spread(dz)

    def rise(self):
        p = self.pl
        if not self.low:
            return
        level = p.level(0)
        self.wait(self.view(level, 3, None, p.plane - 1), self.recv.at[self.rbase[4]])
        pl.when(p.z < p.nz - 1)(lambda: self.relay_copy(p.z, True).start())
        pl.when(p.z > 0)(lambda: self.relay_copy(p.z, False).start())
        self.core_copy(level, 3, p.plane).start()

    def relay(self, d):
        p = self.pl
        if not self.low:
            return

        def step(up):
            group = p.z - d if up else p.z + d
            self.relay_copy(group, up).wait_recv()
            pl.when(p.z < p.nz - 1 if up else p.z > 0)(lambda: self.relay_copy(group, up).start())
            self.core_copy(group * p.plane, 3, p.plane).start()

        pl.when(p.z >= d)(lambda: step(True))
        pl.when(p.z + d < p.nz)(lambda: step(False))

    def plane(self, dz):
        p = self.pl
        for dy in range(1, p.ny):
            self.y_copy(dy, dz, False).wait_recv()
            for dx in range(1, p.nx):
                self.xa_copy(dx, dy, dz).start()
            self.core_copy(p.page(-dz, -dy), 0).start()
        for dx in range(1, p.nx):
            self.x_copy(dx, dz, False).wait_recv()
            if self.kind != SMALL:
                for dy in range(1, p.ny):
                    self.yb_copy(dx, dy, dz).start()
            self.core_copy(p.page(-dz, 0, -dx), 0).start()

    def corner(self, dz):
        p = self.pl
        for dy in range(1, p.ny):
            for dx in range(1, p.nx):
                page = p.page(-dz, -dy, -dx)
                self.wait(self.view(page, 0), self.recv.at[self.rbase[3] + self.corner_slot(dx, dy, dz)])
                self.core_copy(page, 0).start()

    def finish_core(self):
        self.wait(self.view(0, 4, 1 - self.pl.c, self.pl.nz * self.pl.plane), self.recv.at[self.rbase[6]])

    def drain(self):
        p = self.pl
        pages = p.nz * p.plane
        self.wait(self.view(0, 4, None, pages), self.send.at[self.sbase[1]])
        corners = p.nz * (p.ny - 1) * (p.nx - 1)
        blocks = p.nz - 1 + p.nz * (p.nx - 1) + p.nz * (p.ny - 1) + corners
        if self.low:
            self.wait(self.view(0, 3, None, p.plane - 1), self.send.at[self.sbase[2]])
        self.wait(self.view(0, 0, None, blocks), self.send.at[self.sbase[0]])
        if self.low:
            def group(g):
                pl.when(jnp.logical_and(p.z < p.nz - 1, g <= p.z))(lambda: self.relay_copy(g, True).wait_send())
                pl.when(jnp.logical_and(p.z > 0, g >= p.z))(lambda: self.relay_copy(g, False).wait_send())
            for g in range(p.nz):
                group(g)


def reduce_slots(pages, low):
    nz, ny, nx = page_grid(pages)
    corners = nz * (nx - 1) * (ny - 1)
    n = nz if low else 0
    return slots((1, 1, 1, n, n)), slots((nz, corners, corners, nz * (nx - 1), nz * (ny - 1), nz - 1, 1, n, n))


def reduce_scratch(pages, panels, rows, width, kind, low):
    nz, ny, nx = page_grid(pages)
    fx, fy = nx - 1, ny - 1
    half = (panels // 2, rows) if kind == PANELS else (panels, rows // 2)
    rest = width - low
    (_, sends), (_, recvs) = reduce_slots(pages, low)
    return [
        VMEM((panels, nz * ny * nx, rows, width), BF),
        VMEM((nz * fx * fy,) + half + (rest,), BF),
        VMEM((nz * fx * fy,) + half + (rest,), BF),
        VMEM((nz * fx, panels, rows, rest), BF),
        VMEM((nz * fy, panels, rows, rest), BF),
        VMEM((nz - 1, panels, rows, rest), BF),
        VMEM((ny * nx - 1, panels, rows, low) if low else (8, LANES), BF),
        VMEM((2, nz, panels, ny * nx, rows, low) if low else (8, LANES), BF),
        DMA((sends,)),
        DMA((recvs,)),
    ]


REDUCE_REFS = 10


class Reduce:
    def __init__(self, place, part, scratch, kind, low):
        self.pl, self.part, self.kind, self.low = place, part, kind, low
        self.total, self.da, self.db, self.rx, self.ry, self.rz, self.rp, self.rr, self.send, self.recv = scratch
        (self.sbase, _), (self.rbase, _) = reduce_slots(place.nz * place.plane, low)

    def remote(self, send, recv, src, dst, target):
        return pltpu.make_async_remote_copy(
            src_ref=src, dst_ref=dst, send_sem=self.send.at[send], recv_sem=self.recv.at[recv],
            device_id=target, device_id_type=MESH)

    def plain(self, group, slot, src, dst, target):
        return self.remote(self.sbase[0], self.rbase[group] + slot, src, dst, target)

    def wait(self, view, sem):
        pltpu.make_async_copy(view, view, sem).wait()

    def half(self, page, which):
        if self.kind == PANELS:
            n = self.total.shape[0] // 2
            return self.total.at[which * n:(which + 1) * n, page, :, self.low:]
        n = self.total.shape[2] // 2
        return self.total.at[:, page, which * n:(which + 1) * n, self.low:]

    def corner_slot(self, dz, dy, dx):
        return (dz * (self.pl.ny - 1) + dy - 1) * (self.pl.nx - 1) + dx - 1

    def core_copy(self, dz, level=None):
        p = self.pl
        pages = pl.ds(p.level(dz) if level is None else level, p.plane)
        return self.remote(
            self.sbase[1], self.rbase[0] + dz, self.part.at[:, pages, 1 - p.c], self.total.at[:, pages], p.sibling)

    def xa_copy(self, dz, dy, dx):
        p, slot = self.pl, self.corner_slot(dz, dy, dx)
        return self.plain(1, slot, self.half(p.page(dz, dy, dx), 0), self.da.at[slot], p.there(dx=dx))

    def yb_copy(self, dz, dy, dx):
        p, slot = self.pl, self.corner_slot(dz, dy, dx)
        return self.plain(2, slot, self.half(p.page(dz, dy, dx), 1), self.db.at[slot], p.there(dy=dy))

    def x_copy(self, dz, dx):
        p = self.pl
        slot = dz * (p.nx - 1) + dx - 1
        return self.plain(3, slot, self.total.at[:, p.page(dz, 0, dx), :, self.low:], self.rx.at[slot], p.there(dx=dx))

    def y_copy(self, dz, dy):
        p = self.pl
        slot = dz * (p.ny - 1) + dy - 1
        return self.plain(4, slot, self.total.at[:, p.page(dz, dy, 0), :, self.low:], self.ry.at[slot], p.there(dy=dy))

    def z_copy(self, dz):
        p = self.pl
        return self.plain(5, dz - 1, self.total.at[:, p.page(dz), :, self.low:], self.rz.at[dz - 1], p.there(dz=dz))

    def relay_copy(self, group, up):
        p = self.pl
        level, way = group * p.plane, 0 if up else 1
        return self.remote(
            self.sbase[3 + way] + group, self.rbase[7 + way] + group,
            self.total.at[:, pl.ds(level, p.plane), :, 0:self.low], self.rr.at[way, group], p.there(dz=1 if up else p.nz - 1))

    def plane_copy(self, k, dy, dx):
        p = self.pl
        return self.remote(
            self.sbase[2], self.rbase[6], self.total.at[:, p.page(0, dy, dx), :, 0:self.low], self.rp.at[k], p.there(0, dy, dx))

    def begin(self, dz, level=None):
        self.core_copy(dz, level).start()

    def arrive(self, dz):
        self.core_copy(dz).wait_recv()

    def pair(self, page):
        return self.part[:, page, self.pl.c, :, self.low:].astype(F32) + self.total[:, page, :, self.low:].astype(F32)

    def corner(self, dz):
        p = self.pl
        for dy in range(1, p.ny):
            for dx in range(1, p.nx):
                page = p.page(dz, dy, dx)
                self.total[:, page, :, self.low:] = self.pair(page).astype(BF)
                self.xa_copy(dz, dy, dx).start()
                self.yb_copy(dz, dy, dx).start()

    def level_sum(self, group):
        p = self.pl
        pages = pl.ds(group * p.plane, p.plane)
        total = self.part[:, pages, p.c, :, 0:self.low].astype(F32) + self.total[:, pages, :, 0:self.low].astype(F32)
        return total, pages

    def relay(self, d):
        p = self.pl
        if not self.low:
            return

        def step(up):
            group = p.z + d if up else p.z - d
            total, pages = self.level_sum(group)
            self.total[:, pages, :, 0:self.low] = total.astype(BF)

            def add():
                self.relay_copy(group, up).wait_recv()
                got = self.rr[0 if up else 1, group].astype(F32)
                self.total[:, pages, :, 0:self.low] = (total + got).astype(BF)

            pl.when(p.z > 0 if up else p.z < p.nz - 1)(add)
            self.relay_copy(group, up).start()

        pl.when(p.z + d < p.nz)(lambda: step(True))
        pl.when(p.z >= d)(lambda: step(False))

    def settle(self):
        p = self.pl
        if not self.low:
            return
        group = p.z
        total, pages = self.level_sum(group)
        self.total[:, pages, :, 0:self.low] = total.astype(BF)
        for way in range(2):
            def add(way=way):
                self.relay_copy(group, way == 0).wait_recv()
                self.total[:, pages, :, 0:self.low] = (
                    self.total[:, pages, :, 0:self.low].astype(F32) + self.rr[way, group].astype(F32)).astype(BF)
            pl.when(p.z > 0 if way == 0 else p.z < p.nz - 1)(add)
        for k, (dy, dx) in enumerate(p.others):
            self.plane_copy(k, dy, dx).start()

    def owned(self):
        p = self.pl
        self.wait(self.rp, self.recv.at[self.rbase[6]])
        total = self.total[:, p.page(), :, 0:self.low].astype(F32)
        for k in range(len(p.others)):
            total += self.rp[k].astype(F32)
        return total

    def plane(self, dz):
        p = self.pl
        panels, rows = self.total.shape[0], self.total.shape[2]

        def with_half(total, add, which):
            axis, n = (0, panels // 2) if self.kind == PANELS else (1, rows // 2)
            first, second = (total[:n], total[n:]) if axis == 0 else (total[:, :n], total[:, n:])
            return jnp.concatenate([first + add, second] if which == 0 else [first, second + add], axis=axis)

        for dx in range(1, p.nx):
            page = p.page(dz, 0, dx)
            total = self.pair(page)
            for dy in range(1, p.ny):
                self.yb_copy(dz, dy, dx).wait_recv()
                total = with_half(total, self.db[self.corner_slot(dz, dy, dx)].astype(F32), 1)
            self.total[:, page, :, self.low:] = total.astype(BF)
            self.x_copy(dz, dx).start()
        for dy in range(1, p.ny):
            page = p.page(dz, dy, 0)
            total = self.pair(page)
            for dx in range(1, p.nx):
                self.xa_copy(dz, dy, dx).wait_recv()
                total = with_half(total, self.da[self.corner_slot(dz, dy, dx)].astype(F32), 0)
            self.total[:, page, :, self.low:] = total.astype(BF)
            self.y_copy(dz, dy).start()

    def column_sum(self, dz):
        p = self.pl
        total = self.pair(p.page(dz))
        for dx in range(1, p.nx):
            self.x_copy(dz, dx).wait_recv()
            total += self.rx[dz * (p.nx - 1) + dx - 1].astype(F32)
        for dy in range(1, p.ny):
            self.y_copy(dz, dy).wait_recv()
            total += self.ry[dz * (p.ny - 1) + dy - 1].astype(F32)
        return total

    def column(self, dz):
        self.total[:, self.pl.page(dz), :, self.low:] = self.column_sum(dz).astype(BF)
        self.z_copy(dz).start()

    def finish(self):
        total = self.column_sum(0)
        for dz in range(1, self.pl.nz):
            self.z_copy(dz).wait_recv()
            total += self.rz[dz - 1].astype(F32)
        return jnp.concatenate([self.owned(), total], axis=2) if self.low else total

    def drain(self):
        p = self.pl
        pages = p.nz * p.plane
        self.wait(self.part.at[:, :, 0], self.send.at[self.sbase[1]])
        self.wait(self.total.at[:, 0:pages - 1, :, self.low:], self.send.at[self.sbase[0]])
        if not self.low:
            return
        self.wait(self.rp, self.send.at[self.sbase[2]])

        def group(g):
            pl.when(g > p.z)(lambda: self.relay_copy(g, True).wait_send())
            pl.when(g < p.z)(lambda: self.relay_copy(g, False).wait_send())

        for g in range(p.nz):
            group(g)


def vector_scratch(pages, rows, width):
    nz, ny, nx = page_grid(pages)
    n = 1 + ny * nx - 1 + nz - 1
    return [VMEM((3, rows, width), F32), VMEM((3, rows, width), BF), VMEM((n, rows, width), BF), DMA((n,)), DMA((n,))]


class VectorSum:
    def __init__(self, place, scratch):
        self.pl = place
        self.own, self.held, self.got, self.send, self.recv = scratch

    def legs(self):
        p = self.pl
        return [
            [p.sibling],
            [p.there(0, dy, dx) for dy, dx in p.others],
            [p.there(dz=d) for d in range(1, p.nz)],
        ]

    def copies(self, leg):
        legs = self.legs()
        at = sum(len(one) for one in legs[:leg])
        return [
            pltpu.make_async_remote_copy(
                src_ref=self.held.at[leg], dst_ref=self.got.at[at + i], send_sem=self.send.at[at + i],
                recv_sem=self.recv.at[at + i], device_id=target, device_id_type=MESH)
            for i, target in enumerate(legs[leg])
        ], at

    def put(self, leg, value):
        self.own[leg] = value
        self.held[leg] = value.astype(BF)
        for copy in self.copies(leg)[0]:
            copy.start()

    def take(self, leg):
        copies, at = self.copies(leg)
        value = self.own[leg]
        for i, copy in enumerate(copies):
            copy.wait_recv()
            value += self.got[at + i].astype(F32)
        return value

    def drain(self):
        for leg in range(3):
            for copy in self.copies(leg)[0]:
                copy.wait_send()


HEADS = 12


masked_value = -1e30
norm_eps = 1e-06


def layer_norm(values, norm_gain, norm_shift):
    centre = jnp.mean(values, axis=-1, keepdims=True)
    centered = values - centre
    spread = jnp.mean(centered * centered, axis=-1, keepdims=True)
    return centered * lax.rsqrt(spread + norm_eps) * norm_gain + norm_shift


def gelu_exact(values):
    return jax.nn.gelu(values, approximate=False)


def matmul(left_side, right_side):
    return jnp.dot(left_side, right_side, preferred_element_type=jnp.float32)


def column_sum(values):
    return jnp.sum(values.astype(jnp.float32), axis=0)


def usable_keys(page_lengths, seg_len):
    places = lax.broadcasted_iota(jnp.int32, (page_lengths.shape[0], seg_len), 1)
    return places < page_lengths[:, None]


def head_split(values, head_count):
    return values.reshape(
        values.shape[0], values.shape[1], head_count, values.shape[2] // head_count
    )


def page_scores(query_heads, key_piece, usable, score_scale):
    key_heads = head_split(key_piece, query_heads.shape[2])
    scores = (
        jnp.einsum("pqhd,pkhd->phqk", query_heads, key_heads, preferred_element_type=jnp.float32)
        * score_scale
    )
    return jnp.where(usable[:, None, None, :], scores, masked_value)


VECTORS = 8


def pack_vectors(vectors, inner):
    rows = [jnp.pad(v[None], ((j, 15 - j), (0, 128 - v.shape[0]))) for j, v in enumerate((*vectors, inner))]
    return functools.reduce(jnp.add, rows)


LOG2E = 1.4426950408889634
VEC_ROWS = 16
NT = ((1,), (1,))
TN = ((0,), (0,))


def steps_loop(count, body, steps):
    def one(i, _):
        body(i)
        for at, todo in steps.items():
            def run(todo=todo):
                for step in todo:
                    step()
            pl.when(i == at)(run)
        return 0

    lax.fori_loop(0, count, one, 0)


def dot(left, right, dims=((1,), (0,))):
    return lax.dot_general(left, right, (dims, ((), ())), preferred_element_type=F32)


def standardize(values):
    centered = values - jnp.mean(values, axis=-1, keepdims=True)
    r = lax.rsqrt(jnp.mean(centered * centered, axis=-1, keepdims=True) + norm_eps)
    return centered * r, r


def norm_back(grad, xhat, r, gain):
    e = grad * gain
    return r * (e - jnp.mean(e, axis=-1, keepdims=True) - xhat * jnp.mean(e * xhat, axis=-1, keepdims=True))


def add_row(ref, row, values):
    ref[row:row + 1, :] += jnp.sum(values, axis=0, keepdims=True)


def spread_lanes(small, n, width, first):
    devices, vectors, lanes = small.shape
    column = (first + lax.broadcasted_iota(jnp.int32, (lanes, width), 1)).astype(F32)
    owner = jnp.floor((column + 0.5) * (1.0 / n))
    lane = lax.broadcasted_iota(jnp.int32, (lanes, width), 0).astype(F32)
    pick = jnp.where(column - owner * n == lane, 1.0, 0.0).astype(BF)
    values = dot(small.reshape(devices * vectors, lanes), pick).reshape(devices, vectors, width)
    device = lax.broadcasted_iota(jnp.int32, (devices, vectors, width), 0).astype(F32)
    return jnp.sum(jnp.where(owner[:1][None] == device, values, 0.0), axis=0)


def layer_scratch(pages, rows, width, panels, tokens, local_pages):
    (_, gather_sends), (_, gather_recvs) = gather_slots(pages)
    seg = tokens // local_pages
    groups = width // (2 * LANES)
    own = dict(
        g_attn=VMEM((4, pages, 2, rows, width), BF),
        g_inner=VMEM((panels, pages, 2, rows, width), BF),
        g_outer=VMEM((1, pages, 2, panels * rows, width), BF),
        g_small=VMEM((1, pages, 2, VEC_ROWS, LANES), BF),
        p_output=VMEM((2, pages, 2, rows, width // 2), BF),
        p_groups=VMEM((groups, 6, pages, 2, rows, LANES), BF),
        xs=VMEM((tokens, width), BF),
        q=VMEM((tokens, width), BF),
        k=VMEM((local_pages, 2 * seg, width), BF),
        v=VMEM((local_pages, 2 * seg, width), BF),
        ctx=VMEM((tokens, width), BF),
        xhat=VMEM((tokens, width), F32),
        r_one=VMEM((tokens, 1), F32),
        low=VMEM((tokens, width), BF),
        post=VMEM((panels, tokens, width), BF),
        slope=VMEM((panels, tokens, width), BF),
        res=VMEM((tokens, width), F32),
        d_low=VMEM((tokens, width), BF),
        vec=VMEM((VEC_ROWS, width), F32),
        par=VMEM((VEC_ROWS, width), F32),
        rk=VMEM((local_pages, seg, width), BF),
        rv=VMEM((local_pages, seg, width), BF),
        x=VMEM((tokens, width), BF),
        cot=VMEM((tokens, width), BF),
        out=VMEM((tokens, width), BF),
        squares=VMEM((4, rows, width), F32),
        wide=VMEM((rows, panels * width), F32),
        tall=VMEM((panels * rows, width), F32),
        total=VMEM((VEC_ROWS, width), F32),
        in_sem=DMA((8 + panels,)),
        out_sem=DMA((9,)),
        x_sem=DMA((2,)),
        kv_sem=DMA((4, groups)),
    )
    gather = [DMA((gather_sends,)), DMA((gather_recvs,))] * 4
    reduce = []
    parts = [(1, panels * rows, width, ROWS, REDUCE_RELAY), (panels, rows, width, PANELS, REDUCE_RELAY)]
    parts += [(2, rows, width // 2, PANELS, 0)] + [(6, rows, LANES, PANELS, 0)] * groups
    for part in parts:
        reduce += reduce_scratch(pages, *part)
    return own, gather + reduce + vector_scratch(pages, VEC_ROWS, width)


def layer_kernel(pages, heads, names, lengths, x_in, cot_in, wq, wk, wv, wo, wi, wout, small,
                 layer_out, hidden_grad, o_q, o_k, o_v, o_o, o_inner, o_outer, o_vec, *scratch):
    s = types.SimpleNamespace(**dict(zip(names, scratch)))
    s.d_ctx, s.grad = s.xs, s.cot
    rest = scratch[len(names):]
    place = Place(pages)
    c, nz = place.c, place.nz
    mine = place.p, c
    sibling = place.sibling
    x, cot = s.x, s.cot
    tokens, width = x.shape
    panels, _, _, rows = s.g_inner.shape[:4]
    blocks = (pages, 2, rows, width)
    local_pages, page_len = s.k.shape[:2]
    seg = tokens // local_pages
    full = (width, width)
    scale = (width // heads) ** -0.5
    q, k, v, ctx, res, par, vec = s.q, s.k, s.v, s.ctx, s.res, s.par, s.vec

    arrived = place.signal()
    moves = [(x_in, x), (small, s.g_small.at[0, *mine])]
    moves += [(ref, s.g_attn.at[j, *mine]) for j, ref in enumerate((wq, wk, wv, wo))]
    moves += [(wi.at[:, j * width:(j + 1) * width], s.g_inner.at[j, *mine]) for j in range(panels)]
    moves += [(wout, s.g_outer.at[0, *mine]), (cot_in, cot)]
    moves = [pltpu.make_async_copy(src, dst, s.in_sem.at[i]) for i, (src, dst) in enumerate(moves)]
    for move in moves:
        move.start()
    for move in moves[:-1]:
        move.wait()
    arrived()

    def emit(i, src, dst):
        return pltpu.make_async_copy(src, dst, s.out_sem.at[i])

    results = [
        emit(i, src, dst) for i, (src, dst) in enumerate((
            (s.out, layer_out), (s.grad, hidden_grad), (s.squares.at[0], o_q), (s.squares.at[1], o_k), (s.squares.at[2], o_v),
            (s.squares.at[3], o_o), (s.wide, o_inner), (s.tall, o_outer), (s.total, o_vec)))]
    x_copy = pltpu.make_async_remote_copy(
        src_ref=x, dst_ref=s.xs, send_sem=s.x_sem.at[0], recv_sem=s.x_sem.at[1],
        device_id=sibling, device_id_type=MESH)
    x_copy.start()
    tiny, attn, inner, outer = (
        Gather(place, ref, rest[2 * i], rest[2 * i + 1], kind)
        for i, (ref, kind) in enumerate(((s.g_small, SMALL), (s.g_attn, PANELS), (s.g_inner, PANELS), (s.g_outer, ROWS))))
    first = (attn, tiny)
    for one in first:
        one.begin()
    for one in first:
        one.spread(0)
    for dz in range(1, nz):
        for one in first:
            one.column(dz)
    attn.rise()
    inner.begin()
    for dz in range(nz):
        for one in first:
            one.plane(dz)
    inner.spread(0)
    attn.relay(1)
    attn.relay(2)
    for dz in range(1, nz):
        inner.column(dz)
    attn.relay(3)
    inner.rise()
    outer.begin()
    outer.spread(0)
    for dz in range(nz):
        for one in first:
            one.corner(dz)
    for one in first:
        one.finish_core()
    x_copy.wait()

    def begin_all(one):
        for dz in range(nz):
            one.begin(dz)

    def corners(one):
        loop(0, one.arrive)
        loop(0, one.corner)

    def weight(ref, j):
        return ref[j].reshape(full)

    def loop(start, body):
        for dz in range(start, nz):
            body(dz)

    def outer_weight(j):
        n = pages // panels
        return s.g_outer[0, pl.ds(j * n, n)].reshape(full)

    gathered = s.g_small[0].reshape(2 * pages, VEC_ROWS, LANES)
    par[...] = spread_lanes(gathered, rows, width, 0)
    for j in range(panels):
        par[VECTORS + j:VECTORS + j + 1, :] = spread_lanes(gathered, panels * rows, width, j * width)[VECTORS:VECTORS + 1]
    vec[...] = jnp.zeros_like(vec)

    def vector(j):
        return par[j:j + 1, :]

    q[...] = (dot(x[...], weight(s.g_attn, 0)) + vector(0)).astype(BF)
    inner.plane(0)

    def project(i, _):
        ref, half = (x, c) if i == 0 else (s.xs, 1 - c)
        rows_of = pl.ds(pl.multiple_of(half * seg, seg), seg)
        k[:, rows_of, :] = dot(ref[...], weight(s.g_attn, 1)).astype(BF).reshape(local_pages, seg, width)
        v[:, rows_of, :] = (dot(ref[...], weight(s.g_attn, 2)) + vector(1)).astype(BF).reshape(local_pages, seg, width)

    project(0, 0)
    inner.plane(1)
    project(1, 0)
    inner.plane(2)

    pairs = heads // 2
    head_dim = width // heads

    def place_of(i):
        page, pair = i // pairs, lax.rem(i, pairs)
        return page, pl.ds(pl.multiple_of(page * seg, seg), seg), pl.ds(pl.multiple_of(pair * LANES, LANES), LANES)

    low_half = lax.broadcasted_iota(jnp.int32, (1, LANES), 1) < head_dim
    key_at = lax.broadcasted_iota(jnp.int32, (1, page_len), 1)

    def one_head(values, head):
        return jnp.where(low_half if head == 0 else jnp.logical_not(low_half), values, jnp.zeros_like(values))

    def probabilities(q2, k2, head, usable):
        t = jnp.where(usable, dot(q2, one_head(k2, head), NT) * (scale * LOG2E), masked_value)
        e = jnp.exp2(t - jnp.max(t, axis=-1, keepdims=True))
        return e * (1.0 / jnp.sum(e, axis=-1, keepdims=True))

    def attend(i):
        page, rows_of, cols = place_of(i)
        q2, k2, v2 = q[rows_of, cols], k[page, :, cols], v[page, :, cols]
        usable = key_at < lengths[page]
        parts = [dot(probabilities(q2, k2, head, usable).astype(BF), v2) for head in range(2)]
        ctx[rows_of, cols] = jnp.where(low_half, *parts).astype(BF)

    steps_loop(local_pages * pairs, attend, {
        0: [lambda: inner.plane(3), lambda: inner.relay(1)],
        1: [lambda: outer.column(1), lambda: inner.relay(2)],
        2: [lambda: outer.column(2), outer.rise],
        3: [lambda: outer.column(3), lambda: inner.relay(3)],
        4: [lambda: inner.corner(0)],
        5: [lambda: inner.corner(1)],
        6: [lambda: inner.corner(2), lambda: outer.relay(1)],
        7: [lambda: inner.corner(3)],
        8: [lambda: outer.plane(0), lambda: outer.relay(2)],
        9: [lambda: outer.plane(1)],
        10: [lambda: outer.plane(2), lambda: outer.relay(3)],
        11: [lambda: outer.plane(3)],
    })

    res[...] = dot(ctx[...], weight(s.g_attn, 3))
    chunk = 128

    def chunks(body):
        def one(i, _):
            body(pl.ds(pl.multiple_of(i * chunk, chunk), chunk))
            return 0
        lax.fori_loop(0, tokens // chunk, one, 0)

    def norm_one(at):
        xhat, r = standardize(x[at, :].astype(F32) + res[at, :] + vector(2))
        s.xhat[at, :] = xhat
        s.r_one[at, :] = r
        normed = xhat * vector(3) + vector(4)
        s.low[at, :] = normed.astype(BF)
        res[at, :] = normed + vector(5)

    chunks(norm_one)

    inner.finish_core()
    root_half = 0.7071067811865476

    def expand(j):
        pre = dot(s.low[...], weight(s.g_inner, j)) + par[pl.ds(VECTORS + j, 1), :]
        half_one = 0.5 * (1.0 + lax.erf(pre * root_half))
        bell = jnp.exp2(pre * pre * (-0.5 * LOG2E)) * 0.3989422804014327
        s.post[j] = (pre * half_one).astype(BF)
        s.slope[j] = (half_one + pre * bell).astype(BF)

    steps_loop(panels, expand, {j: [lambda j=j: outer.corner(j)] for j in range(nz)})
    outer.finish_core()

    def contract(j, _):
        res[...] += dot(s.post[j], outer_weight(j))
        return 0

    lax.fori_loop(0, panels, contract, 0)

    def norm_two(at):
        xhat, r = standardize(res[at, :])
        s.out[at, :] = (xhat * vector(6) + vector(7)).astype(BF)
        grad = cot[at, :].astype(F32)
        add_row(vec, 6, grad * xhat)
        add_row(vec, 7, grad)
        d_res = norm_back(grad, xhat, r, vector(6))
        res[at, :] = d_res
        d_low = d_res.astype(BF)
        s.d_low[at, :] = d_low
        add_row(vec, 5, d_low.astype(F32))

    moves[-1].wait()
    chunks(norm_two)
    results[0].start()

    parts = [(s.g_outer, ROWS, REDUCE_RELAY), (s.g_inner, PANELS, REDUCE_RELAY), (s.p_output, PANELS, 0)]
    parts += [(s.p_groups.at[g], PANELS, 0) for g in range(s.p_groups.shape[0])]
    reducers = [
        Reduce(place, part, rest[8 + REDUCE_REFS * i:8 + REDUCE_REFS * (i + 1)], kind, low)
        for i, (part, kind, low) in enumerate(parts)]
    r_outer, r_inner, r_output, *r_groups = reducers
    outer.drain()

    def outer_back(dz):
        j = lax.rem(place.z + dz, nz)
        d_low = s.d_low[...]
        d_pre = (dot(d_low, outer_weight(j), NT) * s.slope[j].astype(F32)).astype(BF)
        n = pages // panels
        s.g_outer[0, pl.ds(j * n, n)] = dot(s.post[j], d_low, TN).reshape(n, 2, panels * rows, width).astype(BF)
        r_outer.begin(dz, j * place.plane)
        s.slope[j] = d_pre
        vec[pl.ds(VECTORS + j, 1), :] = jnp.sum(d_pre.astype(F32), axis=0, keepdims=True)

    steps_loop(nz, outer_back, {
        1: [lambda: r_outer.arrive(0), lambda: r_outer.corner(0)],
        2: [lambda: r_outer.arrive(1), lambda: r_outer.corner(1)],
        3: [lambda: r_outer.arrive(2), lambda: r_outer.corner(2)],
    })
    inner.drain()

    def inner_back(j):
        d_pre = s.slope[j]
        res[...] += dot(d_pre, weight(s.g_inner, j), NT)
        s.g_inner[j] = dot(s.low[...], d_pre, TN).reshape(blocks).astype(BF)

    steps_loop(panels, inner_back, {
        0: [lambda: r_outer.arrive(3), lambda: r_outer.corner(3), lambda: r_outer.plane(0), lambda: r_outer.relay(3)],
        1: [lambda: r_outer.plane(1)],
        2: [lambda: r_outer.plane(2), lambda: r_outer.relay(2)],
        3: [lambda: r_outer.plane(3)],
    })
    begin_all(r_inner)

    def norm_one_back(at):
        grad, xhat = res[at, :], s.xhat[at, :]
        add_row(vec, 3, grad * xhat)
        add_row(vec, 4, grad)
        d_res = norm_back(grad, xhat, s.r_one[at, :], vector(3))
        res[at, :] = d_res
        d_low = d_res.astype(BF)
        s.d_low[at, :] = d_low
        add_row(vec, 2, d_low.astype(F32))

    chunks(norm_one_back)
    s.d_ctx[...] = dot(s.d_low[...], weight(s.g_attn, 3), NT).astype(BF)
    grad = dot(ctx[...], s.d_low[...], TN).reshape(blocks)
    half = width // 2
    for j in range(2):
        s.p_output[j] = grad[..., j * half:(j + 1) * half].astype(BF)
    begin_all(r_output)
    r_outer.relay(1)
    r_outer.column(1)
    r_inner.arrive(0)
    r_inner.corner(0)
    r_inner.arrive(3)
    r_inner.corner(3)
    r_inner.arrive(1)
    r_inner.corner(1)
    r_inner.arrive(2)
    r_inner.corner(2)
    r_inner.relay(3)

    d_q, d_k, d_v = s.post.at[0], s.post.at[1:1 + local_pages], s.slope.at[0:local_pages]

    def kv_copies(g):
        theirs = pl.ds(pl.multiple_of((1 - c) * seg, seg), seg)
        cols = slice(2 * LANES * g, 2 * LANES * (g + 1))
        return [
            pltpu.make_async_remote_copy(
                src_ref=grad.at[:, theirs, cols], dst_ref=got.at[:, :, cols], send_sem=s.kv_sem.at[2 * n, g],
                recv_sem=s.kv_sem.at[2 * n + 1, g], device_id=sibling, device_id_type=MESH)
            for n, (grad, got) in enumerate(((d_k, s.rk), (d_v, s.rv)))]

    def exchange(g):
        for copy in kv_copies(g):
            copy.start()

    def group_grads(g):
        cols = slice(2 * LANES * g, 2 * LANES * (g + 1))
        for copy in kv_copies(g):
            copy.wait_recv()
        ours = pl.ds(pl.multiple_of(c * seg, seg), seg)
        for j in range(3):
            if j == 0:
                total = d_q[:, cols]
            else:
                mine_k, got = ((d_k, s.rk), (d_v, s.rv))[j - 1]
                total = (mine_k[:, ours, cols].astype(F32) + got[:, :, cols].astype(F32)).astype(BF)
                got[:, :, cols] = total
                total = total.reshape(tokens, 2 * LANES)
            if j != 1:
                vec[j // 2:j // 2 + 1, cols] = jnp.sum(total.astype(F32), axis=0, keepdims=True)
            grad = dot(x[...], total, TN).reshape(pages, 2, rows, 2 * LANES)
            for n in range(2):
                s.p_groups[g, 2 * j + n] = grad[..., n * LANES:(n + 1) * LANES].astype(BF)
        for dz in range(nz):
            r_groups[g].begin(dz)

    def attend_back(i):
        page, rows_of, cols = place_of(lax.rem(i, local_pages) * pairs + i // local_pages)
        q2, k2, v2 = q[rows_of, cols], k[page, :, cols], v[page, :, cols]
        c2 = s.d_ctx[rows_of, cols]
        usable = key_at < lengths[page]
        found = []
        for head in range(2):
            p = probabilities(q2, k2, head, usable)
            d_p = dot(c2, one_head(v2, head), NT)
            d_s = (p * (d_p - jnp.sum(p * d_p, axis=-1, keepdims=True))).astype(BF)
            found.append((dot(d_s, k2), dot(d_s, q2, TN), dot(p.astype(BF), c2, TN)))
        both = [jnp.where(low_half, one, two) for one, two in zip(*found)]
        d_q[rows_of, cols] = (both[0] * scale).astype(BF)
        d_k[page, :, cols] = (both[1] * scale).astype(BF)
        d_v[page, :, cols] = both[2].astype(BF)

    def finish_outer():
        s.tall[...] = r_outer.finish()[0]
        results[7].start()

    def finish_inner():
        total = r_inner.finish()
        for j in range(panels):
            s.wide[:, j * width:(j + 1) * width] = total[j]
        results[6].start()

    def finish_output():
        total = r_output.finish()
        for j in range(2):
            s.squares[3, :, j * half:(j + 1) * half] = total[j]
        results[5].start()

    def finish_group(g):
        total = r_groups[g].finish()
        for j in range(3):
            for n in range(2):
                at = (2 * g + n) * LANES
                s.squares[j, :, at:at + LANES] = total[2 * j + n]

    vectors = VectorSum(place, rest[8 + len(reducers) * REDUCE_REFS:])
    steps_loop(local_pages * pairs, attend_back, {
        0: [lambda: r_outer.column(2), lambda: r_outer.column(3)],
        1: [lambda: r_outer.settle()],
        2: [lambda: corners(r_output)],
        3: [lambda: r_inner.plane(0), lambda: exchange(0)],
        4: [lambda: r_inner.relay(2), lambda: r_inner.plane(1)],
        5: [lambda: r_inner.plane(2), lambda: r_inner.plane(3), lambda: group_grads(0)],
        6: [lambda: r_inner.relay(1), lambda: loop(0, r_output.plane)],
        7: [lambda: exchange(1), lambda: corners(r_groups[0]), lambda: finish_outer()],
        8: [lambda: r_inner.column(1), lambda: r_inner.column(2), lambda: r_inner.column(3)],
        9: [lambda: r_inner.settle(), lambda: group_grads(1)],
        10: [lambda: loop(0, r_groups[0].plane)],
        11: [lambda: exchange(2), lambda: corners(r_groups[1])],
    })
    loop(1, r_output.column)
    group_grads(2)
    vectors.put(0, vec[...])
    loop(0, r_groups[1].plane)
    loop(1, r_groups[0].column)
    corners(r_groups[2])
    vectors.put(1, vectors.take(0))
    res[...] += dot(d_q[...], weight(s.g_attn, 0), NT)
    loop(0, r_groups[2].plane)
    loop(1, r_groups[1].column)
    vectors.put(2, vectors.take(1))
    res[...] += dot(s.rk[...].reshape(tokens, width), weight(s.g_attn, 1), NT)
    loop(1, r_groups[2].column)
    s.grad[...] = (res[...] + dot(s.rv[...].reshape(tokens, width), weight(s.g_attn, 2), NT)).astype(BF)
    results[1].start()
    finish_inner()
    finish_output()
    finish_group(1)
    finish_group(2)
    finish_group(0)
    s.total[...] = vectors.take(2)
    results[8].start()
    for i in (2, 3, 4):
        results[i].start()
    tiny.drain()
    attn.drain()
    for one in reducers:
        one.drain()
    vectors.drain()
    for g in range(len(r_groups)):
        for copy in kv_copies(g):
            copy.wait_send()
    for result in results:
        result.wait()


def finish_kernel(rows, panels, out, grad, g_q, g_k, g_v, g_o, g_inner, g_outer, total, *refs):
    outs, owned, held, sems = refs[:8], refs[8:8 + VECTORS + 1], refs[8 + VECTORS + 1:-1], refs[-1]
    copies = [
        (pltpu.make_async_copy(src, way, sems.at[i, 0]), pltpu.make_async_copy(way, dst, sems.at[i, 1]))
        for i, (src, way, dst) in enumerate(zip((out, grad, g_q, g_k, g_v, g_o, g_inner, g_outer), held, outs))]
    for copy, _ in copies:
        copy.start()
    for copy, onward in copies:
        copy.wait()
        onward.start()
    at = lax.axis_index(PAGE) * 2 + lax.axis_index(SEQ)
    width = total.shape[1]
    mine = pltpu.roll(total[0:VECTORS, :], width - rows * at, 1)
    for j, ref in enumerate(owned[:VECTORS]):
        ref[...] = mine[j, :rows]
    per_row = width // (panels * rows)
    row = total[pl.ds(VECTORS + at // per_row, 1), :]
    mine = pltpu.roll(row, width - panels * rows * lax.rem(at, per_row), 1)
    owned[VECTORS][...] = mine[0, :panels * rows]
    for _, onward in copies:
        onward.wait()


def finish(rows, panels, arrays):
    hbm, vm = pl.BlockSpec(memory_space=pl.ANY), pl.BlockSpec(memory_space=VMEM)
    return pl.pallas_call(
        functools.partial(finish_kernel, rows, panels),
        name="finish",
        out_shape=tuple(jax.ShapeDtypeStruct(a.shape, a.dtype) for a in arrays[:8])
        + (jax.ShapeDtypeStruct((rows,), F32),) * VECTORS + (jax.ShapeDtypeStruct((panels * rows,), F32),),
        in_specs=[hbm] * 8 + [vm],
        out_specs=(hbm,) * 8 + (vm,) * (VECTORS + 1),
        scratch_shapes=[VMEM(a.shape, a.dtype) for a in arrays[:8]] + [DMA((8, 2))],
    )(*arrays)


def whole_layer(pages, heads, lengths, x, cot, wq, wk, wv, wo, wi, wout, small, local_pages):
    tokens, width = x.shape
    rows, panels = wq.shape[0], wi.shape[1] // width
    own, scratch = layer_scratch(pages, rows, width, panels, tokens, local_pages)
    hbm = pl.BlockSpec(memory_space=pl.ANY)
    row_shape = jax.ShapeDtypeStruct((tokens, width), BF)
    square = jax.ShapeDtypeStruct((rows, width), F32)
    return pl.pallas_call(
        functools.partial(layer_kernel, pages, heads, tuple(own)),
        name="whole_layer",
        out_shape=(row_shape, row_shape, square, square, square, square,
                   jax.ShapeDtypeStruct((rows, panels * width), F32),
                   jax.ShapeDtypeStruct((panels * rows, width), F32),
                   jax.ShapeDtypeStruct((VEC_ROWS, width), F32)),
        in_specs=[pl.BlockSpec(memory_space=pltpu.SMEM)] + [hbm] * 9,
        out_specs=(hbm,) * 9,
        scratch_shapes=[*own.values(), *scratch],
        compiler_params=pltpu.CompilerParams(collective_id=0, has_side_effects=True, vmem_limit_bytes=61 << 20),
    )(lengths, x, cot, wq, wk, wv, wo, wi, wout, small)


def plain_layer(
    hidden,
    lengths,
    w_query,
    w_key,
    w_value,
    w_output,
    b_query,
    b_value,
    b_output,
    attn_gain,
    attn_shift,
    w_inner,
    b_inner,
    w_outer,
    b_outer,
    ffn_gain,
    ffn_shift,
    cotangent,
):
    model_width = hidden.shape[2]
    head_count = HEADS
    score_scale = (model_width // head_count) ** (-0.5)
    f32 = jnp.float32
    bf16 = jnp.bfloat16
    work_hidden, work_cot = (hidden, cotangent)
    local_pages, local_tokens = (work_hidden.shape[0], work_hidden.shape[1])
    row_count = local_pages * local_tokens
    (
        query_full,
        key_full,
        value_full,
        output_full,
        query_bias,
        value_bias,
        output_bias,
        gain_one,
        shift_one,
    ) = (
        lax.all_gather(w_query, AXES, axis=0, tiled=True),
        lax.all_gather(w_key, AXES, axis=0, tiled=True),
        lax.all_gather(w_value, AXES, axis=0, tiled=True),
        lax.all_gather(w_output, AXES, axis=0, tiled=True),
        lax.all_gather(b_query, AXES, axis=0, tiled=True),
        lax.all_gather(b_value, AXES, axis=0, tiled=True),
        lax.all_gather(b_output, AXES, axis=0, tiled=True),
        lax.all_gather(attn_gain, AXES, axis=0, tiled=True),
        lax.all_gather(attn_shift, AXES, axis=0, tiled=True),
    )
    flat_rows = work_hidden.reshape(row_count, model_width)
    queries = (matmul(flat_rows, query_full) + query_bias.astype(f32)).astype(bf16)
    key_rows = matmul(flat_rows, key_full).astype(bf16)
    value_rows = (matmul(flat_rows, value_full) + value_bias.astype(f32)).astype(bf16)
    query_heads = head_split(queries.reshape(local_pages, local_tokens, model_width), head_count)
    key_pages = key_rows.reshape(local_pages, local_tokens, model_width)
    value_pages = value_rows.reshape(local_pages, local_tokens, model_width)
    stat_shape = (local_pages, head_count, local_tokens)
    stat_start = (jnp.full(stat_shape, masked_value, f32), jnp.zeros(stat_shape, f32))
    key_piece = lax.all_gather(key_pages, SEQ, axis=1, tiled=True)
    usable = usable_keys(lengths, key_piece.shape[1])

    def merged():
        run_peak, run_total = stat_start
        scores = page_scores(query_heads, key_piece, usable, score_scale)
        new_peak = jnp.maximum(run_peak, jnp.max(scores, axis=-1))
        summed = jnp.sum(jnp.exp(scores - new_peak[..., None]), axis=-1)
        return (new_peak, summed)

    run_peak, run_total = merged()
    log_norm = run_peak + jnp.log(run_total)
    add_key_piece = lax.all_gather(key_pages, SEQ, axis=1, tiled=True)
    value_piece = lax.all_gather(value_pages, SEQ, axis=1, tiled=True)
    add_usable = usable_keys(lengths, add_key_piece.shape[1])

    def merged():
        scores = page_scores(query_heads, add_key_piece, add_usable, score_scale)
        attn_probs = jnp.exp(scores - log_norm[..., None]).astype(bf16)
        addend = jnp.einsum(
            "phqk,pkhd->pqhd",
            attn_probs,
            head_split(value_piece, head_count),
            preferred_element_type=f32,
        )
        return addend.reshape(local_pages, local_tokens, model_width)

    context = merged()
    context_low = context.astype(bf16).reshape(row_count, model_width)
    residual_one = (
        flat_rows.astype(f32) + matmul(context_low, output_full) + output_bias.astype(f32)
    )
    normed_one, pull_one = jax.vjp(
        layer_norm, residual_one, gain_one.astype(f32), shift_one.astype(f32)
    )
    inner_full, outer_full, inner_bias, outer_bias, gain_two, shift_two = (
        lax.all_gather(w_inner, AXES, axis=0, tiled=True),
        lax.all_gather(w_outer, AXES, axis=0, tiled=True),
        lax.all_gather(b_inner, AXES, axis=0, tiled=True),
        lax.all_gather(b_outer, AXES, axis=0, tiled=True),
        lax.all_gather(ffn_gain, AXES, axis=0, tiled=True),
        lax.all_gather(ffn_shift, AXES, axis=0, tiled=True),
    )
    normed_low = normed_one.astype(bf16)
    pre_gelu = matmul(normed_low, inner_full) + inner_bias.astype(f32)
    post_gelu, pull_gelu = jax.vjp(gelu_exact, pre_gelu)
    post_low = post_gelu.astype(bf16)
    residual_two = normed_one + matmul(post_low, outer_full) + outer_bias.astype(f32)
    layer_out, pull_two = jax.vjp(
        layer_norm, residual_two, gain_two.astype(f32), shift_two.astype(f32)
    )
    cot_rows = work_cot.reshape(row_count, model_width).astype(f32)
    d_res_two, gain_two_grad, shift_two_grad = pull_two(cot_rows)
    d_outer = d_res_two.astype(bf16)
    outer_w_grad = matmul(post_low.T, d_outer)
    outer_b_grad = column_sum(d_outer)
    (d_pre_full,) = pull_gelu(matmul(d_outer, outer_full.T))
    d_pre = d_pre_full.astype(bf16)
    inner_w_grad = matmul(normed_low.T, d_pre)
    inner_b_grad = column_sum(d_pre)
    d_normed = d_res_two + matmul(d_pre, inner_full.T)
    d_res_one, gain_one_grad, shift_one_grad = pull_one(d_normed)
    ffn_owned = (
        lax.psum_scatter(inner_w_grad, AXES, scatter_dimension=0, tiled=True),
        lax.psum_scatter(outer_w_grad, AXES, scatter_dimension=0, tiled=True),
        lax.psum_scatter(inner_b_grad, AXES, scatter_dimension=0, tiled=True),
        lax.psum_scatter(outer_b_grad, AXES, scatter_dimension=0, tiled=True),
        lax.psum_scatter(gain_two_grad, AXES, scatter_dimension=0, tiled=True),
        lax.psum_scatter(shift_two_grad, AXES, scatter_dimension=0, tiled=True),
    )
    d_attn = d_res_one.astype(bf16)
    output_w_grad = matmul(context_low.T, d_attn)
    output_b_grad = column_sum(d_attn)
    d_context = matmul(d_attn, output_full.T).astype(bf16)
    d_context_heads = head_split(
        d_context.reshape(local_pages, local_tokens, model_width), head_count
    )
    context_heads = head_split(context, head_count)
    row_delta = jnp.transpose(
        jnp.sum(d_context_heads.astype(f32) * context_heads, axis=-1), (0, 2, 1)
    )

    def add_grads(segment):
        key_piece, value_piece = segment
        seg_len = key_piece.shape[1]
        usable = usable_keys(lengths, seg_len)

        def merged():
            scores = page_scores(query_heads, key_piece, usable, score_scale)
            attn_probs = jnp.exp(scores - log_norm[..., None])
            key_heads = head_split(key_piece, head_count)
            value_heads = head_split(value_piece, head_count)
            d_probs = jnp.einsum(
                "pqhd,pkhd->phqk", d_context_heads, value_heads, preferred_element_type=f32
            )
            d_scores = (attn_probs * (d_probs - row_delta[..., None])).astype(bf16)
            query_part = jnp.einsum(
                "phqk,pkhd->pqhd", d_scores, key_heads, preferred_element_type=f32
            )
            key_part = jnp.einsum(
                "phqk,pqhd->pkhd", d_scores, query_heads, preferred_element_type=f32
            )
            value_part = jnp.einsum(
                "phqk,pqhd->pkhd",
                attn_probs.astype(bf16),
                d_context_heads,
                preferred_element_type=f32,
            )
            query_grad = query_part.reshape(local_pages, local_tokens, model_width) * score_scale
            key_grads = key_part.reshape(local_pages, seg_len, model_width) * score_scale
            value_grads = value_part.reshape(local_pages, seg_len, model_width)
            return (query_grad, key_grads, value_grads)

        return merged()

    query_grad, key_grads, value_grads = add_grads(
        (
            lax.all_gather(key_pages, SEQ, axis=1, tiled=True),
            lax.all_gather(value_pages, SEQ, axis=1, tiled=True),
        )
    )
    key_owned, value_owned = (
        lax.psum_scatter(
            key_grads.astype(jnp.bfloat16), SEQ, scatter_dimension=1, tiled=True
        ).astype(jnp.float32),
        lax.psum_scatter(
            value_grads.astype(jnp.bfloat16), SEQ, scatter_dimension=1, tiled=True
        ).astype(jnp.float32),
    )
    d_queries = query_grad.astype(bf16).reshape(row_count, model_width)
    d_keys = key_owned.astype(bf16).reshape(row_count, model_width)
    d_values = value_owned.astype(bf16).reshape(row_count, model_width)
    query_w_grad = matmul(flat_rows.T, d_queries)
    key_w_grad = matmul(flat_rows.T, d_keys)
    value_w_grad = matmul(flat_rows.T, d_values)
    query_b_grad = column_sum(d_queries)
    value_b_grad = column_sum(d_values)
    hidden_grad = (
        d_res_one
        + matmul(d_queries, query_full.T)
        + matmul(d_keys, key_full.T)
        + matmul(d_values, value_full.T)
    ).astype(bf16)
    attn_owned = (
        lax.psum_scatter(query_w_grad, AXES, scatter_dimension=0, tiled=True),
        lax.psum_scatter(key_w_grad, AXES, scatter_dimension=0, tiled=True),
        lax.psum_scatter(value_w_grad, AXES, scatter_dimension=0, tiled=True),
        lax.psum_scatter(output_w_grad, AXES, scatter_dimension=0, tiled=True),
        lax.psum_scatter(query_b_grad, AXES, scatter_dimension=0, tiled=True),
        lax.psum_scatter(value_b_grad, AXES, scatter_dimension=0, tiled=True),
        lax.psum_scatter(output_b_grad, AXES, scatter_dimension=0, tiled=True),
        lax.psum_scatter(gain_one_grad, AXES, scatter_dimension=0, tiled=True),
        lax.psum_scatter(shift_one_grad, AXES, scatter_dimension=0, tiled=True),
    )
    out_pages = layer_out.astype(bf16).reshape(local_pages, local_tokens, model_width)
    grad_pages = hidden_grad.reshape(local_pages, local_tokens, model_width)
    return (
        out_pages,
        grad_pages,
        attn_owned[0],
        attn_owned[1],
        attn_owned[2],
        attn_owned[3],
        attn_owned[4],
        attn_owned[5],
        attn_owned[6],
        attn_owned[7],
        attn_owned[8],
        ffn_owned[0],
        ffn_owned[2],
        ffn_owned[1],
        ffn_owned[3],
        ffn_owned[4],
        ffn_owned[5],
    )


def per_device(pages, hidden, lengths, w_query, w_key, w_value, w_output, b_query, b_value, b_output, attn_gain, attn_shift,
               w_inner, b_inner, w_outer, b_outer, ffn_gain, ffn_shift, cotangent):
    local_pages, seg, width = hidden.shape
    rows, panels = w_query.shape[0], w_inner.shape[1] // width
    nz, _, _ = page_grid(pages)
    if rows % 8 or nz != panels or local_pages * seg != 2 * seg or 4 * rows > 128:
        return plain_layer(hidden, lengths, w_query, w_key, w_value, w_output, b_query, b_value, b_output, attn_gain, attn_shift,
                           w_inner, b_inner, w_outer, b_outer, ffn_gain, ffn_shift, cotangent)
    small = pack_vectors((b_query, b_value, b_output, attn_gain, attn_shift, b_outer, ffn_gain, ffn_shift), b_inner)
    flat = local_pages * seg, width
    arrays = whole_layer(
        pages, HEADS, lengths, hidden.reshape(flat), cotangent.reshape(flat), w_query, w_key, w_value, w_output, w_inner, w_outer,
        small, local_pages)
    out, grad, g_q, g_k, g_v, g_o, g_inner, g_outer, *own = finish(rows, panels, arrays)
    return (out.reshape(hidden.shape), grad.reshape(hidden.shape), g_q, g_k, g_v, g_o, own[0], own[1], own[2], own[3], own[4],
            g_inner, own[8], g_outer, own[5], own[6], own[7])


def solution(mesh):
    in_specs = (
        P(PAGE, SEQ, None),
        P(PAGE),
        P(AXES, None),
        P(AXES, None),
        P(AXES, None),
        P(AXES, None),
        P(AXES),
        P(AXES),
        P(AXES),
        P(AXES),
        P(AXES),
        P(AXES, None),
        P(AXES),
        P(AXES, None),
        P(AXES),
        P(AXES),
        P(AXES),
        P(PAGE, SEQ, None),
    )
    out_specs = (
        P(PAGE, SEQ, None),
        P(PAGE, SEQ, None),
        P(AXES, None),
        P(AXES, None),
        P(AXES, None),
        P(AXES, None),
        P(AXES),
        P(AXES),
        P(AXES),
        P(AXES),
        P(AXES),
        P(AXES, None),
        P(AXES),
        P(AXES, None),
        P(AXES),
        P(AXES),
        P(AXES),
    )
    return jax.shard_map(
        functools.partial(per_device, mesh.shape[PAGE]), mesh=mesh, in_specs=in_specs, out_specs=out_specs, check_vma=False
    )
```
